32 devices in a mesh: band: 8 (over y, x, core), cols: 4 (over z).
Axes of the slice: x: 2, y: 2, z: 4, core: 2. Of those that a mesh axis runs over, the one named last changes fastest.
Arguments:
- band_diagonals: float32 [256, 3072], P('cols', 'band'), may hold values from -0.4 to 0.4, as said below
- eigenvectors: float32 [3072, 512], P('band', 'cols'), may hold values from -4 to 4
Outputs:
- band_result: float32 [256, 3072], P('cols', 'band')
- transformed: float32 [3072, 512], P('band', 'cols')
The draws below stay inside these ranges and needn't reach their ends.
Inputs may be any that keep to these rules, and one draw needn't show every extreme that they name: `band_diagonals`: entry [k, r] is the matrix's entry in row r and column r - k; it is zero where k > 128 or r < k.
All inputs are finite; a program needn't handle non-finite values.
Results may differ from the reference program's by a relative error of at most 0.0003.
Values sent between devices are 32-bit elements; how exact they have to be, the bound alone decides.
A program may use at most 64 MiB of HBM per device.

```python
import jax
import jax.numpy as jnp
from jax import lax

BW = 128
SWEEPS = 4
ORDER = 3072
EIGVECS = 512


def draw_band_diagonals(key, part):
    rough = jnp.clip(jax.random.normal(key, (2 * BW, ORDER), jnp.float32), -4.0, 4.0) * 0.1
    diag_index = lax.broadcasted_iota(jnp.int32, (2 * BW, ORDER), 0)
    row_index = lax.broadcasted_iota(jnp.int32, (2 * BW, ORDER), 1)
    keep = (diag_index <= BW) & (row_index >= diag_index)
    return jnp.where(keep, rough, 0.0)


def levels(stream_key, shape, pieces, least, high):
    loudness, own = 1.0, jax.random.fold_in(stream_key, 6)
    for position, blocks in pieces:
        steps = jnp.exp(jax.random.uniform(jax.random.fold_in(own, position), (blocks,), jnp.float32, least / len(pieces), high / len(pieces)))
        loudness = loudness * jnp.repeat(steps, shape[position] // blocks).reshape([-1 if axis == position else 1 for axis in range(len(shape))])
    return loudness


def noise(stream_key, extent, spread, bound, cuts=(), kind=jnp.bfloat16):
    drawn = jax.random.normal(stream_key, extent, jnp.float32) * spread
    if len(cuts) > 0:
        drawn = levels(stream_key, extent, cuts, -0.22, 0.18) * drawn
    return jnp.clip(drawn, min=-bound, max=bound).astype(kind)


def setup_inputs(seed: int = 0) -> dict:
    key_list = jax.random.split(jax.random.key(seed), 3)
    band_diagonals = draw_band_diagonals(jax.random.fold_in(key_list[2], 71), 0)
    eigenvectors = noise(key_list[1], (ORDER, EIGVECS), 1.0, 4.0, ((0, 8), (1, 4)), jnp.float32)
    return {"band_diagonals": band_diagonals, "eigenvectors": eigenvectors}


HIGHEST = lax.Precision.HIGHEST

def skew_rows(block_rows):
    row_count, col_count = block_rows.shape
    flipped = block_rows[:, ::-1]
    padded = jnp.pad(flipped, ((0, 0), (0, row_count)))
    flat_cells = padded.reshape(-1)[:row_count * (col_count + row_count - 1)]
    return flat_cells.reshape(row_count, col_count + row_count - 1)

def unskew_rows(dense_rows, col_count):
    row_count = dense_rows.shape[0]
    flat_cells = jnp.pad(dense_rows.reshape(-1), (0, row_count))
    grid_cells = flat_cells.reshape(row_count, col_count + row_count)
    return grid_cells[:, :col_count][:, ::-1]

def chase_step(region, first_step):
    double = region.shape[0]
    half_width = double // 2
    dense_rows = skew_rows(region)
    offset = half_width - 1
    upper_rows = dense_rows[:half_width, offset:offset + double]
    lower_rows = dense_rows[half_width:, offset + half_width:offset + double]
    left_part = upper_rows[:, :half_width]
    window = upper_rows[:, half_width:]
    column = jnp.where(first_step, left_part[:, half_width - 1], left_part[:, 0])
    length = jnp.sqrt(jnp.sum(column * column))
    vector = column.at[0].add(length)
    factor = 2.0 / jnp.sum(vector * vector)
    mirror = window + window.T - jnp.diag(jnp.diag(window))
    across = factor * jnp.dot(vector, left_part, precision=HIGHEST)
    inside = factor * jnp.dot(mirror, vector, precision=HIGHEST)
    beneath = factor * jnp.dot(lower_rows, vector, precision=HIGHEST)
    inside = inside - 0.5 * factor * jnp.dot(vector, inside, precision=HIGHEST) * vector
    left_part = left_part - vector[:, None] * across[None, :]
    window = window - jnp.tril(vector[:, None] * inside[None, :] + inside[:, None] * vector[None, :])
    lower_rows = lower_rows - beneath[:, None] * vector[None, :]
    cleared = jnp.zeros_like(column).at[0].set(-length)
    left_part = jnp.where(first_step, left_part.at[:, half_width - 1].set(cleared), left_part.at[:, 0].set(cleared))
    dense_rows = dense_rows.at[:half_width, offset:offset + double].set(jnp.concatenate([left_part, window], 1))
    dense_rows = dense_rows.at[half_width:, offset + half_width:offset + double].set(lower_rows)
    return (unskew_rows(dense_rows, double), vector, factor)

def reference(band_diagonals, eigenvectors):
    band_rows = band_diagonals.T
    step_count = ORDER // BW - 2
    kept_vectors = []
    kept_factors = []
    for sweep_number in range(SWEEPS):

        def advance(carry, step_index):
            anchor = (sweep_number + 1 + step_index * BW).astype(jnp.int32)
            region = lax.dynamic_slice_in_dim(carry, anchor, 2 * BW, 0)
            region, vector, factor = chase_step(region, step_index == 0)
            carry = lax.dynamic_update_slice_in_dim(carry, region, anchor, 0)
            return (carry, (vector, factor))
        band_rows, (sweep_vectors, sweep_factors) = lax.scan(advance, band_rows, jnp.arange(step_count, dtype=jnp.int32))
        kept_vectors.append(sweep_vectors)
        kept_factors.append(sweep_factors)
    result = eigenvectors
    for sweep_number in reversed(range(SWEEPS)):
        lead_rows = sweep_number + 1
        sweep_vectors = kept_vectors[sweep_number]
        sweep_factors = kept_factors[sweep_number]
        blocks = result[lead_rows:lead_rows + step_count * BW].reshape(step_count, BW, EIGVECS)
        inner_sums = jnp.einsum('kb,kbc->kc', sweep_vectors, blocks, precision=HIGHEST)
        blocks = blocks - (sweep_factors[:, None] * sweep_vectors)[:, :, None] * inner_sums[:, None, :]
        result = result.at[lead_rows:lead_rows + step_count * BW].set(blocks.reshape(step_count * BW, EIGVECS))
    return (band_rows.T, result)
```

```python
import functools

import jax
import jax.numpy as jnp
from jax import lax
from jax.experimental import pallas as pl
from jax.experimental.pallas import tpu as pltpu
from jax.sharding import PartitionSpec as P

SWEEPS = 4
LAG = 3
UNPACK = 2


def chase_kernel(blocks, half, blocks_dev, halo, piece_count, sweeps, *refs):
    band_ref, above_ref, eig_ref, under_ref, band_out, eig_out = refs[:6]
    refs = refs[2:]
    d_refs = refs[4 : 5 + sweeps]
    l_refs = refs[5 + sweeps : 6 + 2 * sweeps]
    v_refs = refs[6 + 2 * sweeps : 6 + 3 * sweeps]
    tau_refs = refs[6 + 3 * sweeps : 6 + 4 * sweeps]
    edge_ref, eye_ref, turn_ref = refs[6 + 4 * sweeps :]
    steps = blocks - 2
    row = lax.broadcasted_iota(jnp.int32, (half, half), 0)
    col = lax.broadcasted_iota(jnp.int32, (half, half), 1)
    lane = lax.broadcasted_iota(jnp.int32, (1, half), 1)
    eye = row == col
    row8 = lax.broadcasted_iota(jnp.int32, (8, half), 0)
    col8 = lax.broadcasted_iota(jnp.int32, (8, half), 1)
    zero = jnp.zeros((half, half), jnp.float32)
    tiles = range(half // 8)

    def slot(k):
        return jnp.clip(k, -1, blocks + 1) + 1

    def unpack(block):
        dev = block // blocks_dev
        part = block % blocks_dev
        start = pl.multiple_of(part * half, half)
        piece = band_ref[dev, :half, pl.ds(start, half)]
        extra = band_ref[dev, half : half + 1, pl.ds(start, half)]
        rows = pltpu.roll(piece.T, 1, 1, stride=1, stride_axis=0)
        d_refs[0][block + 1] = jnp.where(row >= col, rows, rows.T)
        l_refs[0][block] = jnp.where(
            col > row, rows, jnp.where(eye, jnp.broadcast_to(extra, (half, half)), 0.0)
        )

    def unpack_step(block, carry):
        unpack(block)
        return carry

    lax.fori_loop(0, blocks, unpack_step, 0, unroll=UNPACK)
    for level in range(sweeps):
        d_refs[level][blocks + 1] = zero
        l_refs[level][blocks + 1] = zero
        v_refs[level][0] = zero
        tau_refs[level][0] = zero[:8]
    l_refs[0][blocks] = zero
    eye_ref[...] = jnp.where(eye, 1.0, 0.0)
    edge_ref[...] = jnp.zeros(edge_ref.shape, jnp.float32)

    def load(ref, index):
        return [ref[index, 8 * i : 8 * i + 8, :] for i in tiles]

    def store(ref, index, parts):
        for i in tiles:
            ref[index, 8 * i : 8 * i + 8, :] = parts[i]

    def tree(parts):
        while len(parts) > 1:
            parts = [a + b for a, b in zip(parts[::2], parts[1::2])]
        return jnp.sum(parts[0], axis=0, keepdims=True)

    def norms(x, new):
        squares = [a * a for a in x]
        squares[0] = jnp.where(row8 == new, 0.0, squares[0])
        rest = tree(squares)
        top = x[0][new : new + 1, :]
        return rest, top, jnp.sqrt(rest + top * top)

    def begin(s):
        first = load(d_refs[s], 1)
        corner = l_refs[s][1, s : s + 1, :]
        first[0] = jnp.where(row8 == s, corner, first[0])
        x = [jnp.broadcast_to(a[:, s : s + 1], (8, half)) for a in first]
        store(v_refs[s], 1, x)
        length = norms(x, s + 1)[2]
        edge = jnp.where((row8 == s) & (col8 == s), d_refs[s][1, :8, :], edge_ref[...])
        edge_ref[...] = jnp.where((row8 == s + 1) & (col8 == s), -length, edge)

    def chain(s, k):
        here, after, before = k + 1, k + 2, k
        old, new = s, s + 1
        d_prev, l_prev, d_now, l_now = d_refs[s], l_refs[s], d_refs[s + 1], l_refs[s + 1]
        active = k < steps
        x = load(v_refs[s], here)
        d_old, l_old, d_next = load(d_prev, here), load(l_prev, here), load(d_prev, after)
        left = load(l_now, before)
        l_next = l_prev[after, old : old + 1, :]
        at_old, at_new = col8 == old, lane == new

        x_row = tree([x[i] * eye_ref[8 * i : 8 * i + 8, :] for i in tiles])
        rest, top, length = norms(x, new)
        v_top = top + length
        tau = 2.0 / (rest + v_top * v_top)
        tau = jnp.where(lane < jnp.where(active, half, 0), tau, 0.0)
        v = [jnp.where(row8 == new, v_top, x[0])] + x[1:]
        v_row = jnp.where(at_new, v_top, x_row)
        tv_row = tau * v_row

        corner = jnp.where(lane == old, l_next, 0.0)
        for spot in range(1, s):
            chosen = jnp.where(k == steps - 2, spot, -1)
            corner = jnp.where(lane == chosen, l_refs[spot][steps, old : old + 1, :], corner)
        below = [jnp.where(at_old, b, a) for a, b in zip(l_old, d_next)]
        below[0] = jnp.where(row8 == old, corner, below[0])
        column = [jnp.broadcast_to(a[:, new : new + 1], (8, half)) for a in below]
        beneath = [jnp.sum(a * tv_row, axis=1, keepdims=True) for a in below]

        lead = jnp.where(lane == old, d_next[0][old : old + 1, :], l_old[0][old : old + 1, :])
        lead_col = [
            jnp.sum(lead * eye_ref[8 * i : 8 * i + 8, :], axis=1, keepdims=True) for i in tiles
        ]
        window = [jnp.where(at_old, b, a) for a, b in zip(d_old, lead_col)]
        window[0] = jnp.where(row8 == old, lead, window[0])
        inside = tau * tree([a * b for a, b in zip(v, window)])
        inside_col = [jnp.sum(a * tv_row, axis=1, keepdims=True) for a in window]
        across = tau * tree([a * b for a, b in zip(v, left)])

        store(v_refs[s], after, [c - b * v_top for c, b in zip(column, beneath)])
        store(l_now, here, [a - b * v_row for a, b in zip(below, beneath)])
        scale = jnp.sum(tv_row * inside, axis=1, keepdims=True)
        mixed = inside - scale * v_row
        store(d_now, here, [w - a * mixed - b * v_row for w, a, b in zip(window, v, inside_col)])
        left = [w - a * across for w, a in zip(left, v)]
        if s == sweeps - 1:
            pick = col8 == jnp.where(active, new, -1)
            left = [
                jnp.where(pick, jnp.where(row8 == new, -length, 0.0) if i == 0 else 0.0, left[i])
                for i in tiles
            ]
        store(l_now, before, left)
        v_refs[s][here, :8, :] = v[0]
        tau_refs[s][here] = jnp.broadcast_to(tau, (8, half))

    def phase(first, last, chains):
        def wave(t, carry):
            for s in reversed(chains):
                chain(s, t - LAG * s)
            return carry

        lax.fori_loop(first, last, wave, 0)

    for s in range(sweeps - 1):
        begin(s)
        phase(LAG * s, LAG * (s + 1), range(s + 1))
    begin(sweeps - 1)
    phase(LAG * (sweeps - 1), blocks, range(sweeps))
    for s in range(1, sweeps):
        phase(blocks + LAG * (s - 1), blocks + LAG * s, range(s, sweeps))

    device = lax.axis_index("band")
    base = device * blocks_dev - halo
    eig = [above_ref[e * half : (e + 1) * half, :] for e in range(halo)]
    eig += [eig_ref[e * half : (e + 1) * half, :] for e in range(blocks_dev)]
    eig.append(under_ref[...])
    for s in reversed(range(sweeps)):
        lead_rows = s + 1
        for e in range(sweeps - 1 - s + halo - sweeps, halo + blocks_dev):
            k = base + e
            v = v_refs[s][slot(k)]
            tau = tau_refs[s][slot(k), 0:1, :]
            low, high = eig[e], eig[e + 1]
            mixed = jnp.concatenate([jnp.where(row8 < lead_rows, high[:8], low[:8]), low[8:]], 0)
            inner = tau * jnp.sum(v * mixed, axis=0, keepdims=True)
            mixed = mixed - v * inner
            eig[e] = jnp.concatenate([jnp.where(row8 < lead_rows, low[:8], mixed[:8]), mixed[8:]], 0)
            top = jnp.where(row8 < lead_rows, mixed[:8], high[:8])
            eig[e + 1] = jnp.concatenate([top, high[8:]], 0) if high.shape[0] > 8 else top
    for m in range(blocks_dev):
        eig_out[m * half : (m + 1) * half, :] = eig[halo + m]

    d_last, l_last = d_refs[sweeps], l_refs[sweeps]
    edge = jnp.concatenate([edge_ref[...], zero[8:]], axis=0)
    rest = zero
    for s in range(1, sweeps):
        rest = jnp.where(col == s, l_refs[s][steps], rest)
    d_last[0] = jnp.where(row < sweeps, edge, 0.0)
    l_last[0] = jnp.where(row >= sweeps, edge, 0.0)
    flip = jnp.where((row + col == half) | ((row == 0) & (col == 0)), 1.0, 0.0)
    position = lax.axis_index("cols") * piece_count
    for m in range(blocks_dev):
        b = device * blocks_dev + m
        lim = jnp.where(b > 0, half, 0)
        rest_below = jnp.where(b == steps, half, 0)
        rest_last = jnp.where(b == steps + 1, half, 0)
        d_here, d_before = d_last[slot(b)], d_last[slot(b - 1)]
        l_here, l_before = l_last[slot(b - 1)], l_last[slot(b - 2)]
        c0 = jnp.where(
            row >= sweeps, jnp.where(col >= sweeps, d_here, l_here), jnp.where(col < sweeps, d_before, 0.0)
        )
        c1 = jnp.where(
            row >= sweeps,
            jnp.where(col >= sweeps, l_here, jnp.where(row < rest_below, rest, 0.0)),
            jnp.where(col >= sweeps, d_before, l_before),
        )
        c1 = jnp.where(row < lim, c1, 0.0)
        c2 = jnp.where(col >= sweeps, l_before, jnp.where(row < rest_last, rest, 0.0))
        c2 = jnp.where(row < sweeps, c2, 0.0)
        c2 = jnp.where(row < lim, c2, 0.0)
        lower = jnp.where(col <= row, c0, c1)
        upper = jnp.where(col <= row, c1, c2)
        for n, part in enumerate((lower, upper)):
            turned = jnp.dot(part, flip, precision=lax.Precision.HIGHEST)
            turned = pltpu.roll(turned, 0, 1, stride=1, stride_axis=0)
            turn_ref[n * half : (n + 1) * half, :] = turned.T
        band_out[:, m * half : (m + 1) * half] = turn_ref[pl.ds(pl.multiple_of(position, 8), piece_count), :]


def gather_kernel(half, devices, cols, takes, band_ref, eig_ref, all_ref, above_ref, under_ref, rev_ref, sems):
    z_send, z_recv, p_send, p_recv, c_send, c_recv, e_send, e_recv, own_sem = sems
    d, c = lax.axis_index("band"), lax.axis_index("cols")
    count = band_ref.shape[0]
    full = half // count
    pieces = full + 1
    chips = devices // 2
    tall = chips // 2
    chip, core = d // 2, d % 2
    partner = chip * 2 + 1 - core
    spot = (1 - chip % 2) * (chip // 2) + (chip % 2) * (chips - 1 - chip // 2)

    def at(rel):
        ring = (spot + rel + chips) % chips
        turn = ring // tall
        return ((1 - turn) * 2 * ring + turn * (2 * (chips - 1 - ring) + 1)) * 2 + core

    for r in range(count):
        rev_ref[r : r + 1, :] = band_ref[count - 1 - r : count - r, :]

    barrier = pltpu.get_barrier_semaphore()
    peers = [(at(1), c), (at(-1), c), (partner, c)]
    for hop in range(1, len(takes) + 1):
        peers += [((d + hop) % devices, c), ((d - hop + devices) % devices, c)]
    for peer in peers:
        pl.semaphore_signal(barrier, inc=1, device_id=peer, device_id_type=pl.DeviceIdType.MESH)

    @pl.when(c > 0)
    def _():
        pl.semaphore_signal(barrier, inc=1, device_id=(d, c - 1), device_id_type=pl.DeviceIdType.MESH)

    @pl.when(c < cols - 1)
    def _():
        pl.semaphore_signal(barrier, inc=1, device_id=(d, c + 1), device_id_type=pl.DeviceIdType.MESH)

    beside = (c + cols - 1) // cols + 1 - (c + 1) // cols
    pl.semaphore_wait(barrier, len(peers) + beside)

    def send(src, dst, send_sem, recv_sem, device):
        return pltpu.make_async_remote_copy(
            src_ref=src,
            dst_ref=dst,
            send_sem=send_sem,
            recv_sem=recv_sem,
            device_id=device,
            device_id_type=pl.DeviceIdType.MESH,
        )

    def rows_of(p, part):
        first, size = (half - (p + 1) * count, count) if p < full else (half, 8)
        if part is not None and p < full:
            first, size = first + part * (size // 2), size // 2
        return pl.ds(first, size)

    def place(dev, p, part=None):
        return all_ref.at[dev, rows_of(p, part)]

    def source(p):
        return rev_ref if p < full else band_ref.at[pl.ds(0, 8)]

    def along(p, up, src):
        to = (c + 1) % cols if up else (c - 1 + cols) % cols
        return send(src, place(d, p), z_send.at[p, int(up)], z_recv.at[p], (d, to))

    def hops(p):
        for j in range(1, chips // 2 + 1):
            for way in (1, -1):
                if 2 * j < chips:
                    yield j, way, None
                elif p < full:
                    yield j, way, 0 if way == 1 else 1
                elif way == 1:
                    yield j, way, None

    def across(p, j, way, part, src=None):
        dev = at(-way * (j - 1))
        src = place(dev, p, part) if src is None else src
        which = 2 * j + (way + 1) // 2
        return send(src, place(dev, p, part), p_send.at[p, which], p_recv.at[p, which], (at(way), c))

    def pair(p, j, way, part, src=None):
        dev = at(-way * j)
        src = place(dev, p, part) if src is None else src
        which = 2 * j + (way + 1) // 2
        return send(src, place(dev, p, part), c_send.at[p, which], c_recv.at[p, which], (partner, c))

    def own(p):
        return pltpu.make_async_copy(source(p), place(d, p), own_sem)

    def first_hops(p, src):
        for j, way, part in hops(p):
            if j == 1:
                across(p, 1, way, part, src).start()
        pair(p, 0, 1, None, src).start()

    rows_dev = eig_ref.shape[0]
    halos = []
    end = sum(takes)
    for hop, take in enumerate(takes, 1):
        halos.append(
            send(
                eig_ref.at[pl.ds(rows_dev - take, take)],
                above_ref.at[pl.ds(end - take, take)],
                e_send.at[hop],
                e_recv.at[hop],
                ((d + hop) % devices, c),
            )
        )
        end -= take
    halos.append(
        send(eig_ref.at[pl.ds(0, 8)], under_ref, e_send.at[0], e_recv.at[0], ((d - 1 + devices) % devices, c))
    )

    for p in range(pieces):

        @pl.when(c == p)
        def _():
            @pl.when(c < cols - 1)
            def _():
                along(p, True, source(p)).start()

            @pl.when(c > 0)
            def _():
                along(p, False, source(p)).start()

            first_hops(p, source(p))
            own(p).start()

    def receive(p):
        @pl.when(c != p)
        def _():
            along(p, True, place(d, p)).wait_recv()

            @pl.when((c > p) & (c < cols - 1))
            def _():
                along(p, True, place(d, p)).start()

            @pl.when((c < p) & (c > 0))
            def _():
                along(p, False, place(d, p)).start()

            first_hops(p, place(d, p))

    def relay(p, level):
        for j, way, part in hops(p):
            if j == level:
                across(p, j, way, part).wait_recv()
                for j2, way2, part2 in hops(p):
                    if j2 == j + 1 and way2 == way:
                        across(p, j2, way, part2).start()
                pair(p, j, way, part).start()

    for p in reversed(range(pieces)):
        receive(p)
    for halo in halos:
        halo.start()
    for level in range(1, chips // 2 + 1):
        for p in reversed(range(pieces)):
            relay(p, level)
    for p in range(pieces):

        @pl.when(c == p)
        def _():
            own(p).wait()

        @pl.when((c >= p) & (c < cols - 1))
        def _():
            along(p, True, place(d, p)).wait_send()

        @pl.when((c <= p) & (c > 0))
        def _():
            along(p, False, place(d, p)).wait_send()

        for j, way, part in hops(p):
            across(p, j, way, part).wait_send()
            pair(p, j, way, part).wait()
        pair(p, 0, 1, None).wait()
    for halo in halos:
        halo.wait()


def body(band_diagonals, eigenvectors):
    piece_count, rows_dev = band_diagonals.shape
    cols = lax.axis_size("cols")
    double = piece_count * cols
    half = double // 2
    blocks_dev = rows_dev // half
    devices = lax.axis_size("band")
    blocks = blocks_dev * devices
    sweeps = SWEEPS
    halo = sweeps
    columns = eigenvectors.shape[1]
    f32 = jnp.float32
    vmem = pl.BlockSpec(memory_space=pltpu.VMEM)

    takes = []
    while sum(takes) < halo * half:
        takes.append(min(halo * half - sum(takes), rows_dev))
    pieces = half // piece_count + 1
    dma = pltpu.SemaphoreType.DMA
    band, above, under = pl.pallas_call(
        functools.partial(gather_kernel, half, devices, cols, takes),
        out_shape=(
            jax.ShapeDtypeStruct((devices, half + 8, rows_dev), f32),
            jax.ShapeDtypeStruct((halo * half, columns), f32),
            jax.ShapeDtypeStruct((8, columns), f32),
        ),
        in_specs=[vmem] * 2,
        out_specs=(vmem,) * 3,
        scratch_shapes=[
            pltpu.VMEM((piece_count, rows_dev), f32),
            [
                dma((pieces, 2)),
                dma((pieces,)),
                dma((pieces, devices + 2)),
                dma((pieces, devices + 2)),
                dma((pieces, devices + 2)),
                dma((pieces, devices + 2)),
                dma((len(takes) + 1,)),
                dma((len(takes) + 1,)),
                dma,
            ]
        ],
        compiler_params=pltpu.CompilerParams(collective_id=0, has_side_effects=True),
    )(band_diagonals, eigenvectors)

    slots = blocks + 3
    scratch = (
        [pltpu.VMEM((slots, half, half), f32)] * (2 * (sweeps + 1))
        + [pltpu.VMEM((slots, half, half), f32)] * sweeps
        + [pltpu.VMEM((slots, 8, half), f32)] * sweeps
        + [
            pltpu.VMEM((8, half), f32),
            pltpu.VMEM((half, half), f32),
            pltpu.VMEM((double, half), f32),
        ]
    )
    return pl.pallas_call(
        functools.partial(chase_kernel, blocks, half, blocks_dev, halo, piece_count, sweeps),
        out_shape=(
            jax.ShapeDtypeStruct((piece_count, rows_dev), f32),
            jax.ShapeDtypeStruct((rows_dev, columns), f32),
        ),
        in_specs=[vmem] * 4,
        out_specs=(vmem, vmem),
        scratch_shapes=scratch,
        compiler_params=pltpu.CompilerParams(vmem_limit_bytes=62 * 1024 * 1024),
    )(band, above, eigenvectors, under)


def solution(mesh):
    return jax.shard_map(
        body,
        mesh=mesh,
        in_specs=(P("cols", "band"), P("band", "cols")),
        out_specs=(P("cols", "band"), P("band", "cols")),
        check_vma=False,
    )
```

```python
import functools

import jax
import jax.numpy as jnp
from jax import lax
from jax.experimental import pallas as pl
from jax.experimental.pallas import tpu as pltpu
from jax.sharding import PartitionSpec as P

SWEEPS = 4
LAG = 3
UNPACK = 2


def chase_kernel(blocks, half, blocks_dev, halo, piece_count, sweeps, *refs):
    band_ref, above_ref, eig_ref, under_ref, band_out, eig_out = refs[:6]
    d_ref, l_ref, t_ref, eye_ref, edge_ref, raw_ref, turn_ref = refs[6:13]
    v_refs = refs[13 : 13 + sweeps]
    tau_refs = refs[13 + sweeps : 13 + 2 * sweeps]
    last = sweeps - 1
    pairs = [(a, b) for b in range(1, sweeps) for a in range(b)] + [(last, last)]
    fields = dict(zip(pairs, refs[13 + 2 * sweeps :]))
    steps = blocks - 2
    row = lax.broadcasted_iota(jnp.int32, (half, half), 0)
    col = lax.broadcasted_iota(jnp.int32, (half, half), 1)
    eye = row == col
    row8 = lax.broadcasted_iota(jnp.int32, (8, half), 0)
    col8 = lax.broadcasted_iota(jnp.int32, (8, half), 1)
    zero = jnp.zeros((half, half), jnp.float32)
    count = half // 8

    def unpack(block, carry):
        dev = block // blocks_dev
        part = block % blocks_dev
        start = pl.multiple_of(part * half, half)
        piece = band_ref[dev, :half, pl.ds(start, half)]
        extra = band_ref[dev, half : half + 1, pl.ds(start, half)]
        rows = pltpu.roll(piece.T, 1, 1, stride=1, stride_axis=0)
        turned = rows.T
        extra = jnp.where(eye, jnp.broadcast_to(extra, (half, half)), 0.0)
        d_ref[block + 2] = jnp.where(row >= col, rows, turned)
        l_ref[block + 1] = jnp.where(col > row, rows, extra)
        t_ref[block + 1] = jnp.where(row > col, turned, extra)
        return carry

    lax.fori_loop(0, blocks, unpack, 0, unroll=UNPACK)
    for spot in (0, 1, blocks + 2):
        d_ref[spot] = zero
    for spot in (0, blocks + 1):
        l_ref[spot] = zero
        t_ref[spot] = zero
    for ref in v_refs + tau_refs + tuple(fields.values()) + (raw_ref, edge_ref):
        ref[...] = jnp.zeros(ref.shape, jnp.float32)
    eye_ref[...] = jnp.where(eye, 1.0, 0.0)

    def tile(ref, k, i=0):
        return ref[k + 2, 8 * i : 8 * i + 8, :]

    def lanes(x):
        return jnp.broadcast_to(jnp.sum(x, axis=1, keepdims=True), (8, half))

    def rows_sum(x):
        return jnp.broadcast_to(jnp.sum(x, axis=0, keepdims=True), (8, half))

    def at_lane(x, spot):
        return jnp.broadcast_to(x[:, spot : spot + 1], (8, half))

    def total(parts):
        while len(parts) > 1:
            rest = parts[len(parts) // 2 * 2 :]
            parts = [a + b for a, b in zip(parts[::2], parts[1::2])] + rest
        return parts[0]

    def to_lane(x, fill, spot):
        return jnp.where(col8 == spot, fill, x)

    def norms(x, new):
        rest = lanes(to_lane(x * x, 0.0, new))
        top = at_lane(x, new)
        return rest, top, jnp.sqrt(rest + top * top)

    def begin(s):
        base = jnp.broadcast_to(d_ref[2, s : s + 1, :], (8, half))
        x = jnp.where(col8 > s, base, jnp.broadcast_to(t_ref[2, s : s + 1, :], (8, half)))
        diagonal = base
        for a in range(s):
            raw = raw_ref[a]
            x = x - rows_sum(fields[a, s][2] * at_lane(raw, s))
            diagonal = diagonal - 2.0 * raw[0:1, :] * raw[4:5, :]
        length = norms(x, s + 1)[2]
        edge = jnp.where((row8 == s) & (col8 == s), diagonal, edge_ref[...])
        edge_ref[...] = jnp.where((row8 == s + 1) & (col8 == s), -length, edge)
        return x, jnp.zeros((8, half), jnp.float32)

    def chain(s, k, x, hung):
        new = s + 1
        main = col8 > s
        x_col = [
            jnp.sum(x * eye_ref[8 * i : 8 * i + 8, :], axis=1, keepdims=True) for i in range(count)
        ]
        rest, top, length = norms(x, new)
        v_top = top + length
        tau = 2.0 / (rest + v_top * v_top)
        v = to_lane(x, v_top, new)
        v_first = jnp.where(row8 == new, v_top, x_col[0])
        v_main = jnp.where(row8 > s, v_first, 0.0)
        v_tail = v_first - v_main

        def times(ref, spot, extra):
            parts = [tile(ref, spot, i) * x_col[i] for i in range(1, count)]
            return total(parts) + tile(ref, spot) * v_main + extra

        here = times(d_ref, k, tile(l_ref, k) * v_tail)
        after = times(t_ref, k, tile(d_ref, k + 1) * v_tail)
        beyond = tile(t_ref, k + 1) * v_tail
        before = times(l_ref, k - 1, 0.0)
        inside = jnp.where(main, here, after)
        beneath = jnp.where(main, after, beyond)
        across = jnp.where(main, before, here)
        across = across - jnp.where(row8 == 0, v_refs[s][k] * (lanes(hung * x) + length * at_lane(hung, new)), 0.0)
        column = jnp.where(main, jnp.broadcast_to(t_ref[k + 2, new : new + 1, :], (8, half)), 0.0)
        fixes = []
        for a in range(s):
            now = fields[a, s][k + 2]
            up = jnp.where(row8 == 1, 0.0, fields[a, s][k + 1])
            down = jnp.where(row8 == 2, 0.0, fields[a, s][k + 3])
            unit = at_lane(now, new)
            dots = lanes(now * x) + length * unit
            inside = inside - now * pltpu.roll(dots, 4, 0)
            beneath = beneath - down * pltpu.roll(dots, 1, 0)
            across = across - up * pltpu.roll(dots, 7, 0)
            fixes.append(down * pltpu.roll(unit, 1, 0))
        inside = tau * rows_sum(inside)
        beneath = tau * rows_sum(beneath)
        across = tau * rows_sum(across)
        if fixes:
            column = column - rows_sum(total(fixes))
        inside = inside - 0.5 * tau * lanes(v * inside) * v

        v_refs[s][k + 1] = v
        tau_refs[s][k + 1] = tau
        for b in range(s + 1, sweeps) if s < last else (last,):
            ref = fields[s, b]
            other = (col8 > s) & (col8 <= b)
            ref[k + 2, 0:1, :] = jnp.where(other, 0.0, v)[0:1]
            ref[k + 2, 4:5, :] = jnp.where(other, beneath, inside)[0:1]
            ref[k + 1, 7:8, :] = jnp.where(other, inside, across)[0:1]
            ref[k + 3, 1:2, :] = jnp.where(other, 0.0, beneath)[0:1]
            if b > s:
                ref[k + 1, 3:4, :] = jnp.where(other, v, 0.0)[0:1]
                ref[k, 2:3, :] = jnp.where(other, across, 0.0)[0:1]
        if s < last:
            raw_ref[s, 0:1, :] = jnp.where(col8 < jnp.where(k == 0, half, 0), inside, raw_ref[s])[0:1]
            raw_ref[s, 3:4, :] = jnp.where(col8 < jnp.where(k == 1, half, 0), across, raw_ref[s])[3:4]
            raw_ref[s, 4:5, :] = jnp.where(col8 < jnp.where(k == 0, half, 0), v, raw_ref[s])[4:5]
        return column - beneath * v_top, beneath

    def phase(start, stop, chains, xs):
        def wave(t, xs):
            done = {s: chain(s, t - LAG * s, *x) for s, x in reversed(list(zip(chains, xs)))}
            return tuple(done[s] for s in chains)

        return lax.fori_loop(start, stop, wave, tuple(xs))

    xs = ()
    for s in range(last):
        xs = phase(LAG * s, LAG * (s + 1), range(s + 1), xs + (begin(s),))
    xs = phase(LAG * last, steps, range(sweeps), xs + (begin(last),))
    for s in range(1, sweeps):
        xs = phase(steps + LAG * (s - 1), steps + LAG * s, range(s, sweeps), xs[1:])

    device = lax.axis_index("band")
    base = device * blocks_dev - halo
    eig = [above_ref[e * half : (e + 1) * half, :] for e in range(halo)]
    eig += [eig_ref[e * half : (e + 1) * half, :] for e in range(blocks_dev)]
    eig.append(under_ref[...])
    for s in reversed(range(sweeps)):
        lead_rows = s + 1
        for e in range(sweeps - 1 - s + halo - sweeps, halo + blocks_dev):
            spot = jnp.clip(base + e, -1, blocks - 1) + 1
            v = jnp.sum(v_refs[s][spot, 0:1, :] * eye_ref[...], axis=1, keepdims=True)
            tau = tau_refs[s][spot, 0:1, :]
            low, high = eig[e], eig[e + 1]
            mixed = jnp.concatenate([jnp.where(row8 < lead_rows, high[:8], low[:8]), low[8:]], 0)
            inner = tau * jnp.sum(v * mixed, axis=0, keepdims=True)
            mixed = mixed - v * inner
            eig[e] = jnp.concatenate([jnp.where(row8 < lead_rows, low[:8], mixed[:8]), mixed[8:]], 0)
            top = jnp.where(row8 < lead_rows, mixed[:8], high[:8])
            eig[e + 1] = jnp.concatenate([top, high[8:]], 0) if high.shape[0] > 8 else top
    for m in range(blocks_dev):
        eig_out[m * half : (m + 1) * half, :] = eig[halo + m]

    def product(a, b):
        return lax.dot_general(
            a, b, (((0,), (0,)), ((), ())),
            precision=lax.Precision.HIGHEST, preferred_element_type=jnp.float32,
        )

    def stack(k, shift=0, drop=None):
        parts = []
        for a in range(sweeps):
            part = fields[a, last][k + 2]
            part = part if drop is None else jnp.where(row8 == drop, 0.0, part)
            parts.append(pltpu.roll(part, shift, 0) if shift else part)
        return jnp.concatenate(parts, 0)

    def final_d(k):
        outer = jnp.where(col > last, d_ref[k + 2], t_ref[k + 2])
        inner = jnp.where(col > last, l_ref[k + 2], d_ref[k + 3])
        return jnp.where(row > last, outer, inner) - product(stack(k), stack(k, 4))

    def final_l(k):
        outer = jnp.where(col > last, l_ref[k + 2], d_ref[k + 3])
        inner = jnp.where(col > last, 0.0, l_ref[k + 3])
        block = jnp.where(row > last, outer, inner) - product(stack(k + 1, 0, 2), stack(k, 1))
        cleared = jnp.where(k <= steps - 2, sweeps, -1)
        return jnp.where((col == cleared) & (row != sweeps), 0.0, block)

    edge = jnp.concatenate([edge_ref[...], zero[8:]], axis=0)
    bottom, lead = [], []
    for a in range(last):
        bottom.append(jnp.where(row8 == 1, fields[a, last][steps + 2], 0.0))
        lead.append(pltpu.roll(jnp.where(row8 == 3, fields[a, last][steps], 0.0), 6, 0))
    rest = -product(jnp.concatenate(bottom, 0), jnp.concatenate(lead, 0))
    flip = jnp.where((row + col == half) | ((row == 0) & (col == 0)), 1.0, 0.0)
    position = lax.axis_index("cols") * piece_count
    first = device * blocks_dev
    d_last = [final_d(first + m - 1) for m in range(blocks_dev + 1)]
    l_last = [final_l(first + m - 2) for m in range(blocks_dev + 1)]
    top = jnp.where(device == 0, half, 0)
    d_last[0] = jnp.where(row < top, jnp.where(row < sweeps, edge, 0.0), d_last[0])
    l_last[1] = jnp.where(row < top, jnp.where(row >= sweeps, edge, 0.0), l_last[1])
    for m in range(blocks_dev):
        b = first + m
        lim = jnp.where(b > 0, half, 0)
        rest_below = jnp.where(b == steps, half, 0)
        rest_last = jnp.where(b == steps + 1, half, 0)
        d_here, d_before = d_last[m + 1], d_last[m]
        l_here, l_before = l_last[m + 1], l_last[m]
        c0 = jnp.where(
            row >= sweeps, jnp.where(col >= sweeps, d_here, l_here), jnp.where(col < sweeps, d_before, 0.0)
        )
        c1 = jnp.where(
            row >= sweeps,
            jnp.where(col >= sweeps, l_here, jnp.where(row < rest_below, rest, 0.0)),
            jnp.where(col >= sweeps, d_before, l_before),
        )
        c1 = jnp.where(row < lim, c1, 0.0)
        c2 = jnp.where(col >= sweeps, l_before, jnp.where(row < rest_last, rest, 0.0))
        c2 = jnp.where(row < sweeps, c2, 0.0)
        c2 = jnp.where(row < lim, c2, 0.0)
        lower = jnp.where(col <= row, c0, c1)
        upper = jnp.where(col <= row, c1, c2)
        for n, part in enumerate((lower, upper)):
            turned = jnp.dot(part, flip, precision=lax.Precision.HIGHEST)
            turned = pltpu.roll(turned, 0, 1, stride=1, stride_axis=0)
            turn_ref[n * half : (n + 1) * half, :] = turned.T
        band_out[:, m * half : (m + 1) * half] = turn_ref[pl.ds(pl.multiple_of(position, 8), piece_count), :]


def gather_kernel(half, devices, cols, takes, band_ref, eig_ref, all_ref, above_ref, under_ref, rev_ref, sems):
    z_send, z_recv, p_send, p_recv, c_send, c_recv, e_send, e_recv, own_sem = sems
    d, c = lax.axis_index("band"), lax.axis_index("cols")
    count = band_ref.shape[0]
    full = half // count
    pieces = full + 1
    chips = devices // 2
    tall = chips // 2
    chip, core = d // 2, d % 2
    partner = chip * 2 + 1 - core
    spot = (1 - chip % 2) * (chip // 2) + (chip % 2) * (chips - 1 - chip // 2)

    def at(rel):
        ring = (spot + rel + chips) % chips
        turn = ring // tall
        return ((1 - turn) * 2 * ring + turn * (2 * (chips - 1 - ring) + 1)) * 2 + core

    for r in range(count):
        rev_ref[r : r + 1, :] = band_ref[count - 1 - r : count - r, :]

    barrier = pltpu.get_barrier_semaphore()
    peers = [(at(1), c), (at(-1), c), (partner, c)]
    for hop in range(1, len(takes) + 1):
        peers += [((d + hop) % devices, c), ((d - hop + devices) % devices, c)]
    for peer in peers:
        pl.semaphore_signal(barrier, inc=1, device_id=peer, device_id_type=pl.DeviceIdType.MESH)

    @pl.when(c > 0)
    def _():
        pl.semaphore_signal(barrier, inc=1, device_id=(d, c - 1), device_id_type=pl.DeviceIdType.MESH)

    @pl.when(c < cols - 1)
    def _():
        pl.semaphore_signal(barrier, inc=1, device_id=(d, c + 1), device_id_type=pl.DeviceIdType.MESH)

    beside = (c + cols - 1) // cols + 1 - (c + 1) // cols
    pl.semaphore_wait(barrier, len(peers) + beside)

    def send(src, dst, send_sem, recv_sem, device):
        return pltpu.make_async_remote_copy(
            src_ref=src,
            dst_ref=dst,
            send_sem=send_sem,
            recv_sem=recv_sem,
            device_id=device,
            device_id_type=pl.DeviceIdType.MESH,
        )

    def rows_of(p, part):
        first, size = (half - (p + 1) * count, count) if p < full else (half, 8)
        if part is not None and p < full:
            first, size = first + part * (size // 2), size // 2
        return pl.ds(first, size)

    def place(dev, p, part=None):
        return all_ref.at[dev, rows_of(p, part)]

    def source(p):
        return rev_ref if p < full else band_ref.at[pl.ds(0, 8)]

    def along(p, up, src):
        to = (c + 1) % cols if up else (c - 1 + cols) % cols
        return send(src, place(d, p), z_send.at[p, int(up)], z_recv.at[p], (d, to))

    def hops(p):
        for j in range(1, chips // 2 + 1):
            for way in (1, -1):
                if 2 * j < chips:
                    yield j, way, None
                elif p < full:
                    yield j, way, 0 if way == 1 else 1
                elif way == 1:
                    yield j, way, None

    def across(p, j, way, part, src=None):
        dev = at(-way * (j - 1))
        src = place(dev, p, part) if src is None else src
        which = 2 * j + (way + 1) // 2
        return send(src, place(dev, p, part), p_send.at[p, which], p_recv.at[p, which], (at(way), c))

    def pair(p, j, way, part, src=None):
        dev = at(-way * j)
        src = place(dev, p, part) if src is None else src
        which = 2 * j + (way + 1) // 2
        return send(src, place(dev, p, part), c_send.at[p, which], c_recv.at[p, which], (partner, c))

    def own(p):
        return pltpu.make_async_copy(source(p), place(d, p), own_sem)

    def first_hops(p, src):
        for j, way, part in hops(p):
            if j == 1:
                across(p, 1, way, part, src).start()
        pair(p, 0, 1, None, src).start()

    rows_dev = eig_ref.shape[0]
    halos = []
    end = sum(takes)
    for hop, take in enumerate(takes, 1):
        halos.append(
            send(
                eig_ref.at[pl.ds(rows_dev - take, take)],
                above_ref.at[pl.ds(end - take, take)],
                e_send.at[hop],
                e_recv.at[hop],
                ((d + hop) % devices, c),
            )
        )
        end -= take
    halos.append(
        send(eig_ref.at[pl.ds(0, 8)], under_ref, e_send.at[0], e_recv.at[0], ((d - 1 + devices) % devices, c))
    )

    for p in range(pieces):

        @pl.when(c == p)
        def _():
            @pl.when(c < cols - 1)
            def _():
                along(p, True, source(p)).start()

            @pl.when(c > 0)
            def _():
                along(p, False, source(p)).start()

            first_hops(p, source(p))
            own(p).start()

    def receive(p):
        @pl.when(c != p)
        def _():
            along(p, True, place(d, p)).wait_recv()

            @pl.when((c > p) & (c < cols - 1))
            def _():
                along(p, True, place(d, p)).start()

            @pl.when((c < p) & (c > 0))
            def _():
                along(p, False, place(d, p)).start()

            first_hops(p, place(d, p))

    def relay(p, level):
        for j, way, part in hops(p):
            if j == level:
                across(p, j, way, part).wait_recv()
                for j2, way2, part2 in hops(p):
                    if j2 == j + 1 and way2 == way:
                        across(p, j2, way, part2).start()
                pair(p, j, way, part).start()

    for p in reversed(range(pieces)):
        receive(p)
    for halo in halos:
        halo.start()
    for level in range(1, chips // 2 + 1):
        for p in reversed(range(pieces)):
            relay(p, level)
    for p in range(pieces):

        @pl.when(c == p)
        def _():
            own(p).wait()

        @pl.when((c >= p) & (c < cols - 1))
        def _():
            along(p, True, place(d, p)).wait_send()

        @pl.when((c <= p) & (c > 0))
        def _():
            along(p, False, place(d, p)).wait_send()

        for j, way, part in hops(p):
            across(p, j, way, part).wait_send()
            pair(p, j, way, part).wait()
        pair(p, 0, 1, None).wait()
    for halo in halos:
        halo.wait()


def body(band_diagonals, eigenvectors):
    piece_count, rows_dev = band_diagonals.shape
    cols = lax.axis_size("cols")
    double = piece_count * cols
    half = double // 2
    blocks_dev = rows_dev // half
    devices = lax.axis_size("band")
    blocks = blocks_dev * devices
    sweeps = SWEEPS
    halo = sweeps
    columns = eigenvectors.shape[1]
    f32 = jnp.float32
    vmem = pl.BlockSpec(memory_space=pltpu.VMEM)

    takes = []
    while sum(takes) < halo * half:
        takes.append(min(halo * half - sum(takes), rows_dev))
    pieces = half // piece_count + 1
    dma = pltpu.SemaphoreType.DMA
    band, above, under = pl.pallas_call(
        functools.partial(gather_kernel, half, devices, cols, takes),
        out_shape=(
            jax.ShapeDtypeStruct((devices, half + 8, rows_dev), f32),
            jax.ShapeDtypeStruct((halo * half, columns), f32),
            jax.ShapeDtypeStruct((8, columns), f32),
        ),
        in_specs=[vmem] * 2,
        out_specs=(vmem,) * 3,
        scratch_shapes=[
            pltpu.VMEM((piece_count, rows_dev), f32),
            [
                dma((pieces, 2)),
                dma((pieces,)),
                dma((pieces, devices + 2)),
                dma((pieces, devices + 2)),
                dma((pieces, devices + 2)),
                dma((pieces, devices + 2)),
                dma((len(takes) + 1,)),
                dma((len(takes) + 1,)),
                dma,
            ]
        ],
        compiler_params=pltpu.CompilerParams(collective_id=0, has_side_effects=True),
    )(band_diagonals, eigenvectors)

    slots = blocks + 4
    pair_count = sweeps * (sweeps - 1) // 2 + 1
    scratch = (
        [pltpu.VMEM((slots, half, half), f32)] * 3
        + [
            pltpu.VMEM((half, half), f32),
            pltpu.VMEM((8, half), f32),
            pltpu.VMEM((sweeps, 8, half), f32),
            pltpu.VMEM((double, half), f32),
        ]
        + [pltpu.VMEM((blocks + 1, 8, half), f32)] * (2 * sweeps)
        + [pltpu.VMEM((slots, 8, half), f32)] * pair_count
    )
    return pl.pallas_call(
        functools.partial(chase_kernel, blocks, half, blocks_dev, halo, piece_count, sweeps),
        out_shape=(
            jax.ShapeDtypeStruct((piece_count, rows_dev), f32),
            jax.ShapeDtypeStruct((rows_dev, columns), f32),
        ),
        in_specs=[vmem] * 4,
        out_specs=(vmem, vmem),
        scratch_shapes=scratch,
        compiler_params=pltpu.CompilerParams(vmem_limit_bytes=62 * 1024 * 1024),
    )(band, above, eigenvectors, under)


def solution(mesh):
    return jax.shard_map(
        body,
        mesh=mesh,
        in_specs=(P("cols", "band"), P("band", "cols")),
        out_specs=(P("cols", "band"), P("band", "cols")),
        check_vma=False,
    )
```

```python
import functools

import jax
import jax.numpy as jnp
from jax import lax
from jax.experimental import pallas as pl
from jax.experimental.pallas import tpu as pltpu
from jax.sharding import PartitionSpec as P

SWEEPS = 4
LAG = 3
AHEAD = 4
UNROLL = 2


def chase_kernel(blocks, half, blocks_dev, halo, piece_count, sweeps, *refs):
    band_ref, above_ref, eig_ref, under_ref, band_out, eig_out = refs[:6]
    d_ref, l_ref, t_ref, eye_ref, edge_ref, raw_ref, turn_ref = refs[6:13]
    v_refs = refs[13 : 13 + sweeps]
    tau_refs = refs[13 + sweeps : 13 + 2 * sweeps]
    last = sweeps - 1
    pairs = [(a, b) for b in range(1, sweeps) for a in range(b)] + [(last, last)]
    fields = dict(zip(pairs, refs[13 + 2 * sweeps :]))
    steps = blocks - 2
    row = lax.broadcasted_iota(jnp.int32, (half, half), 0)
    col = lax.broadcasted_iota(jnp.int32, (half, half), 1)
    eye = row == col
    row8 = lax.broadcasted_iota(jnp.int32, (8, half), 0)
    col8 = lax.broadcasted_iota(jnp.int32, (8, half), 1)
    zero = jnp.zeros((half, half), jnp.float32)
    count = half // 8

    def unpack(block):
        dev = block // blocks_dev
        part = block % blocks_dev
        start = pl.multiple_of(part * half, half)
        piece = band_ref[dev, :half, pl.ds(start, half)]
        extra = band_ref[dev, half : half + 1, pl.ds(start, half)]
        rows = pltpu.roll(piece.T, 1, 1, stride=1, stride_axis=0)
        turned = rows.T
        extra = jnp.where(eye, jnp.broadcast_to(extra, (half, half)), 0.0)
        d_ref[block + 2] = jnp.where(row >= col, rows, turned)
        l_ref[block + 1] = jnp.where(col > row, rows, extra)
        t_ref[block + 1] = jnp.where(row > col, turned, extra)

    for spot in (0, 1, blocks + 2):
        d_ref[spot] = zero
    for spot in (0, blocks + 1):
        l_ref[spot] = zero
        t_ref[spot] = zero
    for ref in v_refs + tau_refs + tuple(fields.values()) + (raw_ref, edge_ref):
        ref[...] = jnp.zeros(ref.shape, jnp.float32)
    eye_ref[...] = jnp.where(eye, 1.0, 0.0)

    def tile(ref, k, i=0):
        return ref[k + 2, 8 * i : 8 * i + 8, :]

    def lanes(x):
        return jnp.broadcast_to(jnp.sum(x, axis=1, keepdims=True), (8, half))

    def rows_sum(x):
        return jnp.broadcast_to(jnp.sum(x, axis=0, keepdims=True), (8, half))

    def at_lane(x, spot):
        return jnp.broadcast_to(x[:, spot : spot + 1], (8, half))

    def total(parts):
        while len(parts) > 1:
            rest = parts[len(parts) // 2 * 2 :]
            parts = [a + b for a, b in zip(parts[::2], parts[1::2])] + rest
        return parts[0]

    def to_lane(x, fill, spot):
        return jnp.where(col8 == spot, fill, x)

    def norms(x, new):
        rest = lanes(to_lane(x * x, 0.0, new))
        top = at_lane(x, new)
        square = rest + top * top
        inverse = lax.rsqrt(square)
        return rest, top, square * inverse, inverse

    def wide(line):
        return jnp.broadcast_to(line, (8, half))

    def begin(s):
        base = wide(d_ref[2, s : s + 1, :])
        x = jnp.where(col8 > s, base, wide(t_ref[2, s : s + 1, :]))
        diagonal = base
        for a in range(s):
            raw = raw_ref[a]
            x = x - rows_sum(fields[a, s][2] * at_lane(raw, s))
            diagonal = diagonal - 2.0 * raw[0:1, :] * raw[4:5, :]
        length = norms(x, s + 1)[2]
        edge = jnp.where((row8 == s) & (col8 == s), diagonal, edge_ref[...])
        edge_ref[...] = jnp.where((row8 == s + 1) & (col8 == s), -length, edge)
        return (x,) + (jnp.zeros((8, half), jnp.float32),) * 4

    def targets(s):
        return range(s + 1, sweeps) if s < last else (last,)

    def settle(s, k, inside, v, tau):
        inside = inside - 0.5 * tau * lanes(v * inside) * v
        for b in targets(s):
            ref = fields[s, b]
            other = (col8 > s) & (col8 <= b)
            ref[k + 2, 4:5, :] = jnp.where(other, wide(ref[k + 2, 4:5, :]), inside)[0:1]
            if b > s:
                ref[k + 1, 7:8, :] = jnp.where(other, inside, wide(ref[k + 1, 7:8, :]))[0:1]
        if s < last:
            raw_ref[s, 0:1, :] = jnp.where(col8 < jnp.where(k == 0, half, 0), inside, wide(raw_ref[s, 0:1, :]))[0:1]

    def chain(s, k, x, hung, inside_past, v_past, tau_past):
        new = s + 1
        main = col8 > s
        x_col = [
            jnp.sum(x * eye_ref[8 * i : 8 * i + 8, :], axis=1, keepdims=True) for i in range(count)
        ]
        rest, top, length, inverse = norms(x, new)
        x_main = jnp.where(row8 > s, x_col[0], 0.0)
        x_tail = jnp.where(row8 > s, 0.0, x_col[0])

        def times(ref, spot, extra):
            parts = [tile(ref, spot, i) * x_col[i] for i in range(1, count)]
            return total(parts + [tile(ref, spot) * x_main] + extra)

        here = times(d_ref, k, [tile(l_ref, k) * x_tail])
        after = times(t_ref, k, [tile(d_ref, k + 1) * x_tail])
        beyond = tile(t_ref, k + 1) * x_tail
        before = times(l_ref, k - 1, [])
        here_top = wide(d_ref[k + 2, new : new + 1, :])
        after_top = wide(t_ref[k + 2, new : new + 1, :])
        before_top = wide(l_ref[k + 1, new : new + 1, :])
        inside = jnp.where(main, here, after)
        beneath = jnp.where(main, after, beyond)
        across = jnp.where(main, before, here)
        fixes = []
        for a in range(s):
            now = fields[a, s][k + 2]
            up = jnp.where(row8 == 1, 0.0, fields[a, s][k + 1])
            down = jnp.where(row8 == 2, 0.0, fields[a, s][k + 3])
            unit = at_lane(now, new)
            dots = lanes(now * x)
            beneath = beneath - down * pltpu.roll(dots, 1, 0)
            fixes.append(down * pltpu.roll(unit, 1, 0))
            dots = dots + length * unit
            inside = inside - now * pltpu.roll(dots, 4, 0)
            across = across - up * pltpu.roll(dots, 7, 0)
        beneath = rows_sum(beneath)
        x_next = beneath * -inverse
        column = jnp.where(main, after_top, 0.0)
        if fixes:
            column = column - rows_sum(total(fixes))
        hang = lanes(hung * x) + length * at_lane(hung, new)
        v_top = top + length
        tau = 2.0 / (rest + v_top * v_top)
        v = to_lane(x, v_top, new)
        beneath = tau * (beneath + length * column)
        inside = tau * (rows_sum(inside) + length * jnp.where(main, here_top, after_top))
        across = tau * (rows_sum(across) + length * jnp.where(main, before_top, here_top) - v_past * hang)

        settle(s, k - 1, inside_past, v_past, tau_past)
        v_refs[s][k + 1] = v
        tau_refs[s][k + 1] = tau
        for b in targets(s):
            ref = fields[s, b]
            other = (col8 > s) & (col8 <= b)
            ref[k + 2, 0:1, :] = jnp.where(other, 0.0, v)[0:1]
            ref[k + 1, 7:8, :] = across[0:1]
            ref[k + 3, 1:2, :] = jnp.where(other, 0.0, beneath)[0:1]
            if b > s:
                ref[k + 2, 4:5, :] = beneath[0:1]
                ref[k + 1, 3:4, :] = jnp.where(other, v, 0.0)[0:1]
                ref[k, 2:3, :] = jnp.where(other, across, 0.0)[0:1]
        if s < last:
            raw_ref[s, 3:4, :] = jnp.where(col8 < jnp.where(k == 1, half, 0), across, wide(raw_ref[s, 3:4, :]))[0:1]
            raw_ref[s, 4:5, :] = jnp.where(col8 < jnp.where(k == 0, half, 0), v, wide(raw_ref[s, 4:5, :]))[0:1]
        return x_next, beneath, inside, v, tau

    def phase(start, stop, chains, states):
        def wave(t, states):
            done = {s: chain(s, t - LAG * s, *state) for s, state in reversed(list(zip(chains, states)))}
            if start < steps:
                unpack(jnp.minimum(t + AHEAD, blocks - 1))
            return tuple(done[s] for s in chains)

        return lax.fori_loop(start, stop, wave, tuple(states), unroll=UNROLL)

    def drain(s, state):
        settle(s, steps - 1, *state[2:])

    for block in range(AHEAD):
        unpack(block)
    states = ()
    for s in range(last):
        states = phase(LAG * s, LAG * (s + 1), range(s + 1), states + (begin(s),))
    states = phase(LAG * last, steps, range(sweeps), states + (begin(last),))
    for s in range(1, sweeps):
        drain(s - 1, states[0])
        states = phase(steps + LAG * (s - 1), steps + LAG * s, range(s, sweeps), states[1:])
    drain(last, states[0])

    device = lax.axis_index("band")
    base = device * blocks_dev - halo
    eig = [above_ref[e * half : (e + 1) * half, :] for e in range(halo)]
    eig += [eig_ref[e * half : (e + 1) * half, :] for e in range(blocks_dev)]
    eig.append(under_ref[...])
    for s in reversed(range(sweeps)):
        lead_rows = s + 1
        for e in range(sweeps - 1 - s + halo - sweeps, halo + blocks_dev):
            spot = jnp.clip(base + e, -1, blocks - 1) + 1
            v = jnp.sum(v_refs[s][spot, 0:1, :] * eye_ref[...], axis=1, keepdims=True)
            tau = tau_refs[s][spot, 0:1, :]
            low, high = eig[e], eig[e + 1]
            mixed = jnp.concatenate([jnp.where(row8 < lead_rows, high[:8], low[:8]), low[8:]], 0)
            inner = tau * jnp.sum(v * mixed, axis=0, keepdims=True)
            mixed = mixed - v * inner
            eig[e] = jnp.concatenate([jnp.where(row8 < lead_rows, low[:8], mixed[:8]), mixed[8:]], 0)
            top = jnp.where(row8 < lead_rows, mixed[:8], high[:8])
            eig[e + 1] = jnp.concatenate([top, high[8:]], 0) if high.shape[0] > 8 else top
    for m in range(blocks_dev):
        eig_out[m * half : (m + 1) * half, :] = eig[halo + m]

    def product(a, b):
        return lax.dot_general(
            a, b, (((0,), (0,)), ((), ())),
            precision=lax.Precision.HIGHEST, preferred_element_type=jnp.float32,
        )

    def stack(k, shift=0, drop=None):
        parts = []
        for a in range(sweeps):
            part = fields[a, last][k + 2]
            part = part if drop is None else jnp.where(row8 == drop, 0.0, part)
            parts.append(pltpu.roll(part, shift, 0) if shift else part)
        return jnp.concatenate(parts, 0)

    def final_d(k):
        outer = jnp.where(col > last, d_ref[k + 2], t_ref[k + 2])
        inner = jnp.where(col > last, l_ref[k + 2], d_ref[k + 3])
        return jnp.where(row > last, outer, inner) - product(stack(k), stack(k, 4))

    def final_l(k):
        outer = jnp.where(col > last, l_ref[k + 2], d_ref[k + 3])
        inner = jnp.where(col > last, 0.0, l_ref[k + 3])
        block = jnp.where(row > last, outer, inner) - product(stack(k + 1, 0, 2), stack(k, 1))
        cleared = jnp.where(k <= steps - 2, sweeps, -1)
        return jnp.where((col == cleared) & (row != sweeps), 0.0, block)

    edge = jnp.concatenate([edge_ref[...], zero[8:]], axis=0)
    bottom, lead = [], []
    for a in range(last):
        bottom.append(jnp.where(row8 == 1, fields[a, last][steps + 2], 0.0))
        lead.append(pltpu.roll(jnp.where(row8 == 3, fields[a, last][steps], 0.0), 6, 0))
    rest = -product(jnp.concatenate(bottom, 0), jnp.concatenate(lead, 0))
    flip = jnp.where((row + col == half) | ((row == 0) & (col == 0)), 1.0, 0.0)
    position = lax.axis_index("cols") * piece_count
    first = device * blocks_dev
    d_last = [final_d(first + m - 1) for m in range(blocks_dev + 1)]
    l_last = [final_l(first + m - 2) for m in range(blocks_dev + 1)]
    top = jnp.where(device == 0, half, 0)
    d_last[0] = jnp.where(row < top, jnp.where(row < sweeps, edge, 0.0), d_last[0])
    l_last[1] = jnp.where(row < top, jnp.where(row >= sweeps, edge, 0.0), l_last[1])
    for m in range(blocks_dev):
        b = first + m
        lim = jnp.where(b > 0, half, 0)
        rest_below = jnp.where(b == steps, half, 0)
        rest_last = jnp.where(b == steps + 1, half, 0)
        d_here, d_before = d_last[m + 1], d_last[m]
        l_here, l_before = l_last[m + 1], l_last[m]
        c0 = jnp.where(
            row >= sweeps, jnp.where(col >= sweeps, d_here, l_here), jnp.where(col < sweeps, d_before, 0.0)
        )
        c1 = jnp.where(
            row >= sweeps,
            jnp.where(col >= sweeps, l_here, jnp.where(row < rest_below, rest, 0.0)),
            jnp.where(col >= sweeps, d_before, l_before),
        )
        c1 = jnp.where(row < lim, c1, 0.0)
        c2 = jnp.where(col >= sweeps, l_before, jnp.where(row < rest_last, rest, 0.0))
        c2 = jnp.where(row < sweeps, c2, 0.0)
        c2 = jnp.where(row < lim, c2, 0.0)
        lower = jnp.where(col <= row, c0, c1)
        upper = jnp.where(col <= row, c1, c2)
        for n, part in enumerate((lower, upper)):
            turned = jnp.dot(part, flip, precision=lax.Precision.HIGHEST)
            turned = pltpu.roll(turned, 0, 1, stride=1, stride_axis=0)
            turn_ref[n * half : (n + 1) * half, :] = turned.T
        band_out[:, m * half : (m + 1) * half] = turn_ref[pl.ds(pl.multiple_of(position, 8), piece_count), :]


def gather_kernel(half, devices, cols, takes, band_ref, eig_ref, all_ref, above_ref, under_ref, rev_ref, sems):
    z_send, z_recv, p_send, p_recv, c_send, c_recv, e_send, e_recv, own_sem = sems
    d, c = lax.axis_index("band"), lax.axis_index("cols")
    count = band_ref.shape[0]
    full = half // count
    pieces = full + 1
    chips = devices // 2
    tall = chips // 2
    chip, core = d // 2, d % 2
    partner = chip * 2 + 1 - core
    spot = (1 - chip % 2) * (chip // 2) + (chip % 2) * (chips - 1 - chip // 2)

    def at(rel):
        ring = (spot + rel + chips) % chips
        turn = ring // tall
        return ((1 - turn) * 2 * ring + turn * (2 * (chips - 1 - ring) + 1)) * 2 + core

    for r in range(count):
        rev_ref[r : r + 1, :] = band_ref[count - 1 - r : count - r, :]

    barrier = pltpu.get_barrier_semaphore()
    peers = [(at(1), c), (at(-1), c), (partner, c)]
    for hop in range(1, len(takes) + 1):
        peers += [((d + hop) % devices, c), ((d - hop + devices) % devices, c)]
    for peer in peers:
        pl.semaphore_signal(barrier, inc=1, device_id=peer, device_id_type=pl.DeviceIdType.MESH)

    @pl.when(c > 0)
    def _():
        pl.semaphore_signal(barrier, inc=1, device_id=(d, c - 1), device_id_type=pl.DeviceIdType.MESH)

    @pl.when(c < cols - 1)
    def _():
        pl.semaphore_signal(barrier, inc=1, device_id=(d, c + 1), device_id_type=pl.DeviceIdType.MESH)

    beside = (c + cols - 1) // cols + 1 - (c + 1) // cols
    pl.semaphore_wait(barrier, len(peers) + beside)

    def send(src, dst, send_sem, recv_sem, device):
        return pltpu.make_async_remote_copy(
            src_ref=src,
            dst_ref=dst,
            send_sem=send_sem,
            recv_sem=recv_sem,
            device_id=device,
            device_id_type=pl.DeviceIdType.MESH,
        )

    def rows_of(p, part):
        first, size = (half - (p + 1) * count, count) if p < full else (half, 8)
        if part is not None and p < full:
            first, size = first + part * (size // 2), size // 2
        return pl.ds(first, size)

    def place(dev, p, part=None):
        return all_ref.at[dev, rows_of(p, part)]

    def source(p):
        return rev_ref if p < full else band_ref.at[pl.ds(0, 8)]

    def along(p, up, src):
        to = (c + 1) % cols if up else (c - 1 + cols) % cols
        return send(src, place(d, p), z_send.at[p, int(up)], z_recv.at[p], (d, to))

    def hops(p):
        for j in range(1, chips // 2 + 1):
            for way in (1, -1):
                if 2 * j < chips:
                    yield j, way, None
                elif p < full:
                    yield j, way, 0 if way == 1 else 1
                elif way == 1:
                    yield j, way, None

    def across(p, j, way, part, src=None):
        dev = at(-way * (j - 1))
        src = place(dev, p, part) if src is None else src
        which = 2 * j + (way + 1) // 2
        return send(src, place(dev, p, part), p_send.at[p, which], p_recv.at[p, which], (at(way), c))

    def pair(p, j, way, part, src=None):
        dev = at(-way * j)
        src = place(dev, p, part) if src is None else src
        which = 2 * j + (way + 1) // 2
        return send(src, place(dev, p, part), c_send.at[p, which], c_recv.at[p, which], (partner, c))

    def own(p):
        return pltpu.make_async_copy(source(p), place(d, p), own_sem)

    def first_hops(p, src):
        for j, way, part in hops(p):
            if j == 1:
                across(p, 1, way, part, src).start()
        pair(p, 0, 1, None, src).start()

    rows_dev = eig_ref.shape[0]
    halos = []
    end = sum(takes)
    for hop, take in enumerate(takes, 1):
        halos.append(
            send(
                eig_ref.at[pl.ds(rows_dev - take, take)],
                above_ref.at[pl.ds(end - take, take)],
                e_send.at[hop],
                e_recv.at[hop],
                ((d + hop) % devices, c),
            )
        )
        end -= take
    halos.append(
        send(eig_ref.at[pl.ds(0, 8)], under_ref, e_send.at[0], e_recv.at[0], ((d - 1 + devices) % devices, c))
    )

    for p in range(pieces):

        @pl.when(c == p)
        def _():
            @pl.when(c < cols - 1)
            def _():
                along(p, True, source(p)).start()

            @pl.when(c > 0)
            def _():
                along(p, False, source(p)).start()

            first_hops(p, source(p))
            own(p).start()

    def receive(p):
        @pl.when(c != p)
        def _():
            along(p, True, place(d, p)).wait_recv()

            @pl.when((c > p) & (c < cols - 1))
            def _():
                along(p, True, place(d, p)).start()

            @pl.when((c < p) & (c > 0))
            def _():
                along(p, False, place(d, p)).start()

            first_hops(p, place(d, p))

    def relay(p, level):
        for j, way, part in hops(p):
            if j == level:
                across(p, j, way, part).wait_recv()
                for j2, way2, part2 in hops(p):
                    if j2 == j + 1 and way2 == way:
                        across(p, j2, way, part2).start()
                pair(p, j, way, part).start()

    for p in reversed(range(pieces)):
        receive(p)
    for halo in halos:
        halo.start()
    for level in range(1, chips // 2 + 1):
        for p in reversed(range(pieces)):
            relay(p, level)
    for p in range(pieces):

        @pl.when(c == p)
        def _():
            own(p).wait()

        @pl.when((c >= p) & (c < cols - 1))
        def _():
            along(p, True, place(d, p)).wait_send()

        @pl.when((c <= p) & (c > 0))
        def _():
            along(p, False, place(d, p)).wait_send()

        for j, way, part in hops(p):
            across(p, j, way, part).wait_send()
            pair(p, j, way, part).wait()
        pair(p, 0, 1, None).wait()
    for halo in halos:
        halo.wait()


def body(band_diagonals, eigenvectors):
    piece_count, rows_dev = band_diagonals.shape
    cols = lax.axis_size("cols")
    double = piece_count * cols
    half = double // 2
    blocks_dev = rows_dev // half
    devices = lax.axis_size("band")
    blocks = blocks_dev * devices
    sweeps = SWEEPS
    halo = sweeps
    columns = eigenvectors.shape[1]
    f32 = jnp.float32
    vmem = pl.BlockSpec(memory_space=pltpu.VMEM)

    takes = []
    while sum(takes) < halo * half:
        takes.append(min(halo * half - sum(takes), rows_dev))
    pieces = half // piece_count + 1
    dma = pltpu.SemaphoreType.DMA
    band, above, under = pl.pallas_call(
        functools.partial(gather_kernel, half, devices, cols, takes),
        out_shape=(
            jax.ShapeDtypeStruct((devices, half + 8, rows_dev), f32),
            jax.ShapeDtypeStruct((halo * half, columns), f32),
            jax.ShapeDtypeStruct((8, columns), f32),
        ),
        in_specs=[vmem] * 2,
        out_specs=(vmem,) * 3,
        scratch_shapes=[
            pltpu.VMEM((piece_count, rows_dev), f32),
            [
                dma((pieces, 2)),
                dma((pieces,)),
                dma((pieces, devices + 2)),
                dma((pieces, devices + 2)),
                dma((pieces, devices + 2)),
                dma((pieces, devices + 2)),
                dma((len(takes) + 1,)),
                dma((len(takes) + 1,)),
                dma,
            ]
        ],
        compiler_params=pltpu.CompilerParams(collective_id=0, has_side_effects=True),
    )(band_diagonals, eigenvectors)

    slots = blocks + 4
    pair_count = sweeps * (sweeps - 1) // 2 + 1
    scratch = (
        [pltpu.VMEM((slots, half, half), f32)] * 3
        + [
            pltpu.VMEM((half, half), f32),
            pltpu.VMEM((8, half), f32),
            pltpu.VMEM((sweeps, 8, half), f32),
            pltpu.VMEM((double, half), f32),
        ]
        + [pltpu.VMEM((blocks + 1, 8, half), f32)] * (2 * sweeps)
        + [pltpu.VMEM((slots, 8, half), f32)] * pair_count
    )
    return pl.pallas_call(
        functools.partial(chase_kernel, blocks, half, blocks_dev, halo, piece_count, sweeps),
        out_shape=(
            jax.ShapeDtypeStruct((piece_count, rows_dev), f32),
            jax.ShapeDtypeStruct((rows_dev, columns), f32),
        ),
        in_specs=[vmem] * 4,
        out_specs=(vmem, vmem),
        scratch_shapes=scratch,
        compiler_params=pltpu.CompilerParams(vmem_limit_bytes=62 * 1024 * 1024),
    )(band, above, eigenvectors, under)


def solution(mesh):
    return jax.shard_map(
        body,
        mesh=mesh,
        in_specs=(P("cols", "band"), P("band", "cols")),
        out_specs=(P("cols", "band"), P("band", "cols")),
        check_vma=False,
    )
```

```python
import functools

import jax
import jax.numpy as jnp
from jax import lax
from jax.experimental import pallas as pl
from jax.experimental.pallas import tpu as pltpu
from jax.sharding import PartitionSpec as P

SWEEPS = 4
LAG = 3
AHEAD = 4
EARLY = 3
UNROLL = 2


def kernel(half, devices, cols, takes, blocks, halo, sweeps, band_in, eig_ref, band_out, eig_out, *refs):
    all_ref, above_ref, under_ref, rev_ref, sems = refs[:5]
    refs = refs[5:]
    d_ref, l_ref, t_ref, eye_ref, edge_ref, raw_ref, turn_ref = refs[:7]
    v_refs = refs[7 : 7 + sweeps]
    tau_refs = refs[7 + sweeps : 7 + 2 * sweeps]
    last = sweeps - 1
    pairs = [(a, b) for b in range(1, sweeps) for a in range(b)] + [(last, last)]
    fields = dict(zip(pairs, refs[7 + 2 * sweeps :]))
    piece_count, blocks_dev = band_in.shape[0], band_in.shape[1] // half
    steps = blocks - 2
    row = lax.broadcasted_iota(jnp.int32, (half, half), 0)
    col = lax.broadcasted_iota(jnp.int32, (half, half), 1)
    eye = row == col
    row8 = lax.broadcasted_iota(jnp.int32, (8, half), 0)
    col8 = lax.broadcasted_iota(jnp.int32, (8, half), 1)
    zero = jnp.zeros((half, half), jnp.float32)
    count = half // 8

    z_send, z_recv, own_sem, x_send, x_recv, p_send, p_recv, e_send, e_recv = sems
    d, c = lax.axis_index("band"), lax.axis_index("cols")
    deep, rows_dev = band_in.shape
    full = half // deep
    pieces = full + 1
    parts = rows_dev // half
    chips = devices // 2
    chip, core = d // 2, d % 2
    partner = chip * 2 + 1 - core

    barrier = pltpu.get_barrier_semaphore()
    peers = [(d, (c + hop) % cols) for hop in range(1, cols)]
    peers += [((chip + hop) % chips * 2 + core, c) for hop in range(1, chips)]
    peers.append((partner, c))
    for hop in range(1, len(takes) + 1):
        peers += [((d + hop) % devices, c), ((d - hop + devices) % devices, c)]
    for peer in peers:
        pl.semaphore_signal(barrier, inc=1, device_id=peer, device_id_type=pl.DeviceIdType.MESH)

    for r in range(deep):
        for m in range(parts):
            rev_ref[m, r : r + 1, :] = band_in[deep - 1 - r : deep - r, m * half : (m + 1) * half]

    for spot in (0, 1, blocks + 2):
        d_ref[spot] = zero
    for spot in (0, blocks + 1):
        l_ref[spot] = zero
        t_ref[spot] = zero
    for ref in v_refs + tau_refs + tuple(fields.values()) + (raw_ref, edge_ref):
        ref[...] = jnp.zeros(ref.shape, jnp.float32)
    eye_ref[...] = jnp.where(eye, 1.0, 0.0)

    pl.semaphore_wait(barrier, len(peers))

    def send(src, dst, send_sem, recv_sem, device):
        return pltpu.make_async_remote_copy(
            src_ref=src,
            dst_ref=dst,
            send_sem=send_sem,
            recv_sem=recv_sem,
            device_id=device,
            device_id_type=pl.DeviceIdType.MESH,
        )

    def rows_of(p):
        return pl.ds(half - (p + 1) * deep, deep) if p < full else pl.ds(half, 8)

    def source(p, m):
        return rev_ref.at[m] if p < full else band_in.at[pl.ds(0, 8), pl.ds(m * half, half)]

    def place(p, m):
        return all_ref.at[d * parts + m, rows_of(p)]

    def along(p, m, to):
        return send(source(p, m), place(p, m), z_send.at[m, to], z_recv.at[p, m], (d, to))

    def own(p, m):
        return pltpu.make_async_copy(source(p, m), place(p, m), own_sem.at[m])

    def chunk(owner, m):
        return all_ref.at[owner * parts + m]

    def across(to, m):
        src = chunk(d, m)
        return send(src, src, x_send.at[to, m], x_recv.at[chip, m], (to * 2 + core, c))

    def arrived(owner, m):
        src = chunk(owner * 2 + core, m)
        return send(src, src, x_send.at[owner, m], x_recv.at[owner, m], (owner * 2 + core, c))

    def share(owner, m):
        src = chunk(owner * 2 + core, m)
        return send(src, src, p_send.at[owner, m], p_recv.at[owner, m], (partner, c))

    halos = []
    end = sum(takes)
    for hop, take in enumerate(takes, 1):
        halos.append(
            send(
                eig_ref.at[pl.ds(rows_dev - take, take)],
                above_ref.at[pl.ds(end - take, take)],
                e_send.at[hop],
                e_recv.at[hop],
                ((d + hop) % devices, c),
            )
        )
        end -= take
    halos.append(
        send(eig_ref.at[pl.ds(0, 8)], under_ref, e_send.at[0], e_recv.at[0], ((d - 1 + devices) % devices, c))
    )

    for p in range(pieces):

        @pl.when(c == p)
        def _():
            for m in range(parts):
                for to in reversed(range(cols)):
                    if to != p:
                        along(p, m, to).start()
                own(p, m).start()

    for copy in halos:
        copy.start()

    for m in range(parts):
        for p in range(pieces):

            @pl.when(c == p)
            def _():
                own(p, m).wait()

            @pl.when(c != p)
            def _():
                along(p, m, c).wait_recv()

        for to in reversed(range(chips)):

            @pl.when(chip != to)
            def _():
                across(to, m).start()

        share(chip, m).start()

    def sides(block):
        owner, m = block // parts, block % parts
        return owner // 2, owner % 2, m

    def duty(block):
        owner, side, m = sides(block)

        @pl.when((side == core) & (owner != chip) & (block < blocks))
        def _():
            arrived(owner, m).wait_recv()
            share(owner, m).start()

    def need(block):
        owner, side, m = sides(block)

        @pl.when((side != core) & (block < blocks))
        def _():
            share(owner, m).wait_recv()

    def unpack(block):
        piece = all_ref[block, :half]
        extra = all_ref[block, half : half + 1]
        rows = pltpu.roll(piece.T, 1, 1, stride=1, stride_axis=0)
        turned = rows.T
        extra = jnp.where(eye, jnp.broadcast_to(extra, (half, half)), 0.0)
        d_ref[block + 2] = jnp.where(row >= col, rows, turned)
        l_ref[block + 1] = jnp.where(col > row, rows, extra)
        t_ref[block + 1] = jnp.where(row > col, turned, extra)

    def tile(ref, k, i=0):
        return ref[k + 2, 8 * i : 8 * i + 8, :]

    def lanes(x):
        return jnp.broadcast_to(jnp.sum(x, axis=1, keepdims=True), (8, half))

    def rows_sum(x):
        return jnp.broadcast_to(jnp.sum(x, axis=0, keepdims=True), (8, half))

    def at_lane(x, spot):
        return jnp.broadcast_to(x[:, spot : spot + 1], (8, half))

    def total(parts):
        while len(parts) > 1:
            rest = parts[len(parts) // 2 * 2 :]
            parts = [a + b for a, b in zip(parts[::2], parts[1::2])] + rest
        return parts[0]

    def to_lane(x, fill, spot):
        return jnp.where(col8 == spot, fill, x)

    def norms(x, new):
        rest = lanes(to_lane(x * x, 0.0, new))
        top = at_lane(x, new)
        square = rest + top * top
        inverse = lax.rsqrt(square)
        return rest, top, square * inverse, inverse

    def wide(line):
        return jnp.broadcast_to(line, (8, half))

    def begin(s):
        base = wide(d_ref[2, s : s + 1, :])
        x = jnp.where(col8 > s, base, wide(t_ref[2, s : s + 1, :]))
        diagonal = base
        for a in range(s):
            raw = raw_ref[a]
            x = x - rows_sum(fields[a, s][2] * at_lane(raw, s))
            diagonal = diagonal - 2.0 * raw[0:1, :] * raw[4:5, :]
        length = norms(x, s + 1)[2]
        edge = jnp.where((row8 == s) & (col8 == s), diagonal, edge_ref[...])
        edge_ref[...] = jnp.where((row8 == s + 1) & (col8 == s), -length, edge)
        return (x,) + (jnp.zeros((8, half), jnp.float32),) * 4

    def targets(s):
        return range(s + 1, sweeps) if s < last else (last,)

    def settle(s, k, inside, v, tau):
        inside = inside - 0.5 * tau * lanes(v * inside) * v
        for b in targets(s):
            ref = fields[s, b]
            other = (col8 > s) & (col8 <= b)
            ref[k + 2, 4:5, :] = jnp.where(other, wide(ref[k + 2, 4:5, :]), inside)[0:1]
            if b > s:
                ref[k + 1, 7:8, :] = jnp.where(other, inside, wide(ref[k + 1, 7:8, :]))[0:1]
        if s < last:
            raw_ref[s, 0:1, :] = jnp.where(col8 < jnp.where(k == 0, half, 0), inside, wide(raw_ref[s, 0:1, :]))[0:1]

    def chain(s, k, x, hung, inside_past, v_past, tau_past):
        new = s + 1
        main = col8 > s
        x_col = [
            jnp.sum(x * eye_ref[8 * i : 8 * i + 8, :], axis=1, keepdims=True) for i in range(count)
        ]
        rest, top, length, inverse = norms(x, new)
        x_main = jnp.where(row8 > s, x_col[0], 0.0)
        x_tail = jnp.where(row8 > s, 0.0, x_col[0])

        def times(ref, spot, extra):
            parts = [tile(ref, spot, i) * x_col[i] for i in range(1, count)]
            return total(parts + [tile(ref, spot) * x_main] + extra)

        here = times(d_ref, k, [tile(l_ref, k) * x_tail])
        after = times(t_ref, k, [tile(d_ref, k + 1) * x_tail])
        beyond = tile(t_ref, k + 1) * x_tail
        before = times(l_ref, k - 1, [])
        here_top = wide(d_ref[k + 2, new : new + 1, :])
        after_top = wide(t_ref[k + 2, new : new + 1, :])
        before_top = wide(l_ref[k + 1, new : new + 1, :])
        inside = jnp.where(main, here, after)
        beneath = jnp.where(main, after, beyond)
        across = jnp.where(main, before, here)
        fixes = []
        for a in range(s):
            now = fields[a, s][k + 2]
            up = jnp.where(row8 == 1, 0.0, fields[a, s][k + 1])
            down = jnp.where(row8 == 2, 0.0, fields[a, s][k + 3])
            unit = at_lane(now, new)
            dots = lanes(now * x)
            beneath = beneath - down * pltpu.roll(dots, 1, 0)
            fixes.append(down * pltpu.roll(unit, 1, 0))
            dots = dots + length * unit
            inside = inside - now * pltpu.roll(dots, 4, 0)
            across = across - up * pltpu.roll(dots, 7, 0)
        beneath = rows_sum(beneath)
        x_next = beneath * -inverse
        column = jnp.where(main, after_top, 0.0)
        if fixes:
            column = column - rows_sum(total(fixes))
        hang = lanes(hung * x) + length * at_lane(hung, new)
        v_top = top + length
        tau = 2.0 / (rest + v_top * v_top)
        v = to_lane(x, v_top, new)
        beneath = tau * (beneath + length * column)
        inside = tau * (rows_sum(inside) + length * jnp.where(main, here_top, after_top))
        across = tau * (rows_sum(across) + length * jnp.where(main, before_top, here_top) - v_past * hang)

        settle(s, k - 1, inside_past, v_past, tau_past)
        v_refs[s][k + 1] = v
        tau_refs[s][k + 1] = tau
        for b in targets(s):
            ref = fields[s, b]
            other = (col8 > s) & (col8 <= b)
            ref[k + 2, 0:1, :] = jnp.where(other, 0.0, v)[0:1]
            ref[k + 1, 7:8, :] = across[0:1]
            ref[k + 3, 1:2, :] = jnp.where(other, 0.0, beneath)[0:1]
            if b > s:
                ref[k + 2, 4:5, :] = beneath[0:1]
                ref[k + 1, 3:4, :] = jnp.where(other, v, 0.0)[0:1]
                ref[k, 2:3, :] = jnp.where(other, across, 0.0)[0:1]
        if s < last:
            raw_ref[s, 3:4, :] = jnp.where(col8 < jnp.where(k == 1, half, 0), across, wide(raw_ref[s, 3:4, :]))[0:1]
            raw_ref[s, 4:5, :] = jnp.where(col8 < jnp.where(k == 0, half, 0), v, wide(raw_ref[s, 4:5, :]))[0:1]
        return x_next, beneath, inside, v, tau

    def phase(start, stop, chains, states):
        def wave(t, states):
            done = {s: chain(s, t - LAG * s, *state) for s, state in reversed(list(zip(chains, states)))}
            if start < steps:
                unpack(jnp.minimum(t + AHEAD, blocks - 1))
            return tuple(done[s] for s in chains)

        def turn(t, states, size):
            if start < steps:
                for more in range(size):
                    duty(t + more + AHEAD + EARLY)
                for more in range(size):
                    need(t + more + AHEAD)
            for more in range(size):
                states = wave(t + more, states)
            return states

        size = min(UNROLL, stop - start)
        turns = (stop - start) // size
        states = lax.fori_loop(0, turns, lambda i, st: turn(start + i * size, st, size), tuple(states))
        if start + turns * size < stop:
            states = turn(start + turns * size, states, stop - start - turns * size)
        return states

    def drain(s, state):
        settle(s, steps - 1, *state[2:])

    for block in range(AHEAD + EARLY):
        duty(block)
    for block in range(AHEAD):
        need(block)
        unpack(block)
    states = ()
    for s in range(last):
        states = phase(LAG * s, LAG * (s + 1), range(s + 1), states + (begin(s),))
    states = phase(LAG * last, steps, range(sweeps), states + (begin(last),))
    for s in range(1, sweeps):
        drain(s - 1, states[0])
        states = phase(steps + LAG * (s - 1), steps + LAG * s, range(s, sweeps), states[1:])
    drain(last, states[0])

    for m in range(parts):
        for p in range(pieces):

            @pl.when(c == p)
            def _():
                for to in range(cols):
                    if to != p:
                        along(p, m, to).wait_send()

        for owner in range(chips):

            @pl.when(chip != owner)
            def _():
                across(owner, m).wait_send()

            share(owner, m).wait_send()
    for copy in halos:
        copy.wait()

    device = lax.axis_index("band")
    base = device * blocks_dev - halo
    eig = [above_ref[e * half : (e + 1) * half, :] for e in range(halo)]
    eig += [eig_ref[e * half : (e + 1) * half, :] for e in range(blocks_dev)]
    eig.append(under_ref[...])
    for s in reversed(range(sweeps)):
        lead_rows = s + 1
        for e in range(sweeps - 1 - s + halo - sweeps, halo + blocks_dev):
            spot = jnp.clip(base + e, -1, blocks - 1) + 1
            v = jnp.sum(v_refs[s][spot, 0:1, :] * eye_ref[...], axis=1, keepdims=True)
            tau = tau_refs[s][spot, 0:1, :]
            low, high = eig[e], eig[e + 1]
            mixed = jnp.concatenate([jnp.where(row8 < lead_rows, high[:8], low[:8]), low[8:]], 0)
            inner = tau * jnp.sum(v * mixed, axis=0, keepdims=True)
            mixed = mixed - v * inner
            eig[e] = jnp.concatenate([jnp.where(row8 < lead_rows, low[:8], mixed[:8]), mixed[8:]], 0)
            top = jnp.where(row8 < lead_rows, mixed[:8], high[:8])
            eig[e + 1] = jnp.concatenate([top, high[8:]], 0) if high.shape[0] > 8 else top
    for m in range(blocks_dev):
        eig_out[m * half : (m + 1) * half, :] = eig[halo + m]

    def product(a, b):
        return lax.dot_general(
            a, b, (((0,), (0,)), ((), ())),
            precision=lax.Precision.HIGHEST, preferred_element_type=jnp.float32,
        )

    def stack(k, shift=0, drop=None):
        parts = []
        for a in range(sweeps):
            part = fields[a, last][k + 2]
            part = part if drop is None else jnp.where(row8 == drop, 0.0, part)
            parts.append(pltpu.roll(part, shift, 0) if shift else part)
        return jnp.concatenate(parts, 0)

    def final_d(k):
        outer = jnp.where(col > last, d_ref[k + 2], t_ref[k + 2])
        inner = jnp.where(col > last, l_ref[k + 2], d_ref[k + 3])
        return jnp.where(row > last, outer, inner) - product(stack(k), stack(k, 4))

    def final_l(k):
        outer = jnp.where(col > last, l_ref[k + 2], d_ref[k + 3])
        inner = jnp.where(col > last, 0.0, l_ref[k + 3])
        block = jnp.where(row > last, outer, inner) - product(stack(k + 1, 0, 2), stack(k, 1))
        cleared = jnp.where(k <= steps - 2, sweeps, -1)
        return jnp.where((col == cleared) & (row != sweeps), 0.0, block)

    edge = jnp.concatenate([edge_ref[...], zero[8:]], axis=0)
    bottom, lead = [], []
    for a in range(last):
        bottom.append(jnp.where(row8 == 1, fields[a, last][steps + 2], 0.0))
        lead.append(pltpu.roll(jnp.where(row8 == 3, fields[a, last][steps], 0.0), 6, 0))
    rest = -product(jnp.concatenate(bottom, 0), jnp.concatenate(lead, 0))
    flip = jnp.where((row + col == half) | ((row == 0) & (col == 0)), 1.0, 0.0)
    position = lax.axis_index("cols") * piece_count
    first = device * blocks_dev
    d_last = [final_d(first + m - 1) for m in range(blocks_dev + 1)]
    l_last = [final_l(first + m - 2) for m in range(blocks_dev + 1)]
    top = jnp.where(device == 0, half, 0)
    d_last[0] = jnp.where(row < top, jnp.where(row < sweeps, edge, 0.0), d_last[0])
    l_last[1] = jnp.where(row < top, jnp.where(row >= sweeps, edge, 0.0), l_last[1])
    for m in range(blocks_dev):
        b = first + m
        lim = jnp.where(b > 0, half, 0)
        rest_below = jnp.where(b == steps, half, 0)
        rest_last = jnp.where(b == steps + 1, half, 0)
        d_here, d_before = d_last[m + 1], d_last[m]
        l_here, l_before = l_last[m + 1], l_last[m]
        c0 = jnp.where(
            row >= sweeps, jnp.where(col >= sweeps, d_here, l_here), jnp.where(col < sweeps, d_before, 0.0)
        )
        c1 = jnp.where(
            row >= sweeps,
            jnp.where(col >= sweeps, l_here, jnp.where(row < rest_below, rest, 0.0)),
            jnp.where(col >= sweeps, d_before, l_before),
        )
        c1 = jnp.where(row < lim, c1, 0.0)
        c2 = jnp.where(col >= sweeps, l_before, jnp.where(row < rest_last, rest, 0.0))
        c2 = jnp.where(row < sweeps, c2, 0.0)
        c2 = jnp.where(row < lim, c2, 0.0)
        lower = jnp.where(col <= row, c0, c1)
        upper = jnp.where(col <= row, c1, c2)
        for n, part in enumerate((lower, upper)):
            turned = jnp.dot(part, flip, precision=lax.Precision.HIGHEST)
            turned = pltpu.roll(turned, 0, 1, stride=1, stride_axis=0)
            turn_ref[n * half : (n + 1) * half, :] = turned.T
        band_out[:, m * half : (m + 1) * half] = turn_ref[pl.ds(pl.multiple_of(position, 8), piece_count), :]


def body(band_diagonals, eigenvectors):
    piece_count, rows_dev = band_diagonals.shape
    cols = lax.axis_size("cols")
    double = piece_count * cols
    half = double // 2
    blocks_dev = rows_dev // half
    devices = lax.axis_size("band")
    blocks = blocks_dev * devices
    sweeps = SWEEPS
    halo = sweeps
    columns = eigenvectors.shape[1]
    f32 = jnp.float32
    vmem = pl.BlockSpec(memory_space=pltpu.VMEM)

    takes = []
    while sum(takes) < halo * half:
        takes.append(min(halo * half - sum(takes), rows_dev))
    pieces = half // piece_count + 1
    dma = pltpu.SemaphoreType.DMA
    slots = blocks + 4
    pair_count = sweeps * (sweeps - 1) // 2 + 1
    scratch = (
        [
            pltpu.VMEM((blocks, half + 8, half), f32),
            pltpu.VMEM((halo * half, columns), f32),
            pltpu.VMEM((8, columns), f32),
            pltpu.VMEM((blocks_dev, piece_count, half), f32),
            [
                dma((blocks_dev, cols)),
                dma((pieces, blocks_dev)),
                dma((blocks_dev,)),
                dma((devices // 2, blocks_dev)),
                dma((devices // 2, blocks_dev)),
                dma((devices // 2, blocks_dev)),
                dma((devices // 2, blocks_dev)),
                dma((len(takes) + 1,)),
                dma((len(takes) + 1,)),
            ],
        ]
        + [pltpu.VMEM((slots, half, half), f32)] * 3
        + [
            pltpu.VMEM((half, half), f32),
            pltpu.VMEM((8, half), f32),
            pltpu.VMEM((sweeps, 8, half), f32),
            pltpu.VMEM((double, half), f32),
        ]
        + [pltpu.VMEM((blocks + 1, 8, half), f32)] * (2 * sweeps)
        + [pltpu.VMEM((slots, 8, half), f32)] * pair_count
    )
    return pl.pallas_call(
        functools.partial(kernel, half, devices, cols, takes, blocks, halo, sweeps),
        out_shape=(
            jax.ShapeDtypeStruct((piece_count, rows_dev), f32),
            jax.ShapeDtypeStruct((rows_dev, columns), f32),
        ),
        in_specs=[vmem] * 2,
        out_specs=(vmem, vmem),
        scratch_shapes=scratch,
        compiler_params=pltpu.CompilerParams(
            collective_id=0, has_side_effects=True, vmem_limit_bytes=62 * 1024 * 1024
        ),
    )(band_diagonals, eigenvectors)


def solution(mesh):
    return jax.shard_map(
        body,
        mesh=mesh,
        in_specs=(P("cols", "band"), P("band", "cols")),
        out_specs=(P("cols", "band"), P("band", "cols")),
        check_vma=False,
    )
```

```python
import functools

import jax
import jax.numpy as jnp
from jax import lax
from jax.experimental import pallas as pl
from jax.experimental.pallas import tpu as pltpu
from jax.sharding import PartitionSpec as P

SWEEPS = 4
LAG = 3
AHEAD = 4
EARLY = 3
UNROLL = 2


def kernel(half, devices, cols, takes, blocks, halo, sweeps, band_ref, eig_ref, *refs):
    field_out, v_out, tau_out, above_ref, under_ref = refs[:5]
    all_ref, band_in, rev_ref, in_sem, sems = refs[5:10]
    refs = refs[10:]
    d_ref, l_ref, t_ref, eye_ref, raw_ref = refs[:5]
    v_refs = refs[5 : 5 + sweeps]
    tau_refs = refs[5 + sweeps : 5 + 2 * sweeps]
    last = sweeps - 1
    pairs = [(a, b) for b in range(1, sweeps) for a in range(b)] + [(last, last)]
    fields = dict(zip(pairs, refs[5 + 2 * sweeps :]))
    blocks_dev = band_ref.shape[1] // half
    steps = blocks - 2
    row = lax.broadcasted_iota(jnp.int32, (half, half), 0)
    col = lax.broadcasted_iota(jnp.int32, (half, half), 1)
    eye = row == col
    row8 = lax.broadcasted_iota(jnp.int32, (8, half), 0)
    col8 = lax.broadcasted_iota(jnp.int32, (8, half), 1)
    zero = jnp.zeros((half, half), jnp.float32)
    count = half // 8

    z_send, z_recv, own_sem, x_send, x_recv, p_send, p_recv, e_send, e_recv = sems
    d, c = lax.axis_index("band"), lax.axis_index("cols")
    deep, rows_dev = band_ref.shape
    full = half // deep
    pieces = full + 1
    parts = rows_dev // half
    chips = devices // 2
    chip, core = d // 2, d % 2
    partner = chip * 2 + 1 - core

    inward = pltpu.make_async_copy(band_ref, band_in, in_sem)
    inward.start()
    barrier = pltpu.get_barrier_semaphore()
    peers = [(d, (c + hop) % cols) for hop in range(1, cols)]
    peers += [((chip + hop) % chips * 2 + core, c) for hop in range(1, chips)]
    peers.append((partner, c))
    for hop in range(1, len(takes) + 1):
        peers += [((d + hop) % devices, c), ((d - hop + devices) % devices, c)]
    for peer in peers:
        pl.semaphore_signal(barrier, inc=1, device_id=peer, device_id_type=pl.DeviceIdType.MESH)

    for spot in (0, 1, blocks + 2):
        d_ref[spot] = zero
    for spot in (0, blocks + 1):
        l_ref[spot] = zero
        t_ref[spot] = zero
    for ref in v_refs + tau_refs + tuple(fields.values()) + (raw_ref,):
        ref[...] = jnp.zeros(ref.shape, jnp.float32)
    eye_ref[...] = jnp.where(eye, 1.0, 0.0)

    inward.wait()
    for r in range(deep):
        for m in range(parts):
            rev_ref[m, r : r + 1, :] = band_in[deep - 1 - r : deep - r, m * half : (m + 1) * half]

    pl.semaphore_wait(barrier, len(peers))

    def send(src, dst, send_sem, recv_sem, device):
        return pltpu.make_async_remote_copy(
            src_ref=src,
            dst_ref=dst,
            send_sem=send_sem,
            recv_sem=recv_sem,
            device_id=device,
            device_id_type=pl.DeviceIdType.MESH,
        )

    def rows_of(p):
        return pl.ds(half - (p + 1) * deep, deep) if p < full else pl.ds(half, 8)

    def source(p, m):
        return rev_ref.at[m] if p < full else band_in.at[pl.ds(0, 8), pl.ds(m * half, half)]

    def place(p, m):
        return all_ref.at[d * parts + m, rows_of(p)]

    def along(p, m, to):
        return send(source(p, m), place(p, m), z_send.at[m, to], z_recv.at[p, m], (d, to))

    def own(p, m):
        return pltpu.make_async_copy(source(p, m), place(p, m), own_sem.at[m])

    def chunk(owner, m):
        return all_ref.at[owner * parts + m]

    def across(to, m):
        src = chunk(d, m)
        return send(src, src, x_send.at[to, m], x_recv.at[chip, m], (to * 2 + core, c))

    def arrived(owner, m):
        src = chunk(owner * 2 + core, m)
        return send(src, src, x_send.at[owner, m], x_recv.at[owner, m], (owner * 2 + core, c))

    def share(owner, m):
        src = chunk(owner * 2 + core, m)
        return send(src, src, p_send.at[owner, m], p_recv.at[owner, m], (partner, c))

    halos = []
    end = sum(takes)
    for hop, take in enumerate(takes, 1):
        halos.append(
            send(
                eig_ref.at[pl.ds(rows_dev - take, take)],
                above_ref.at[pl.ds(end - take, take)],
                e_send.at[hop],
                e_recv.at[hop],
                ((d + hop) % devices, c),
            )
        )
        end -= take
    halos.append(
        send(eig_ref.at[pl.ds(0, 8)], under_ref, e_send.at[0], e_recv.at[0], ((d - 1 + devices) % devices, c))
    )

    for p in range(pieces):

        @pl.when(c == p)
        def _():
            for m in range(parts):
                for to in reversed(range(cols)):
                    if to != p:
                        along(p, m, to).start()
                own(p, m).start()

    for copy in halos:
        copy.start()

    for m in range(parts):
        for p in range(pieces):

            @pl.when(c == p)
            def _():
                own(p, m).wait()

            @pl.when(c != p)
            def _():
                along(p, m, c).wait_recv()

        for to in reversed(range(chips)):

            @pl.when(chip != to)
            def _():
                across(to, m).start()

        share(chip, m).start()

    def sides(block):
        owner, m = block // parts, block % parts
        return owner // 2, owner % 2, m

    def duty(block):
        owner, side, m = sides(block)

        @pl.when((side == core) & (owner != chip) & (block < blocks))
        def _():
            arrived(owner, m).wait_recv()
            share(owner, m).start()

    def need(block):
        owner, side, m = sides(block)

        @pl.when((side != core) & (block < blocks))
        def _():
            share(owner, m).wait_recv()

    def unpack(block):
        piece = all_ref[block, :half]
        extra = all_ref[block, half : half + 1]
        rows = pltpu.roll(piece.T, 1, 1, stride=1, stride_axis=0)
        turned = rows.T
        extra = jnp.where(eye, jnp.broadcast_to(extra, (half, half)), 0.0)
        d_ref[block + 2] = jnp.where(row >= col, rows, turned)
        l_ref[block + 1] = jnp.where(col > row, rows, extra)
        t_ref[block + 1] = jnp.where(row > col, turned, extra)

    def tile(ref, k, i=0):
        return ref[k + 2, 8 * i : 8 * i + 8, :]

    def lanes(x):
        return jnp.broadcast_to(jnp.sum(x, axis=1, keepdims=True), (8, half))

    def rows_sum(x):
        return jnp.broadcast_to(jnp.sum(x, axis=0, keepdims=True), (8, half))

    def at_lane(x, spot):
        return jnp.broadcast_to(x[:, spot : spot + 1], (8, half))

    def total(parts):
        while len(parts) > 1:
            rest = parts[len(parts) // 2 * 2 :]
            parts = [a + b for a, b in zip(parts[::2], parts[1::2])] + rest
        return parts[0]

    def to_lane(x, fill, spot):
        return jnp.where(col8 == spot, fill, x)

    def norms(x, new):
        rest = lanes(to_lane(x * x, 0.0, new))
        top = at_lane(x, new)
        square = rest + top * top
        inverse = lax.rsqrt(square)
        return rest, top, square * inverse, inverse

    def wide(line):
        return jnp.broadcast_to(line, (8, half))

    def begin(s):
        x = jnp.where(col8 > s, wide(d_ref[2, s : s + 1, :]), wide(t_ref[2, s : s + 1, :]))
        for a in range(s):
            x = x - rows_sum(fields[a, s][2] * at_lane(raw_ref[a], s))
        return (x,) + (jnp.zeros((8, half), jnp.float32),) * 4

    def targets(s):
        return range(s + 1, sweeps) if s < last else (last,)

    def settle(s, k, inside, v, tau):
        inside = inside - 0.5 * tau * lanes(v * inside) * v
        for b in targets(s):
            ref = fields[s, b]
            other = (col8 > s) & (col8 <= b)
            ref[k + 2, 4:5, :] = jnp.where(other, wide(ref[k + 2, 4:5, :]), inside)[0:1]
            if b > s:
                ref[k + 1, 7:8, :] = jnp.where(other, inside, wide(ref[k + 1, 7:8, :]))[0:1]
        if s < last:
            raw_ref[s, 0:1, :] = jnp.where(col8 < jnp.where(k == 0, half, 0), inside, wide(raw_ref[s, 0:1, :]))[0:1]

    def chain(s, k, x, hung, inside_past, v_past, tau_past):
        new = s + 1
        main = col8 > s
        x_col = [
            jnp.sum(x * eye_ref[8 * i : 8 * i + 8, :], axis=1, keepdims=True) for i in range(count)
        ]
        rest, top, length, inverse = norms(x, new)
        x_main = jnp.where(row8 > s, x_col[0], 0.0)
        x_tail = jnp.where(row8 > s, 0.0, x_col[0])

        def times(ref, spot, extra):
            parts = [tile(ref, spot, i) * x_col[i] for i in range(1, count)]
            return total(parts + [tile(ref, spot) * x_main] + extra)

        here = times(d_ref, k, [tile(l_ref, k) * x_tail])
        after = times(t_ref, k, [tile(d_ref, k + 1) * x_tail])
        beyond = tile(t_ref, k + 1) * x_tail
        before = times(l_ref, k - 1, [])
        here_top = wide(d_ref[k + 2, new : new + 1, :])
        after_top = wide(t_ref[k + 2, new : new + 1, :])
        before_top = wide(l_ref[k + 1, new : new + 1, :])
        inside = jnp.where(main, here, after)
        beneath = jnp.where(main, after, beyond)
        across = jnp.where(main, before, here)
        fixes = []
        for a in range(s):
            now = fields[a, s][k + 2]
            up = jnp.where(row8 == 1, 0.0, fields[a, s][k + 1])
            down = jnp.where(row8 == 2, 0.0, fields[a, s][k + 3])
            unit = at_lane(now, new)
            dots = lanes(now * x)
            beneath = beneath - down * pltpu.roll(dots, 1, 0)
            fixes.append(down * pltpu.roll(unit, 1, 0))
            dots = dots + length * unit
            inside = inside - now * pltpu.roll(dots, 4, 0)
            across = across - up * pltpu.roll(dots, 7, 0)
        beneath = rows_sum(beneath)
        x_next = beneath * -inverse
        column = jnp.where(main, after_top, 0.0)
        if fixes:
            column = column - rows_sum(total(fixes))
        hang = lanes(hung * x) + length * at_lane(hung, new)
        v_top = top + length
        tau = 2.0 / (rest + v_top * v_top)
        v = to_lane(x, v_top, new)
        beneath = tau * (beneath + length * column)
        inside = tau * (rows_sum(inside) + length * jnp.where(main, here_top, after_top))
        across = tau * (rows_sum(across) + length * jnp.where(main, before_top, here_top) - v_past * hang)

        settle(s, k - 1, inside_past, v_past, tau_past)
        v_refs[s][k + 1] = v
        tau_refs[s][k + 1] = tau
        for b in targets(s):
            ref = fields[s, b]
            other = (col8 > s) & (col8 <= b)
            ref[k + 2, 0:1, :] = jnp.where(other, 0.0, v)[0:1]
            ref[k + 1, 7:8, :] = across[0:1]
            ref[k + 3, 1:2, :] = jnp.where(other, 0.0, beneath)[0:1]
            if b > s:
                ref[k + 2, 4:5, :] = beneath[0:1]
                ref[k + 1, 3:4, :] = jnp.where(other, v, 0.0)[0:1]
                ref[k, 2:3, :] = jnp.where(other, across, 0.0)[0:1]
        if s < last:
            raw_ref[s, 3:4, :] = jnp.where(col8 < jnp.where(k == 1, half, 0), across, wide(raw_ref[s, 3:4, :]))[0:1]
            raw_ref[s, 4:5, :] = jnp.where(col8 < jnp.where(k == 0, half, 0), v, wide(raw_ref[s, 4:5, :]))[0:1]
        return x_next, beneath, inside, v, tau

    def phase(start, stop, chains, states):
        def wave(t, states):
            done = {s: chain(s, t - LAG * s, *state) for s, state in reversed(list(zip(chains, states)))}
            if start < steps:
                unpack(jnp.minimum(t + AHEAD, blocks - 1))
            return tuple(done[s] for s in chains)

        def turn(t, states, size):
            if start < steps:
                for more in range(size):
                    duty(t + more + AHEAD + EARLY)
                for more in range(size):
                    need(t + more + AHEAD)
            for more in range(size):
                states = wave(t + more, states)
            return states

        size = min(UNROLL, stop - start)
        turns = (stop - start) // size
        states = lax.fori_loop(0, turns, lambda i, st: turn(start + i * size, st, size), tuple(states))
        if start + turns * size < stop:
            states = turn(start + turns * size, states, stop - start - turns * size)
        return states

    def drain(s, state):
        settle(s, steps - 1, *state[2:])

    for block in range(AHEAD + EARLY):
        duty(block)
    for block in range(AHEAD):
        need(block)
        unpack(block)
    states = ()
    for s in range(last):
        states = phase(LAG * s, LAG * (s + 1), range(s + 1), states + (begin(s),))
    states = phase(LAG * last, steps, range(sweeps), states + (begin(last),))
    for s in range(1, sweeps):
        drain(s - 1, states[0])
        states = phase(steps + LAG * (s - 1), steps + LAG * s, range(s, sweeps), states[1:])
    drain(last, states[0])

    for m in range(parts):
        for p in range(pieces):

            @pl.when(c == p)
            def _():
                for to in range(cols):
                    if to != p:
                        along(p, m, to).wait_send()

        for owner in range(chips):

            @pl.when(chip != owner)
            def _():
                across(owner, m).wait_send()

            share(owner, m).wait_send()
    for copy in halos:
        copy.wait()

    first = d * parts
    for s in range(sweeps):
        for e in range(halo + parts):
            spot = jnp.clip(first - halo + e, -1, blocks - 1) + 1
            v_out[s, e : e + 1, :] = v_refs[s][spot, 0:1, :]
            tau_out[s, e : e + 1, :] = tau_refs[s][spot, 0:1, :]
        for n in range(parts + 2):
            field_out[s, n] = fields[s, last][first + n]


def finish_kernel(half, blocks, halo, sweeps, *refs):
    band_ref, eig_ref, field_ref, v_ref, tau_ref, above_ref, under_ref, band_out, eig_out, turn_ref = refs
    piece_count, blocks_dev = band_ref.shape[0], band_ref.shape[1] // half
    steps = blocks - 2
    row = lax.broadcasted_iota(jnp.int32, (half, half), 0)
    col = lax.broadcasted_iota(jnp.int32, (half, half), 1)
    eye = row == col
    row8 = lax.broadcasted_iota(jnp.int32, (8, half), 0)
    device = lax.axis_index("band")
    first = device * blocks_dev
    eig = [above_ref[e * half : (e + 1) * half, :] for e in range(halo)]
    eig += [eig_ref[e * half : (e + 1) * half, :] for e in range(blocks_dev)]
    eig.append(under_ref[...])
    for s in reversed(range(sweeps)):
        lead_rows = s + 1
        for e in range(sweeps - 1 - s + halo - sweeps, halo + blocks_dev):
            v = jnp.sum(jnp.where(eye, v_ref[s, e : e + 1, :], 0.0), axis=1, keepdims=True)
            tau = tau_ref[s, e : e + 1, :]
            low, high = eig[e], eig[e + 1]
            mixed = jnp.concatenate([jnp.where(row8 < lead_rows, high[:8], low[:8]), low[8:]], 0)
            inner = tau * jnp.sum(v * mixed, axis=0, keepdims=True)
            mixed = mixed - v * inner
            eig[e] = jnp.concatenate([jnp.where(row8 < lead_rows, low[:8], mixed[:8]), mixed[8:]], 0)
            top = jnp.where(row8 < lead_rows, mixed[:8], high[:8])
            eig[e + 1] = jnp.concatenate([top, high[8:]], 0) if high.shape[0] > 8 else top
    for m in range(blocks_dev):
        eig_out[m * half : (m + 1) * half, :] = eig[halo + m]

    def product(a, b):
        return lax.dot_general(
            a, b, (((0,), (0,)), ((), ())),
            precision=lax.Precision.HIGHEST, preferred_element_type=jnp.float32,
        )

    def stack(n, shift=0, drop=None):
        parts = []
        for a in range(sweeps):
            part = field_ref[a, n]
            part = part if drop is None else jnp.where(row8 == drop, 0.0, part)
            parts.append(pltpu.roll(part, shift, 0) if shift else part)
        return jnp.concatenate(parts, 0)

    bottom, lead = [], []
    for a in range(sweeps - 1):
        bottom.append(jnp.where(row8 == 1, field_ref[a, blocks_dev], 0.0))
        lead.append(pltpu.roll(jnp.where(row8 == 3, field_ref[a, blocks_dev - 2], 0.0), 6, 0))
    rest = -product(jnp.concatenate(bottom, 0), jnp.concatenate(lead, 0))
    flip = jnp.where((row + col == half) | ((row == 0) & (col == 0)), 1.0, 0.0)
    position = lax.axis_index("cols") * piece_count
    d_last = [-product(stack(m + 1), stack(m + 1, 4)) for m in range(blocks_dev + 1)]
    l_last = [-product(stack(m + 1, 0, 2), stack(m, 1)) for m in range(blocks_dev + 1)]
    diagonal = position + lax.broadcasted_iota(jnp.int32, (piece_count, half), 0)
    across = lax.broadcasted_iota(jnp.int32, (piece_count, half), 1)
    for m in range(blocks_dev):
        b = first + m
        lim = jnp.where(b > 0, half, 0)
        rest_below = jnp.where(b == steps, half, 0)
        rest_last = jnp.where(b == steps + 1, half, 0)
        d_here, d_before = d_last[m + 1], d_last[m]
        l_here, l_before = l_last[m + 1], l_last[m]
        c0 = jnp.where(
            row >= sweeps, jnp.where(col >= sweeps, d_here, l_here), jnp.where(col < sweeps, d_before, 0.0)
        )
        c1 = jnp.where(
            row >= sweeps,
            jnp.where(col >= sweeps, l_here, jnp.where(row < rest_below, rest, 0.0)),
            jnp.where(col >= sweeps, d_before, l_before),
        )
        c1 = jnp.where(row < lim, c1, 0.0)
        c2 = jnp.where(col >= sweeps, l_before, jnp.where(row < rest_last, rest, 0.0))
        c2 = jnp.where(row < sweeps, c2, 0.0)
        c2 = jnp.where(row < lim, c2, 0.0)
        lower = jnp.where(col <= row, c0, c1)
        upper = jnp.where(col <= row, c1, c2)
        for n, part in enumerate((lower, upper)):
            turned = jnp.dot(part, flip, precision=lax.Precision.HIGHEST)
            turned = pltpu.roll(turned, 0, 1, stride=1, stride_axis=0)
            turn_ref[n * half : (n + 1) * half, :] = turned.T
        turned = turn_ref[pl.ds(pl.multiple_of(position, 8), piece_count), :]
        place = b * half + across - diagonal
        cleared = (place & (half - 1) == sweeps) & (diagonal > half) & (place < (steps - 1) * half)
        cleared = cleared | ((place < sweeps) & (diagonal >= 2))
        span = slice(m * half, (m + 1) * half)
        band_out[:, span] = jnp.where(cleared, 0.0, band_ref[:, span] + turned)


def body(band_diagonals, eigenvectors):
    piece_count, rows_dev = band_diagonals.shape
    cols = lax.axis_size("cols")
    double = piece_count * cols
    half = double // 2
    blocks_dev = rows_dev // half
    devices = lax.axis_size("band")
    blocks = blocks_dev * devices
    sweeps = SWEEPS
    halo = sweeps
    columns = eigenvectors.shape[1]
    f32 = jnp.float32
    vmem = pl.BlockSpec(memory_space=pltpu.VMEM)

    takes = []
    while sum(takes) < halo * half:
        takes.append(min(halo * half - sum(takes), rows_dev))
    pieces = half // piece_count + 1
    dma = pltpu.SemaphoreType.DMA
    slots = blocks + 4
    pair_count = sweeps * (sweeps - 1) // 2 + 1
    scratch = (
        [
            pltpu.VMEM((blocks, half + 8, half), f32),
            pltpu.VMEM((piece_count, rows_dev), f32),
            pltpu.VMEM((blocks_dev, piece_count, half), f32),
            dma,
            [
                dma((blocks_dev, cols)),
                dma((pieces, blocks_dev)),
                dma((blocks_dev,)),
                dma((devices // 2, blocks_dev)),
                dma((devices // 2, blocks_dev)),
                dma((devices // 2, blocks_dev)),
                dma((devices // 2, blocks_dev)),
                dma((len(takes) + 1,)),
                dma((len(takes) + 1,)),
            ],
        ]
        + [pltpu.VMEM((slots, half, half), f32)] * 3
        + [
            pltpu.VMEM((half, half), f32),
            pltpu.VMEM((sweeps, 8, half), f32),
        ]
        + [pltpu.VMEM((blocks + 1, 8, half), f32)] * (2 * sweeps)
        + [pltpu.VMEM((slots, 8, half), f32)] * pair_count
    )
    anywhere = pl.BlockSpec(memory_space=pl.ANY)
    lines = -(-(halo + blocks_dev) // 8) * 8
    fields, v, tau, above, under = pl.pallas_call(
        functools.partial(kernel, half, devices, cols, takes, blocks, halo, sweeps),
        out_shape=(
            jax.ShapeDtypeStruct((sweeps, blocks_dev + 2, 8, half), f32),
            jax.ShapeDtypeStruct((sweeps, lines, half), f32),
            jax.ShapeDtypeStruct((sweeps, lines, half), f32),
            jax.ShapeDtypeStruct((halo * half, columns), f32),
            jax.ShapeDtypeStruct((8, columns), f32),
        ),
        in_specs=[anywhere] * 2,
        out_specs=(vmem,) * 3 + (anywhere,) * 2,
        scratch_shapes=scratch,
        compiler_params=pltpu.CompilerParams(
            collective_id=0, has_side_effects=True, vmem_limit_bytes=62 * 1024 * 1024
        ),
    )(band_diagonals, eigenvectors)
    return pl.pallas_call(
        functools.partial(finish_kernel, half, blocks, halo, sweeps),
        out_shape=(
            jax.ShapeDtypeStruct((piece_count, rows_dev), f32),
            jax.ShapeDtypeStruct((rows_dev, columns), f32),
        ),
        in_specs=[vmem] * 7,
        out_specs=(vmem, vmem),
        scratch_shapes=[pltpu.VMEM((double, half), f32)],
    )(band_diagonals, eigenvectors, fields, v, tau, above, under)


def solution(mesh):
    return jax.shard_map(
        body,
        mesh=mesh,
        in_specs=(P("cols", "band"), P("band", "cols")),
        out_specs=(P("cols", "band"), P("band", "cols")),
        check_vma=False,
    )
```

```python
import functools

import jax
import jax.numpy as jnp
from jax import lax
from jax.experimental import pallas as pl
from jax.experimental.pallas import tpu as pltpu
from jax.sharding import PartitionSpec as P

SWEEPS = 4
LAG = 3
AHEAD = 4
EARLY = 3
GROUP = 3


def kernel(half, devices, cols, takes, blocks, halo, sweeps, band_ref, eig_ref, *refs):
    field_out, v_out, tau_out, above_ref, under_ref = refs[:5]
    all_ref, band_in, rev_ref, in_sem, sems = refs[5:10]
    refs = refs[10:]
    d_ref, l_ref, t_ref, eye_ref, raw_ref = refs[:5]
    v_refs = refs[5 : 5 + sweeps]
    tau_refs = refs[5 + sweeps : 5 + 2 * sweeps]
    last = sweeps - 1
    pairs = [(a, b) for b in range(1, sweeps) for a in range(b)] + [(last, last)]
    fields = dict(zip(pairs, refs[5 + 2 * sweeps :]))
    blocks_dev = band_ref.shape[1] // half
    steps = blocks - 2
    row = lax.broadcasted_iota(jnp.int32, (half, half), 0)
    col = lax.broadcasted_iota(jnp.int32, (half, half), 1)
    eye = row == col
    row8 = lax.broadcasted_iota(jnp.int32, (8, half), 0)
    col8 = lax.broadcasted_iota(jnp.int32, (8, half), 1)
    zero = jnp.zeros((half, half), jnp.float32)
    count = half // 8

    z_send, z_recv, own_sem, x_send, x_recv, p_send, p_recv, e_send, e_recv = sems
    d, c = lax.axis_index("band"), lax.axis_index("cols")
    deep, rows_dev = band_ref.shape
    full = half // deep
    pieces = full + 1
    parts = rows_dev // half
    chips = devices // 2
    chip, core = d // 2, d % 2
    partner = chip * 2 + 1 - core

    inward = pltpu.make_async_copy(band_ref, band_in, in_sem)
    inward.start()
    barrier = pltpu.get_barrier_semaphore()
    peers = [(d, (c + hop) % cols) for hop in range(1, cols)]
    peers += [((chip + hop) % chips * 2 + core, c) for hop in range(1, chips)]
    peers.append((partner, c))
    for hop in range(1, len(takes) + 1):
        peers += [((d + hop) % devices, c), ((d - hop + devices) % devices, c)]
    for peer in peers:
        pl.semaphore_signal(barrier, inc=1, device_id=peer, device_id_type=pl.DeviceIdType.MESH)

    for spot in (0, 1, blocks + 2):
        d_ref[spot] = zero
    for spot in (0, blocks + 1):
        l_ref[spot] = zero
        t_ref[spot] = zero
    for ref in v_refs + tau_refs + tuple(fields.values()) + (raw_ref,):
        ref[...] = jnp.zeros(ref.shape, jnp.float32)
    eye_ref[...] = jnp.where(eye, 1.0, 0.0)

    inward.wait()
    for r in range(deep):
        for m in range(parts):
            rev_ref[m, r : r + 1, :] = band_in[deep - 1 - r : deep - r, m * half : (m + 1) * half]

    pl.semaphore_wait(barrier, len(peers))

    def send(src, dst, send_sem, recv_sem, device):
        return pltpu.make_async_remote_copy(
            src_ref=src,
            dst_ref=dst,
            send_sem=send_sem,
            recv_sem=recv_sem,
            device_id=device,
            device_id_type=pl.DeviceIdType.MESH,
        )

    def rows_of(p):
        return pl.ds(half - (p + 1) * deep, deep) if p < full else pl.ds(half, 8)

    def source(p, m):
        return rev_ref.at[m] if p < full else band_in.at[pl.ds(0, 8), pl.ds(m * half, half)]

    def place(p, m):
        return all_ref.at[d * parts + m, rows_of(p)]

    def along(p, m, to):
        return send(source(p, m), place(p, m), z_send.at[m, to], z_recv.at[p, m], (d, to))

    def own(p, m):
        return pltpu.make_async_copy(source(p, m), place(p, m), own_sem.at[m])

    def chunk(owner, m):
        return all_ref.at[owner * parts + m]

    def across(to, m):
        src = chunk(d, m)
        return send(src, src, x_send.at[to, m], x_recv.at[chip, m], (to * 2 + core, c))

    def arrived(owner, m):
        src = chunk(owner * 2 + core, m)
        return send(src, src, x_send.at[owner, m], x_recv.at[owner, m], (owner * 2 + core, c))

    def share(owner, m):
        src = chunk(owner * 2 + core, m)
        return send(src, src, p_send.at[owner, m], p_recv.at[owner, m], (partner, c))

    halos = []
    end = sum(takes)
    for hop, take in enumerate(takes, 1):
        halos.append(
            send(
                eig_ref.at[pl.ds(rows_dev - take, take)],
                above_ref.at[pl.ds(end - take, take)],
                e_send.at[hop],
                e_recv.at[hop],
                ((d + hop) % devices, c),
            )
        )
        end -= take
    halos.append(
        send(eig_ref.at[pl.ds(0, 8)], under_ref, e_send.at[0], e_recv.at[0], ((d - 1 + devices) % devices, c))
    )

    for p in range(pieces):

        @pl.when(c == p)
        def _():
            for m in range(parts):
                for to in reversed(range(cols)):
                    if to != p:
                        along(p, m, to).start()
                own(p, m).start()

    for copy in halos:
        copy.start()

    for m in range(parts):
        for p in range(pieces):

            @pl.when(c == p)
            def _():
                own(p, m).wait()

            @pl.when(c != p)
            def _():
                along(p, m, c).wait_recv()

        for to in reversed(range(chips)):

            @pl.when(chip != to)
            def _():
                across(to, m).start()

        share(chip, m).start()

    def sides(block):
        owner, m = block // parts, block % parts
        return owner // 2, owner % 2, m

    def duty(block):
        owner, side, m = sides(block)

        if block >= blocks:
            return

        @pl.when((core == side) & (chip != owner))
        def _():
            arrived(owner, m).wait_recv()
            share(owner, m).start()

    def need(block):
        owner, side, m = sides(block)

        if block >= blocks:
            return

        @pl.when(core != side)
        def _():
            share(owner, m).wait_recv()

    def unpack(block):
        piece = all_ref[block, :half]
        extra = all_ref[block, half : half + 1]
        rows = pltpu.roll(piece.T, 1, 1, stride=1, stride_axis=0)
        turned = rows.T
        extra = jnp.where(eye, jnp.broadcast_to(extra, (half, half)), 0.0)
        d_ref[block + 2] = jnp.where(row >= col, rows, turned)
        l_ref[block + 1] = jnp.where(col > row, rows, extra)
        t_ref[block + 1] = jnp.where(row > col, turned, extra)

    def tile(ref, k, i=0):
        return ref[k + 2, 8 * i : 8 * i + 8, :]

    def lanes(x):
        return jnp.broadcast_to(jnp.sum(x, axis=1, keepdims=True), (8, half))

    def rows_sum(x):
        return jnp.broadcast_to(jnp.sum(x, axis=0, keepdims=True), (8, half))

    def at_lane(x, spot):
        return jnp.broadcast_to(x[:, spot : spot + 1], (8, half))

    def total(parts):
        while len(parts) > 1:
            rest = parts[len(parts) // 2 * 2 :]
            parts = [a + b for a, b in zip(parts[::2], parts[1::2])] + rest
        return parts[0]

    def to_lane(x, fill, spot):
        return jnp.where(col8 == spot, fill, x)

    def norms(x, new):
        rest = lanes(to_lane(x * x, 0.0, new))
        top = at_lane(x, new)
        square = rest + top * top
        inverse = lax.rsqrt(square)
        return rest, top, square * inverse, inverse

    def wide(line):
        return jnp.broadcast_to(line, (8, half))

    def begin(s):
        x = jnp.where(col8 > s, wide(d_ref[2, s : s + 1, :]), wide(t_ref[2, s : s + 1, :]))
        for a in range(s):
            x = x - rows_sum(fields[a, s][2] * at_lane(raw_ref[a], s))
        return (x,) + (jnp.zeros((8, half), jnp.float32),) * 4

    def targets(s):
        return range(s + 1, sweeps) if s < last else (last,)

    def settle(s, k, inside, v, tau):
        inside = inside - 0.5 * tau * lanes(v * inside) * v
        for b in targets(s):
            ref = fields[s, b]
            other = (col8 > s) & (col8 <= b)
            ref[k + 2, 4:5, :] = jnp.where(other, wide(ref[k + 2, 4:5, :]), inside)[0:1]
            if b > s:
                ref[k + 1, 7:8, :] = jnp.where(other, inside, wide(ref[k + 1, 7:8, :]))[0:1]
        if s < last and k == 0:
            raw_ref[s, 0:1, :] = inside[0:1]

    def chain(s, k, x, hung, inside_past, v_past, tau_past):
        new = s + 1
        main = col8 > s
        x_col = [
            jnp.sum(x * eye_ref[8 * i : 8 * i + 8, :], axis=1, keepdims=True) for i in range(count)
        ]
        rest, top, length, inverse = norms(x, new)
        x_main = jnp.where(row8 > s, x_col[0], 0.0)
        x_tail = jnp.where(row8 > s, 0.0, x_col[0])

        def times(ref, spot, extra):
            parts = [tile(ref, spot, i) * x_col[i] for i in range(1, count)]
            return total(parts + [tile(ref, spot) * x_main] + extra)

        here = times(d_ref, k, [tile(l_ref, k) * x_tail])
        after = times(t_ref, k, [tile(d_ref, k + 1) * x_tail])
        beyond = tile(t_ref, k + 1) * x_tail
        before = times(l_ref, k - 1, [])
        here_top = wide(d_ref[k + 2, new : new + 1, :])
        after_top = wide(t_ref[k + 2, new : new + 1, :])
        before_top = wide(l_ref[k + 1, new : new + 1, :])
        inside = jnp.where(main, here, after)
        beneath = jnp.where(main, after, beyond)
        across = jnp.where(main, before, here)
        fixes = []
        for a in range(s):
            now = fields[a, s][k + 2]
            up = jnp.where(row8 == 1, 0.0, fields[a, s][k + 1])
            down = jnp.where(row8 == 2, 0.0, fields[a, s][k + 3])
            unit = at_lane(now, new)
            dots = lanes(now * x)
            beneath = beneath - down * pltpu.roll(dots, 1, 0)
            fixes.append(down * pltpu.roll(unit, 1, 0))
            dots = dots + length * unit
            inside = inside - now * pltpu.roll(dots, 4, 0)
            across = across - up * pltpu.roll(dots, 7, 0)
        beneath = rows_sum(beneath)
        x_next = beneath * -inverse
        column = jnp.where(main, after_top, 0.0)
        if fixes:
            column = column - rows_sum(total(fixes))
        hang = lanes(hung * x) + length * at_lane(hung, new)
        v_top = top + length
        tau = 2.0 / (rest + v_top * v_top)
        v = to_lane(x, v_top, new)
        beneath = tau * (beneath + length * column)
        inside = tau * (rows_sum(inside) + length * jnp.where(main, here_top, after_top))
        across = tau * (rows_sum(across) + length * jnp.where(main, before_top, here_top) - v_past * hang)

        settle(s, k - 1, inside_past, v_past, tau_past)
        v_refs[s][k + 1] = v
        tau_refs[s][k + 1] = tau
        for b in targets(s):
            ref = fields[s, b]
            other = (col8 > s) & (col8 <= b)
            ref[k + 2, 0:1, :] = jnp.where(other, 0.0, v)[0:1]
            ref[k + 1, 7:8, :] = across[0:1]
            ref[k + 3, 1:2, :] = jnp.where(other, 0.0, beneath)[0:1]
            if b > s:
                ref[k + 2, 4:5, :] = beneath[0:1]
                ref[k + 1, 3:4, :] = jnp.where(other, v, 0.0)[0:1]
                ref[k, 2:3, :] = jnp.where(other, across, 0.0)[0:1]
        if s < last and k == 1:
            raw_ref[s, 3:4, :] = across[0:1]
        if s < last and k == 0:
            raw_ref[s, 4:5, :] = v[0:1]
        return x_next, beneath, inside, v, tau

    def phase(start, stop, chains, states):
        def wave(t, states):
            done = {s: chain(s, t - LAG * s, *state) for s, state in reversed(list(zip(chains, states)))}
            if t + AHEAD < blocks:
                unpack(t + AHEAD)
            return tuple(done[s] for s in chains)

        for begun in range(start, stop, GROUP):
            waves = range(begun, min(begun + GROUP, stop))
            for t in waves:
                duty(t + AHEAD + EARLY)
            for t in waves:
                need(t + AHEAD)
            for t in waves:
                states = wave(t, states)
        return states

    def drain(s, state):
        settle(s, steps - 1, *state[2:])

    for block in range(AHEAD + EARLY):
        duty(block)
    for block in range(AHEAD):
        need(block)
        unpack(block)
    states = ()
    for s in range(last):
        states = phase(LAG * s, LAG * (s + 1), range(s + 1), states + (begin(s),))
    states = phase(LAG * last, steps, range(sweeps), states + (begin(last),))
    for s in range(1, sweeps):
        drain(s - 1, states[0])
        states = phase(steps + LAG * (s - 1), steps + LAG * s, range(s, sweeps), states[1:])
    drain(last, states[0])

    for m in range(parts):
        for p in range(pieces):

            @pl.when(c == p)
            def _():
                for to in range(cols):
                    if to != p:
                        along(p, m, to).wait_send()

        for owner in range(chips):

            @pl.when(chip != owner)
            def _():
                across(owner, m).wait_send()

            share(owner, m).wait_send()
    for copy in halos:
        copy.wait()

    first = d * parts
    for s in range(sweeps):
        for e in range(halo + parts):
            spot = jnp.clip(first - halo + e, -1, blocks - 1) + 1
            v_out[s, e : e + 1, :] = v_refs[s][spot, 0:1, :]
            tau_out[s, e : e + 1, :] = tau_refs[s][spot, 0:1, :]
        for n in range(parts + 2):
            field_out[s, n] = fields[s, last][first + n]


def finish_kernel(half, blocks, halo, sweeps, *refs):
    band_ref, eig_ref, field_ref, v_ref, tau_ref, above_ref, under_ref, band_out, eig_out, turn_ref = refs
    piece_count, blocks_dev = band_ref.shape[0], band_ref.shape[1] // half
    steps = blocks - 2
    row = lax.broadcasted_iota(jnp.int32, (half, half), 0)
    col = lax.broadcasted_iota(jnp.int32, (half, half), 1)
    eye = row == col
    row8 = lax.broadcasted_iota(jnp.int32, (8, half), 0)
    device = lax.axis_index("band")
    first = device * blocks_dev
    eig = [above_ref[e * half : (e + 1) * half, :] for e in range(halo)]
    eig += [eig_ref[e * half : (e + 1) * half, :] for e in range(blocks_dev)]
    eig.append(under_ref[...])
    for s in reversed(range(sweeps)):
        lead_rows = s + 1
        for e in range(sweeps - 1 - s + halo - sweeps, halo + blocks_dev):
            v = jnp.sum(jnp.where(eye, v_ref[s, e : e + 1, :], 0.0), axis=1, keepdims=True)
            tau = tau_ref[s, e : e + 1, :]
            low, high = eig[e], eig[e + 1]
            mixed = jnp.concatenate([jnp.where(row8 < lead_rows, high[:8], low[:8]), low[8:]], 0)
            inner = tau * jnp.sum(v * mixed, axis=0, keepdims=True)
            mixed = mixed - v * inner
            eig[e] = jnp.concatenate([jnp.where(row8 < lead_rows, low[:8], mixed[:8]), mixed[8:]], 0)
            top = jnp.where(row8 < lead_rows, mixed[:8], high[:8])
            eig[e + 1] = jnp.concatenate([top, high[8:]], 0) if high.shape[0] > 8 else top
    for m in range(blocks_dev):
        eig_out[m * half : (m + 1) * half, :] = eig[halo + m]

    def product(a, b):
        return lax.dot_general(
            a, b, (((0,), (0,)), ((), ())),
            precision=lax.Precision.HIGHEST, preferred_element_type=jnp.float32,
        )

    def stack(n, shift=0, drop=None):
        parts = []
        for a in range(sweeps):
            part = field_ref[a, n]
            part = part if drop is None else jnp.where(row8 == drop, 0.0, part)
            parts.append(pltpu.roll(part, shift, 0) if shift else part)
        return jnp.concatenate(parts, 0)

    bottom, lead = [], []
    for a in range(sweeps - 1):
        bottom.append(jnp.where(row8 == 1, field_ref[a, blocks_dev], 0.0))
        lead.append(pltpu.roll(jnp.where(row8 == 3, field_ref[a, blocks_dev - 2], 0.0), 6, 0))
    rest = -product(jnp.concatenate(bottom, 0), jnp.concatenate(lead, 0))
    flip = jnp.where((row + col == half) | ((row == 0) & (col == 0)), 1.0, 0.0)
    position = lax.axis_index("cols") * piece_count
    d_last = [-product(stack(m + 1), stack(m + 1, 4)) for m in range(blocks_dev + 1)]
    l_last = [-product(stack(m + 1, 0, 2), stack(m, 1)) for m in range(blocks_dev + 1)]
    diagonal = position + lax.broadcasted_iota(jnp.int32, (piece_count, half), 0)
    across = lax.broadcasted_iota(jnp.int32, (piece_count, half), 1)
    for m in range(blocks_dev):
        b = first + m
        lim = jnp.where(b > 0, half, 0)
        rest_below = jnp.where(b == steps, half, 0)
        rest_last = jnp.where(b == steps + 1, half, 0)
        d_here, d_before = d_last[m + 1], d_last[m]
        l_here, l_before = l_last[m + 1], l_last[m]
        c0 = jnp.where(
            row >= sweeps, jnp.where(col >= sweeps, d_here, l_here), jnp.where(col < sweeps, d_before, 0.0)
        )
        c1 = jnp.where(
            row >= sweeps,
            jnp.where(col >= sweeps, l_here, jnp.where(row < rest_below, rest, 0.0)),
            jnp.where(col >= sweeps, d_before, l_before),
        )
        c1 = jnp.where(row < lim, c1, 0.0)
        c2 = jnp.where(col >= sweeps, l_before, jnp.where(row < rest_last, rest, 0.0))
        c2 = jnp.where(row < sweeps, c2, 0.0)
        c2 = jnp.where(row < lim, c2, 0.0)
        lower = jnp.where(col <= row, c0, c1)
        upper = jnp.where(col <= row, c1, c2)
        for n, part in enumerate((lower, upper)):
            turned = jnp.dot(part, flip, precision=lax.Precision.HIGHEST)
            turned = pltpu.roll(turned, 0, 1, stride=1, stride_axis=0)
            turn_ref[n * half : (n + 1) * half, :] = turned.T
        turned = turn_ref[pl.ds(pl.multiple_of(position, 8), piece_count), :]
        place = b * half + across - diagonal
        cleared = (place & (half - 1) == sweeps) & (diagonal > half) & (place < (steps - 1) * half)
        cleared = cleared | ((place < sweeps) & (diagonal >= 2))
        span = slice(m * half, (m + 1) * half)
        band_out[:, span] = jnp.where(cleared, 0.0, band_ref[:, span] + turned)


def body(band_diagonals, eigenvectors):
    piece_count, rows_dev = band_diagonals.shape
    cols = lax.axis_size("cols")
    double = piece_count * cols
    half = double // 2
    blocks_dev = rows_dev // half
    devices = lax.axis_size("band")
    blocks = blocks_dev * devices
    sweeps = SWEEPS
    halo = sweeps
    columns = eigenvectors.shape[1]
    f32 = jnp.float32
    vmem = pl.BlockSpec(memory_space=pltpu.VMEM)

    takes = []
    while sum(takes) < halo * half:
        takes.append(min(halo * half - sum(takes), rows_dev))
    pieces = half // piece_count + 1
    dma = pltpu.SemaphoreType.DMA
    slots = blocks + 4
    pair_count = sweeps * (sweeps - 1) // 2 + 1
    scratch = (
        [
            pltpu.VMEM((blocks, half + 8, half), f32),
            pltpu.VMEM((piece_count, rows_dev), f32),
            pltpu.VMEM((blocks_dev, piece_count, half), f32),
            dma,
            [
                dma((blocks_dev, cols)),
                dma((pieces, blocks_dev)),
                dma((blocks_dev,)),
                dma((devices // 2, blocks_dev)),
                dma((devices // 2, blocks_dev)),
                dma((devices // 2, blocks_dev)),
                dma((devices // 2, blocks_dev)),
                dma((len(takes) + 1,)),
                dma((len(takes) + 1,)),
            ],
        ]
        + [pltpu.VMEM((slots, half, half), f32)] * 3
        + [
            pltpu.VMEM((half, half), f32),
            pltpu.VMEM((sweeps, 8, half), f32),
        ]
        + [pltpu.VMEM((blocks + 1, 8, half), f32)] * (2 * sweeps)
        + [pltpu.VMEM((slots, 8, half), f32)] * pair_count
    )
    anywhere = pl.BlockSpec(memory_space=pl.ANY)
    lines = -(-(halo + blocks_dev) // 8) * 8
    fields, v, tau, above, under = pl.pallas_call(
        functools.partial(kernel, half, devices, cols, takes, blocks, halo, sweeps),
        out_shape=(
            jax.ShapeDtypeStruct((sweeps, blocks_dev + 2, 8, half), f32),
            jax.ShapeDtypeStruct((sweeps, lines, half), f32),
            jax.ShapeDtypeStruct((sweeps, lines, half), f32),
            jax.ShapeDtypeStruct((halo * half, columns), f32),
            jax.ShapeDtypeStruct((8, columns), f32),
        ),
        in_specs=[anywhere] * 2,
        out_specs=(vmem,) * 3 + (anywhere,) * 2,
        scratch_shapes=scratch,
        compiler_params=pltpu.CompilerParams(
            collective_id=0, has_side_effects=True, vmem_limit_bytes=62 * 1024 * 1024
        ),
    )(band_diagonals, eigenvectors)
    return pl.pallas_call(
        functools.partial(finish_kernel, half, blocks, halo, sweeps),
        out_shape=(
            jax.ShapeDtypeStruct((piece_count, rows_dev), f32),
            jax.ShapeDtypeStruct((rows_dev, columns), f32),
        ),
        in_specs=[vmem] * 7,
        out_specs=(vmem, vmem),
        scratch_shapes=[pltpu.VMEM((double, half), f32)],
    )(band_diagonals, eigenvectors, fields, v, tau, above, under)


def solution(mesh):
    return jax.shard_map(
        body,
        mesh=mesh,
        in_specs=(P("cols", "band"), P("band", "cols")),
        out_specs=(P("cols", "band"), P("band", "cols")),
        check_vma=False,
    )
```

```python
import functools

import jax
import jax.numpy as jnp
from jax import lax
from jax.experimental import pallas as pl
from jax.experimental.pallas import tpu as pltpu
from jax.sharding import PartitionSpec as P

SWEEPS = 4
LAG = 3
AHEAD = 4
EARLY = 3
GROUP = 3


def kernel(half, devices, cols, takes, blocks, halo, sweeps, band_ref, eig_ref, *refs):
    field_out, v_out, tau_out, above_ref, under_ref = refs[:5]
    all_ref, band_in, rev_ref, in_sem, sems = refs[5:10]
    refs = refs[10:]
    d_ref, l_ref, t_ref, eye_ref, raw_ref = refs[:5]
    v_refs = refs[5 : 5 + sweeps]
    tau_refs = refs[5 + sweeps : 5 + 2 * sweeps]
    last = sweeps - 1
    pairs = [(a, b) for b in range(1, sweeps) for a in range(b)] + [(last, last)]
    fields = dict(zip(pairs, refs[5 + 2 * sweeps :]))
    blocks_dev = band_ref.shape[1] // half
    steps = blocks - 2
    row = lax.broadcasted_iota(jnp.int32, (half, half), 0)
    col = lax.broadcasted_iota(jnp.int32, (half, half), 1)
    eye = row == col
    row8 = lax.broadcasted_iota(jnp.int32, (8, half), 0)
    col8 = lax.broadcasted_iota(jnp.int32, (8, half), 1)
    zero = jnp.zeros((half, half), jnp.float32)
    count = half // 8

    z_send, z_recv, own_sem, x_send, x_recv, p_send, p_recv, e_send, e_recv = sems
    d, c = lax.axis_index("band"), lax.axis_index("cols")
    deep, rows_dev = band_ref.shape
    full = half // deep
    pieces = full + 1
    parts = rows_dev // half
    chips = devices // 2
    chip, core = d // 2, d % 2
    partner = chip * 2 + 1 - core

    inward = pltpu.make_async_copy(band_ref, band_in, in_sem)
    inward.start()
    barrier = pltpu.get_barrier_semaphore()
    peers = [(d, (c + hop) % cols) for hop in range(1, cols)]
    peers += [((chip + hop) % chips * 2 + core, c) for hop in range(1, chips)]
    peers.append((partner, c))
    for hop in range(1, len(takes) + 1):
        peers += [((d + hop) % devices, c), ((d - hop + devices) % devices, c)]
    for peer in peers:
        pl.semaphore_signal(barrier, inc=1, device_id=peer, device_id_type=pl.DeviceIdType.MESH)

    for spot in (0, 1, blocks + 2):
        d_ref[spot] = zero
    for spot in (0, blocks + 1):
        l_ref[spot] = zero
        t_ref[spot] = zero
    for ref in v_refs + tau_refs + tuple(fields.values()) + (raw_ref,):
        ref[...] = jnp.zeros(ref.shape, jnp.float32)
    eye_ref[...] = jnp.where(eye, 1.0, 0.0)

    inward.wait()
    for r in range(deep):
        for m in range(parts):
            rev_ref[m, r : r + 1, :] = band_in[deep - 1 - r : deep - r, m * half : (m + 1) * half]

    pl.semaphore_wait(barrier, len(peers))

    def send(src, dst, send_sem, recv_sem, device):
        return pltpu.make_async_remote_copy(
            src_ref=src,
            dst_ref=dst,
            send_sem=send_sem,
            recv_sem=recv_sem,
            device_id=device,
            device_id_type=pl.DeviceIdType.MESH,
        )

    def rows_of(p):
        return pl.ds(half - (p + 1) * deep, deep) if p < full else pl.ds(half, 8)

    def source(p, m):
        return rev_ref.at[m] if p < full else band_in.at[pl.ds(0, 8), pl.ds(m * half, half)]

    def place(p, m):
        return all_ref.at[d * parts + m, rows_of(p)]

    def along(p, m, to):
        return send(source(p, m), place(p, m), z_send.at[m, to], z_recv.at[p, m], (d, to))

    def own(p, m):
        return pltpu.make_async_copy(source(p, m), place(p, m), own_sem.at[m])

    def chunk(owner, m):
        return all_ref.at[owner * parts + m]

    def across(to, m, p, src=None):
        dst = place(p, m)
        src = dst if src is None else src
        return send(src, dst, x_send.at[to, m, p], x_recv.at[chip, m, p], (to * 2 + core, c))

    def arrived(owner, m, p):
        dst = all_ref.at[(owner * 2 + core) * parts + m, rows_of(p)]
        return send(dst, dst, x_send.at[owner, m, p], x_recv.at[owner, m, p], (owner * 2 + core, c))

    def spread(m, p, src=None):
        for to in reversed(range(chips)):

            @pl.when(chip != to)
            def _():
                across(to, m, p, src).start()

    def share(owner, m):
        src = chunk(owner * 2 + core, m)
        return send(src, src, p_send.at[owner, m], p_recv.at[owner, m], (partner, c))

    halos = []
    end = sum(takes)
    for hop, take in enumerate(takes, 1):
        halos.append(
            send(
                eig_ref.at[pl.ds(rows_dev - take, take)],
                above_ref.at[pl.ds(end - take, take)],
                e_send.at[hop],
                e_recv.at[hop],
                ((d + hop) % devices, c),
            )
        )
        end -= take
    halos.append(
        send(eig_ref.at[pl.ds(0, 8)], under_ref, e_send.at[0], e_recv.at[0], ((d - 1 + devices) % devices, c))
    )

    for p in range(pieces):

        @pl.when(c == p)
        def _():
            for m in range(parts):
                for to in reversed(range(cols)):
                    if to != p:
                        along(p, m, to).start()
                own(p, m).start()
                spread(m, p, source(p, m))

    for copy in halos:
        copy.start()

    for m in range(parts):
        for p in reversed(range(pieces)):

            @pl.when(c == p)
            def _():
                own(p, m).wait()

            @pl.when(c != p)
            def _():
                along(p, m, c).wait_recv()
                spread(m, p)

        share(chip, m).start()

    def sides(block):
        owner, m = block // parts, block % parts
        return owner // 2, owner % 2, m

    def duty(block):
        owner, side, m = sides(block)

        if block >= blocks:
            return

        @pl.when((core == side) & (chip != owner))
        def _():
            for p in range(pieces):
                arrived(owner, m, p).wait_recv()
            share(owner, m).start()

    def need(block):
        owner, side, m = sides(block)

        if block >= blocks:
            return

        @pl.when(core != side)
        def _():
            share(owner, m).wait_recv()

    def unpack(block):
        piece = all_ref[block, :half]
        extra = all_ref[block, half : half + 1]
        rows = pltpu.roll(piece.T, 1, 1, stride=1, stride_axis=0)
        turned = rows.T
        extra = jnp.where(eye, jnp.broadcast_to(extra, (half, half)), 0.0)
        d_ref[block + 2] = jnp.where(row >= col, rows, turned)
        l_ref[block + 1] = jnp.where(col > row, rows, extra)
        t_ref[block + 1] = jnp.where(row > col, turned, extra)

    def tile(ref, k, i=0):
        return ref[k + 2, 8 * i : 8 * i + 8, :]

    def lanes(x):
        return jnp.broadcast_to(jnp.sum(x, axis=1, keepdims=True), (8, half))

    def rows_sum(x):
        return jnp.broadcast_to(jnp.sum(x, axis=0, keepdims=True), (8, half))

    def at_lane(x, spot):
        return jnp.broadcast_to(x[:, spot : spot + 1], (8, half))

    def total(parts):
        while len(parts) > 1:
            rest = parts[len(parts) // 2 * 2 :]
            parts = [a + b for a, b in zip(parts[::2], parts[1::2])] + rest
        return parts[0]

    def to_lane(x, fill, spot):
        return jnp.where(col8 == spot, fill, x)

    def norms(x, new):
        rest = lanes(to_lane(x * x, 0.0, new))
        top = at_lane(x, new)
        square = rest + top * top
        inverse = lax.rsqrt(square)
        return rest, top, square * inverse, inverse

    def wide(line):
        return jnp.broadcast_to(line, (8, half))

    def begin(s):
        x = jnp.where(col8 > s, wide(d_ref[2, s : s + 1, :]), wide(t_ref[2, s : s + 1, :]))
        for a in range(s):
            x = x - rows_sum(fields[a, s][2] * at_lane(raw_ref[a], s))
        return (x,) + (jnp.zeros((8, half), jnp.float32),) * 4

    def targets(s):
        return range(s + 1, sweeps) if s < last else (last,)

    def settle(s, k, inside, v, tau):
        inside = inside - 0.5 * tau * lanes(v * inside) * v
        for b in targets(s):
            ref = fields[s, b]
            other = (col8 > s) & (col8 <= b)
            ref[k + 2, 4:5, :] = jnp.where(other, wide(ref[k + 2, 4:5, :]), inside)[0:1]
            if b > s:
                ref[k + 1, 7:8, :] = jnp.where(other, inside, wide(ref[k + 1, 7:8, :]))[0:1]
        if s < last and k == 0:
            raw_ref[s, 0:1, :] = inside[0:1]

    def chain(s, k, x, hung, inside_past, v_past, tau_past):
        new = s + 1
        main = col8 > s
        x_col = [
            jnp.sum(x * eye_ref[8 * i : 8 * i + 8, :], axis=1, keepdims=True) for i in range(count)
        ]
        rest, top, length, inverse = norms(x, new)
        x_main = jnp.where(row8 > s, x_col[0], 0.0)
        x_tail = jnp.where(row8 > s, 0.0, x_col[0])

        def times(ref, spot, extra):
            parts = [tile(ref, spot, i) * x_col[i] for i in range(1, count)]
            return total(parts + [tile(ref, spot) * x_main] + extra)

        here = times(d_ref, k, [tile(l_ref, k) * x_tail])
        after = times(t_ref, k, [tile(d_ref, k + 1) * x_tail])
        beyond = tile(t_ref, k + 1) * x_tail
        before = times(l_ref, k - 1, [])
        here_top = wide(d_ref[k + 2, new : new + 1, :])
        after_top = wide(t_ref[k + 2, new : new + 1, :])
        before_top = wide(l_ref[k + 1, new : new + 1, :])
        inside = jnp.where(main, here, after)
        beneath = jnp.where(main, after, beyond)
        across = jnp.where(main, before, here)
        fixes = []
        for a in range(s):
            now = fields[a, s][k + 2]
            up = jnp.where(row8 == 1, 0.0, fields[a, s][k + 1])
            down = jnp.where(row8 == 2, 0.0, fields[a, s][k + 3])
            unit = at_lane(now, new)
            dots = lanes(now * x)
            beneath = beneath - down * pltpu.roll(dots, 1, 0)
            fixes.append(down * pltpu.roll(unit, 1, 0))
            dots = dots + length * unit
            inside = inside - now * pltpu.roll(dots, 4, 0)
            across = across - up * pltpu.roll(dots, 7, 0)
        beneath = rows_sum(beneath)
        x_next = beneath * -inverse
        column = jnp.where(main, after_top, 0.0)
        if fixes:
            column = column - rows_sum(total(fixes))
        hang = lanes(hung * x) + length * at_lane(hung, new)
        v_top = top + length
        tau = 2.0 / (rest + v_top * v_top)
        v = to_lane(x, v_top, new)
        beneath = tau * (beneath + length * column)
        inside = tau * (rows_sum(inside) + length * jnp.where(main, here_top, after_top))
        across = tau * (rows_sum(across) + length * jnp.where(main, before_top, here_top) - v_past * hang)

        settle(s, k - 1, inside_past, v_past, tau_past)
        v_refs[s][k + 1] = v
        tau_refs[s][k + 1] = tau
        for b in targets(s):
            ref = fields[s, b]
            other = (col8 > s) & (col8 <= b)
            ref[k + 2, 0:1, :] = jnp.where(other, 0.0, v)[0:1]
            ref[k + 1, 7:8, :] = across[0:1]
            ref[k + 3, 1:2, :] = jnp.where(other, 0.0, beneath)[0:1]
            if b > s:
                ref[k + 2, 4:5, :] = beneath[0:1]
                ref[k + 1, 3:4, :] = jnp.where(other, v, 0.0)[0:1]
                ref[k, 2:3, :] = jnp.where(other, across, 0.0)[0:1]
        if s < last and k == 1:
            raw_ref[s, 3:4, :] = across[0:1]
        if s < last and k == 0:
            raw_ref[s, 4:5, :] = v[0:1]
        return x_next, beneath, inside, v, tau

    def phase(start, stop, chains, states):
        def wave(t, states):
            done = {s: chain(s, t - LAG * s, *state) for s, state in reversed(list(zip(chains, states)))}
            if t + AHEAD < blocks:
                unpack(t + AHEAD)
            return tuple(done[s] for s in chains)

        for begun in range(start, stop, GROUP):
            waves = range(begun, min(begun + GROUP, stop))
            for t in waves:
                duty(t + AHEAD + EARLY)
            for t in waves:
                need(t + AHEAD)
            for t in waves:
                states = wave(t, states)
        return states

    def drain(s, state):
        settle(s, steps - 1, *state[2:])

    for block in range(AHEAD + EARLY):
        duty(block)
    for block in range(AHEAD):
        need(block)
        unpack(block)
    states = ()
    for s in range(last):
        states = phase(LAG * s, LAG * (s + 1), range(s + 1), states + (begin(s),))
    states = phase(LAG * last, steps, range(sweeps), states + (begin(last),))
    for s in range(1, sweeps):
        drain(s - 1, states[0])
        states = phase(steps + LAG * (s - 1), steps + LAG * s, range(s, sweeps), states[1:])
    drain(last, states[0])

    for m in range(parts):
        for p in range(pieces):

            @pl.when(c == p)
            def _():
                for to in range(cols):
                    if to != p:
                        along(p, m, to).wait_send()

        for owner in range(chips):

            @pl.when(chip != owner)
            def _():
                for p in range(pieces):
                    across(owner, m, p).wait_send()

            share(owner, m).wait_send()
    for copy in halos:
        copy.wait()

    first = d * parts
    for s in range(sweeps):
        for e in range(halo + parts):
            spot = jnp.clip(first - halo + e, -1, blocks - 1) + 1
            v_out[s, e : e + 1, :] = v_refs[s][spot, 0:1, :]
            tau_out[s, e : e + 1, :] = tau_refs[s][spot, 0:1, :]
        for n in range(parts + 2):
            field_out[s, n] = fields[s, last][first + n]


def finish_kernel(half, blocks, halo, sweeps, *refs):
    band_ref, eig_ref, field_ref, v_ref, tau_ref, above_ref, under_ref, band_out, eig_out, turn_ref = refs
    piece_count, blocks_dev = band_ref.shape[0], band_ref.shape[1] // half
    steps = blocks - 2
    row = lax.broadcasted_iota(jnp.int32, (half, half), 0)
    col = lax.broadcasted_iota(jnp.int32, (half, half), 1)
    eye = row == col
    row8 = lax.broadcasted_iota(jnp.int32, (8, half), 0)
    device = lax.axis_index("band")
    first = device * blocks_dev
    eig = [above_ref[e * half : (e + 1) * half, :] for e in range(halo)]
    eig += [eig_ref[e * half : (e + 1) * half, :] for e in range(blocks_dev)]
    eig.append(under_ref[...])
    for s in reversed(range(sweeps)):
        lead_rows = s + 1
        for e in range(sweeps - 1 - s + halo - sweeps, halo + blocks_dev):
            v = jnp.sum(jnp.where(eye, v_ref[s, e : e + 1, :], 0.0), axis=1, keepdims=True)
            tau = tau_ref[s, e : e + 1, :]
            low, high = eig[e], eig[e + 1]
            mixed = jnp.concatenate([jnp.where(row8 < lead_rows, high[:8], low[:8]), low[8:]], 0)
            inner = tau * jnp.sum(v * mixed, axis=0, keepdims=True)
            mixed = mixed - v * inner
            eig[e] = jnp.concatenate([jnp.where(row8 < lead_rows, low[:8], mixed[:8]), mixed[8:]], 0)
            top = jnp.where(row8 < lead_rows, mixed[:8], high[:8])
            eig[e + 1] = jnp.concatenate([top, high[8:]], 0) if high.shape[0] > 8 else top
    for m in range(blocks_dev):
        eig_out[m * half : (m + 1) * half, :] = eig[halo + m]

    def product(a, b):
        return lax.dot_general(
            a, b, (((0,), (0,)), ((), ())),
            precision=lax.Precision.HIGHEST, preferred_element_type=jnp.float32,
        )

    def stack(n, shift=0, drop=None):
        parts = []
        for a in range(sweeps):
            part = field_ref[a, n]
            part = part if drop is None else jnp.where(row8 == drop, 0.0, part)
            parts.append(pltpu.roll(part, shift, 0) if shift else part)
        return jnp.concatenate(parts, 0)

    bottom, lead = [], []
    for a in range(sweeps - 1):
        bottom.append(jnp.where(row8 == 1, field_ref[a, blocks_dev], 0.0))
        lead.append(pltpu.roll(jnp.where(row8 == 3, field_ref[a, blocks_dev - 2], 0.0), 6, 0))
    rest = -product(jnp.concatenate(bottom, 0), jnp.concatenate(lead, 0))
    flip = jnp.where((row + col == half) | ((row == 0) & (col == 0)), 1.0, 0.0)
    position = lax.axis_index("cols") * piece_count
    d_last = [-product(stack(m + 1), stack(m + 1, 4)) for m in range(blocks_dev + 1)]
    l_last = [-product(stack(m + 1, 0, 2), stack(m, 1)) for m in range(blocks_dev + 1)]
    diagonal = position + lax.broadcasted_iota(jnp.int32, (piece_count, half), 0)
    across = lax.broadcasted_iota(jnp.int32, (piece_count, half), 1)
    for m in range(blocks_dev):
        b = first + m
        lim = jnp.where(b > 0, half, 0)
        rest_below = jnp.where(b == steps, half, 0)
        rest_last = jnp.where(b == steps + 1, half, 0)
        d_here, d_before = d_last[m + 1], d_last[m]
        l_here, l_before = l_last[m + 1], l_last[m]
        c0 = jnp.where(
            row >= sweeps, jnp.where(col >= sweeps, d_here, l_here), jnp.where(col < sweeps, d_before, 0.0)
        )
        c1 = jnp.where(
            row >= sweeps,
            jnp.where(col >= sweeps, l_here, jnp.where(row < rest_below, rest, 0.0)),
            jnp.where(col >= sweeps, d_before, l_before),
        )
        c1 = jnp.where(row < lim, c1, 0.0)
        c2 = jnp.where(col >= sweeps, l_before, jnp.where(row < rest_last, rest, 0.0))
        c2 = jnp.where(row < sweeps, c2, 0.0)
        c2 = jnp.where(row < lim, c2, 0.0)
        lower = jnp.where(col <= row, c0, c1)
        upper = jnp.where(col <= row, c1, c2)
        part = jnp.where(row < jnp.where(position < half, half, 0), lower, upper)
        turned = jnp.dot(part, flip, precision=lax.Precision.HIGHEST)
        turn_ref[m] = pltpu.roll(turned, 0, 1, stride=1, stride_axis=0).T
        turned = turn_ref[m, pl.ds(pl.multiple_of(position % half, 8), piece_count), :]
        place = b * half + across - diagonal
        cleared = (place & (half - 1) == sweeps) & (diagonal > half) & (place < (steps - 1) * half)
        cleared = cleared | ((place < sweeps) & (diagonal >= 2))
        span = slice(m * half, (m + 1) * half)
        band_out[:, span] = jnp.where(cleared, 0.0, band_ref[:, span] + turned)


def body(band_diagonals, eigenvectors):
    piece_count, rows_dev = band_diagonals.shape
    cols = lax.axis_size("cols")
    double = piece_count * cols
    half = double // 2
    blocks_dev = rows_dev // half
    devices = lax.axis_size("band")
    blocks = blocks_dev * devices
    sweeps = SWEEPS
    halo = sweeps
    columns = eigenvectors.shape[1]
    f32 = jnp.float32
    vmem = pl.BlockSpec(memory_space=pltpu.VMEM)

    takes = []
    while sum(takes) < halo * half:
        takes.append(min(halo * half - sum(takes), rows_dev))
    pieces = half // piece_count + 1
    dma = pltpu.SemaphoreType.DMA
    slots = blocks + 4
    pair_count = sweeps * (sweeps - 1) // 2 + 1
    scratch = (
        [
            pltpu.VMEM((blocks, half + 8, half), f32),
            pltpu.VMEM((piece_count, rows_dev), f32),
            pltpu.VMEM((blocks_dev, piece_count, half), f32),
            dma,
            [
                dma((blocks_dev, cols)),
                dma((pieces, blocks_dev)),
                dma((blocks_dev,)),
                dma((devices // 2, blocks_dev, pieces)),
                dma((devices // 2, blocks_dev, pieces)),
                dma((devices // 2, blocks_dev)),
                dma((devices // 2, blocks_dev)),
                dma((len(takes) + 1,)),
                dma((len(takes) + 1,)),
            ],
        ]
        + [pltpu.VMEM((slots, half, half), f32)] * 3
        + [
            pltpu.VMEM((half, half), f32),
            pltpu.VMEM((sweeps, 8, half), f32),
        ]
        + [pltpu.VMEM((blocks + 1, 8, half), f32)] * (2 * sweeps)
        + [pltpu.VMEM((slots, 8, half), f32)] * pair_count
    )
    anywhere = pl.BlockSpec(memory_space=pl.ANY)
    lines = -(-(halo + blocks_dev) // 8) * 8
    fields, v, tau, above, under = pl.pallas_call(
        functools.partial(kernel, half, devices, cols, takes, blocks, halo, sweeps),
        out_shape=(
            jax.ShapeDtypeStruct((sweeps, blocks_dev + 2, 8, half), f32),
            jax.ShapeDtypeStruct((sweeps, lines, half), f32),
            jax.ShapeDtypeStruct((sweeps, lines, half), f32),
            jax.ShapeDtypeStruct((halo * half, columns), f32),
            jax.ShapeDtypeStruct((8, columns), f32),
        ),
        in_specs=[anywhere] * 2,
        out_specs=(vmem,) * 3 + (anywhere,) * 2,
        scratch_shapes=scratch,
        compiler_params=pltpu.CompilerParams(
            collective_id=0, has_side_effects=True, vmem_limit_bytes=62 * 1024 * 1024
        ),
    )(band_diagonals, eigenvectors)
    return pl.pallas_call(
        functools.partial(finish_kernel, half, blocks, halo, sweeps),
        out_shape=(
            jax.ShapeDtypeStruct((piece_count, rows_dev), f32),
            jax.ShapeDtypeStruct((rows_dev, columns), f32),
        ),
        in_specs=[vmem] * 7,
        out_specs=(vmem, vmem),
        scratch_shapes=[pltpu.VMEM((blocks_dev, half, half), f32)],
    )(band_diagonals, eigenvectors, fields, v, tau, above, under)


def solution(mesh):
    return jax.shard_map(
        body,
        mesh=mesh,
        in_specs=(P("cols", "band"), P("band", "cols")),
        out_specs=(P("cols", "band"), P("band", "cols")),
        check_vma=False,
    )
```

```python
import functools

import jax
import jax.numpy as jnp
from jax import lax
from jax.experimental import pallas as pl
from jax.experimental.pallas import tpu as pltpu
from jax.sharding import PartitionSpec as P

SWEEPS = 4
LAG = 3
AHEAD = 4
EARLY = 3
GROUP = 3


def kernel(half, devices, cols, takes, blocks, halo, sweeps, band_ref, eig_ref, *refs):
    field_out, v_out, tau_out, above_ref, under_ref = refs[:5]
    all_ref, band_in, rev_ref, in_sem, sems = refs[5:10]
    refs = refs[10:]
    d_ref, l_ref, t_ref, eye_ref, raw_ref = refs[:5]
    v_refs = refs[5 : 5 + sweeps]
    tau_refs = refs[5 + sweeps : 5 + 2 * sweeps]
    last = sweeps - 1
    pairs = [(a, b) for b in range(1, sweeps) for a in range(b)] + [(last, last)]
    fields = dict(zip(pairs, refs[5 + 2 * sweeps :]))
    blocks_dev = band_ref.shape[1] // half
    steps = blocks - 2
    row = lax.broadcasted_iota(jnp.int32, (half, half), 0)
    col = lax.broadcasted_iota(jnp.int32, (half, half), 1)
    eye = row == col
    row8 = lax.broadcasted_iota(jnp.int32, (8, half), 0)
    col8 = lax.broadcasted_iota(jnp.int32, (8, half), 1)
    zero = jnp.zeros((half, half), jnp.float32)
    count = half // 8

    z_send, z_recv, own_sem, x_send, x_recv, p_send, p_recv, e_send, e_recv = sems
    d, c = lax.axis_index("band"), lax.axis_index("cols")
    deep, rows_dev = band_ref.shape
    full = half // deep
    pieces = full + 1
    parts = rows_dev // half
    chips = devices // 2
    chip, core = d // 2, d % 2
    partner = chip * 2 + 1 - core

    inward = pltpu.make_async_copy(band_ref, band_in, in_sem)
    inward.start()
    barrier = pltpu.get_barrier_semaphore()
    peers = [(d, (c + hop) % cols) for hop in range(1, cols)]
    peers += [((chip + hop) % chips * 2 + core, c) for hop in range(1, chips)]
    peers.append((partner, c))
    for hop in range(1, len(takes) + 1):
        peers += [((d + hop) % devices, c), ((d - hop + devices) % devices, c)]
    for peer in peers:
        pl.semaphore_signal(barrier, inc=1, device_id=peer, device_id_type=pl.DeviceIdType.MESH)

    for spot in (0, 1, blocks + 2):
        d_ref[spot] = zero
    for spot in (0, blocks + 1):
        l_ref[spot] = zero
        t_ref[spot] = zero
    for ref in v_refs + tau_refs + tuple(fields.values()) + (raw_ref,):
        ref[...] = jnp.zeros(ref.shape, jnp.float32)
    eye_ref[...] = jnp.where(eye, 1.0, 0.0)

    inward.wait()
    for r in range(deep):
        for m in range(parts):
            rev_ref[m, r : r + 1, :] = band_in[deep - 1 - r : deep - r, m * half : (m + 1) * half]

    pl.semaphore_wait(barrier, len(peers))

    def send(src, dst, send_sem, recv_sem, device):
        return pltpu.make_async_remote_copy(
            src_ref=src,
            dst_ref=dst,
            send_sem=send_sem,
            recv_sem=recv_sem,
            device_id=device,
            device_id_type=pl.DeviceIdType.MESH,
        )

    def rows_of(p):
        return pl.ds(half - (p + 1) * deep, deep) if p < full else pl.ds(half, 8)

    def source(p, m):
        return rev_ref.at[m] if p < full else band_in.at[pl.ds(0, 8), pl.ds(m * half, half)]

    def place(p, m):
        return all_ref.at[d * parts + m, rows_of(p)]

    def along(p, m, to):
        return send(source(p, m), place(p, m), z_send.at[m, to], z_recv.at[p, m], (d, to))

    def own(p, m):
        return pltpu.make_async_copy(source(p, m), place(p, m), own_sem.at[m])

    def chunk(owner, m):
        return all_ref.at[owner * parts + m]

    def across(to, m, p, src=None):
        dst = place(p, m)
        src = dst if src is None else src
        return send(src, dst, x_send.at[to, m, p], x_recv.at[chip, m, p], (to * 2 + core, c))

    def arrived(owner, m, p):
        dst = all_ref.at[(owner * 2 + core) * parts + m, rows_of(p)]
        return send(dst, dst, x_send.at[owner, m, p], x_recv.at[owner, m, p], (owner * 2 + core, c))

    def spread(m, p, src=None):
        for to in reversed(range(chips)):

            @pl.when(chip != to)
            def _():
                across(to, m, p, src).start()

    def share(owner, m):
        src = chunk(owner * 2 + core, m)
        return send(src, src, p_send.at[owner, m], p_recv.at[owner, m], (partner, c))

    halos = []
    end = sum(takes)
    for hop, take in enumerate(takes, 1):
        halos.append(
            send(
                eig_ref.at[pl.ds(rows_dev - take, take)],
                above_ref.at[pl.ds(end - take, take)],
                e_send.at[hop],
                e_recv.at[hop],
                ((d + hop) % devices, c),
            )
        )
        end -= take
    halos.append(
        send(eig_ref.at[pl.ds(0, 8)], under_ref, e_send.at[0], e_recv.at[0], ((d - 1 + devices) % devices, c))
    )

    for p in range(pieces):

        @pl.when(c == p)
        def _():
            for m in range(parts):
                for to in range(cols):
                    if to != p:
                        along(p, m, to).start()
                own(p, m).start()
                spread(m, p, source(p, m))

    for m in range(parts):
        for p in reversed(range(pieces)):

            @pl.when(c == p)
            def _():
                own(p, m).wait()

            @pl.when(c != p)
            def _():
                along(p, m, c).wait_recv()
                spread(m, p)

        share(chip, m).start()

    def sides(block):
        owner, m = block // parts, block % parts
        return owner // 2, owner % 2, m

    def duty(block):
        owner, side, m = sides(block)

        if block >= blocks:
            return

        @pl.when((core == side) & (chip != owner))
        def _():
            for p in range(pieces):
                arrived(owner, m, p).wait_recv()
            share(owner, m).start()

    def need(block):
        owner, side, m = sides(block)

        if block >= blocks:
            return

        @pl.when(core != side)
        def _():
            share(owner, m).wait_recv()

    def unpack(block):
        piece = all_ref[block, :half]
        extra = all_ref[block, half : half + 1]
        rows = pltpu.roll(piece.T, 1, 1, stride=1, stride_axis=0)
        turned = rows.T
        extra = jnp.where(eye, jnp.broadcast_to(extra, (half, half)), 0.0)
        d_ref[block + 2] = jnp.where(row >= col, rows, turned)
        l_ref[block + 1] = jnp.where(col > row, rows, extra)
        t_ref[block + 1] = jnp.where(row > col, turned, extra)

    def tile(ref, k, i=0):
        return ref[k + 2, 8 * i : 8 * i + 8, :]

    def lanes(x):
        return jnp.broadcast_to(jnp.sum(x, axis=1, keepdims=True), (8, half))

    def rows_sum(x):
        return jnp.broadcast_to(jnp.sum(x, axis=0, keepdims=True), (8, half))

    def at_lane(x, spot):
        return jnp.broadcast_to(x[:, spot : spot + 1], (8, half))

    def total(parts):
        while len(parts) > 1:
            rest = parts[len(parts) // 2 * 2 :]
            parts = [a + b for a, b in zip(parts[::2], parts[1::2])] + rest
        return parts[0]

    def to_lane(x, fill, spot):
        return jnp.where(col8 == spot, fill, x)

    def norms(x, new):
        rest = lanes(to_lane(x * x, 0.0, new))
        top = at_lane(x, new)
        square = rest + top * top
        inverse = lax.rsqrt(square)
        return rest, top, square * inverse, inverse

    def wide(line):
        return jnp.broadcast_to(line, (8, half))

    def begin(s):
        x = jnp.where(col8 > s, wide(d_ref[2, s : s + 1, :]), wide(t_ref[2, s : s + 1, :]))
        for a in range(s):
            x = x - rows_sum(fields[a, s][2] * at_lane(raw_ref[a], s))
        return (x,) + (jnp.zeros((8, half), jnp.float32),) * 4

    def targets(s):
        return range(s + 1, sweeps) if s < last else (last,)

    def settle(s, k, inside, v, tau):
        inside = inside - 0.5 * tau * lanes(v * inside) * v
        for b in targets(s):
            ref = fields[s, b]
            other = (col8 > s) & (col8 <= b)
            ref[k + 2, 4:5, :] = jnp.where(other, wide(ref[k + 2, 4:5, :]), inside)[0:1]
            if b > s:
                ref[k + 1, 7:8, :] = jnp.where(other, inside, wide(ref[k + 1, 7:8, :]))[0:1]
        if s < last and k == 0:
            raw_ref[s, 0:1, :] = inside[0:1]

    def chain(s, k, x, hung, inside_past, v_past, tau_past):
        new = s + 1
        main = col8 > s
        x_col = [
            jnp.sum(x * eye_ref[8 * i : 8 * i + 8, :], axis=1, keepdims=True) for i in range(count)
        ]
        rest, top, length, inverse = norms(x, new)
        x_main = jnp.where(row8 > s, x_col[0], 0.0)
        x_tail = jnp.where(row8 > s, 0.0, x_col[0])

        def times(ref, spot, extra):
            parts = [tile(ref, spot, i) * x_col[i] for i in range(1, count)]
            return total(parts + [tile(ref, spot) * x_main] + extra)

        here = times(d_ref, k, [tile(l_ref, k) * x_tail])
        after = times(t_ref, k, [tile(d_ref, k + 1) * x_tail])
        beyond = tile(t_ref, k + 1) * x_tail
        before = times(l_ref, k - 1, [])
        here_top = wide(d_ref[k + 2, new : new + 1, :])
        after_top = wide(t_ref[k + 2, new : new + 1, :])
        before_top = wide(l_ref[k + 1, new : new + 1, :])
        inside = jnp.where(main, here, after)
        beneath = jnp.where(main, after, beyond)
        across = jnp.where(main, before, here)
        fixes = []
        for a in range(s):
            now = fields[a, s][k + 2]
            up = jnp.where(row8 == 1, 0.0, fields[a, s][k + 1])
            down = jnp.where(row8 == 2, 0.0, fields[a, s][k + 3])
            unit = at_lane(now, new)
            dots = lanes(now * x)
            beneath = beneath - down * pltpu.roll(dots, 1, 0)
            fixes.append(down * pltpu.roll(unit, 1, 0))
            dots = dots + length * unit
            inside = inside - now * pltpu.roll(dots, 4, 0)
            across = across - up * pltpu.roll(dots, 7, 0)
        beneath = rows_sum(beneath)
        x_next = beneath * -inverse
        column = jnp.where(main, after_top, 0.0)
        if fixes:
            column = column - rows_sum(total(fixes))
        hang = lanes(hung * x) + length * at_lane(hung, new)
        v_top = top + length
        tau = 2.0 / (rest + v_top * v_top)
        v = to_lane(x, v_top, new)
        beneath = tau * (beneath + length * column)
        inside = tau * (rows_sum(inside) + length * jnp.where(main, here_top, after_top))
        across = tau * (rows_sum(across) + length * jnp.where(main, before_top, here_top) - v_past * hang)

        settle(s, k - 1, inside_past, v_past, tau_past)
        v_refs[s][k + 1] = v
        tau_refs[s][k + 1] = tau
        for b in targets(s):
            ref = fields[s, b]
            other = (col8 > s) & (col8 <= b)
            ref[k + 2, 0:1, :] = jnp.where(other, 0.0, v)[0:1]
            ref[k + 1, 7:8, :] = across[0:1]
            ref[k + 3, 1:2, :] = jnp.where(other, 0.0, beneath)[0:1]
            if b > s:
                ref[k + 2, 4:5, :] = beneath[0:1]
                ref[k + 1, 3:4, :] = jnp.where(other, v, 0.0)[0:1]
                ref[k, 2:3, :] = jnp.where(other, across, 0.0)[0:1]
        if s < last and k == 1:
            raw_ref[s, 3:4, :] = across[0:1]
        if s < last and k == 0:
            raw_ref[s, 4:5, :] = v[0:1]
        return x_next, beneath, inside, v, tau

    def phase(start, stop, chains, states):
        def wave(t, states):
            done = {s: chain(s, t - LAG * s, *state) for s, state in reversed(list(zip(chains, states)))}
            if t + AHEAD < blocks:
                unpack(t + AHEAD)
            return tuple(done[s] for s in chains)

        for begun in range(start, stop, GROUP):
            waves = range(begun, min(begun + GROUP, stop))
            for t in waves:
                duty(t + AHEAD + EARLY)
            for t in waves:
                need(t + AHEAD)
            for t in waves:
                states = wave(t, states)
        return states

    def drain(s, state):
        settle(s, steps - 1, *state[2:])

    for block in range(AHEAD + EARLY):
        duty(block)
    for block in range(AHEAD):
        need(block)
        unpack(block)
    states = ()
    for s in range(last):
        states = phase(LAG * s, LAG * (s + 1), range(s + 1), states + (begin(s),))
    for copy in halos:
        copy.start()
    states = phase(LAG * last, steps, range(sweeps), states + (begin(last),))
    for s in range(1, sweeps):
        drain(s - 1, states[0])
        states = phase(steps + LAG * (s - 1), steps + LAG * s, range(s, sweeps), states[1:])
    drain(last, states[0])

    for m in range(parts):
        for p in range(pieces):

            @pl.when(c == p)
            def _():
                for to in range(cols):
                    if to != p:
                        along(p, m, to).wait_send()

        for owner in range(chips):

            @pl.when(chip != owner)
            def _():
                for p in range(pieces):
                    across(owner, m, p).wait_send()

            share(owner, m).wait_send()
    for copy in halos:
        copy.wait()

    first = d * parts
    for s in range(sweeps):
        for e in range(halo + parts):
            spot = jnp.clip(first - halo + e, -1, blocks - 1) + 1
            v_out[s, e : e + 1, :] = v_refs[s][spot, 0:1, :]
            tau_out[s, e : e + 1, :] = tau_refs[s][spot, 0:1, :]
        for n in range(parts + 2):
            field_out[s, n] = fields[s, last][first + n]


def finish_kernel(half, blocks, halo, sweeps, *refs):
    band_ref, eig_ref, field_ref, v_ref, tau_ref, above_ref, under_ref, band_out, eig_out, turn_ref = refs
    piece_count, blocks_dev = band_ref.shape[0], band_ref.shape[1] // half
    steps = blocks - 2
    row = lax.broadcasted_iota(jnp.int32, (half, half), 0)
    col = lax.broadcasted_iota(jnp.int32, (half, half), 1)
    eye = row == col
    row8 = lax.broadcasted_iota(jnp.int32, (8, half), 0)
    device = lax.axis_index("band")
    first = device * blocks_dev
    eig = [above_ref[e * half : (e + 1) * half, :] for e in range(halo)]
    eig += [eig_ref[e * half : (e + 1) * half, :] for e in range(blocks_dev)]
    eig.append(under_ref[...])
    for s in reversed(range(sweeps)):
        lead_rows = s + 1
        for e in range(sweeps - 1 - s + halo - sweeps, halo + blocks_dev):
            v = jnp.sum(jnp.where(eye, v_ref[s, e : e + 1, :], 0.0), axis=1, keepdims=True)
            tau = tau_ref[s, e : e + 1, :]
            low, high = eig[e], eig[e + 1]
            mixed = jnp.concatenate([jnp.where(row8 < lead_rows, high[:8], low[:8]), low[8:]], 0)
            inner = tau * jnp.sum(v * mixed, axis=0, keepdims=True)
            mixed = mixed - v * inner
            eig[e] = jnp.concatenate([jnp.where(row8 < lead_rows, low[:8], mixed[:8]), mixed[8:]], 0)
            top = jnp.where(row8 < lead_rows, mixed[:8], high[:8])
            eig[e + 1] = jnp.concatenate([top, high[8:]], 0) if high.shape[0] > 8 else top
    for m in range(blocks_dev):
        eig_out[m * half : (m + 1) * half, :] = eig[halo + m]

    def product(a, b):
        return lax.dot_general(
            a, b, (((0,), (0,)), ((), ())),
            precision=lax.Precision.HIGHEST, preferred_element_type=jnp.float32,
        )

    def stack(n, shift=0, drop=None):
        parts = []
        for a in range(sweeps):
            part = field_ref[a, n]
            part = part if drop is None else jnp.where(row8 == drop, 0.0, part)
            parts.append(pltpu.roll(part, shift, 0) if shift else part)
        return jnp.concatenate(parts, 0)

    bottom, lead = [], []
    for a in range(sweeps - 1):
        bottom.append(jnp.where(row8 == 1, field_ref[a, blocks_dev], 0.0))
        lead.append(pltpu.roll(jnp.where(row8 == 3, field_ref[a, blocks_dev - 2], 0.0), 6, 0))
    rest = -product(jnp.concatenate(bottom, 0), jnp.concatenate(lead, 0))
    flip = jnp.where((row + col == half) | ((row == 0) & (col == 0)), 1.0, 0.0)
    position = lax.axis_index("cols") * piece_count
    d_last = [-product(stack(m + 1), stack(m + 1, 4)) for m in range(blocks_dev + 1)]
    l_last = [-product(stack(m + 1, 0, 2), stack(m, 1)) for m in range(blocks_dev + 1)]
    diagonal = position + lax.broadcasted_iota(jnp.int32, (piece_count, half), 0)
    across = lax.broadcasted_iota(jnp.int32, (piece_count, half), 1)
    for m in range(blocks_dev):
        b = first + m
        lim = jnp.where(b > 0, half, 0)
        rest_below = jnp.where(b == steps, half, 0)
        rest_last = jnp.where(b == steps + 1, half, 0)
        d_here, d_before = d_last[m + 1], d_last[m]
        l_here, l_before = l_last[m + 1], l_last[m]
        c0 = jnp.where(
            row >= sweeps, jnp.where(col >= sweeps, d_here, l_here), jnp.where(col < sweeps, d_before, 0.0)
        )
        c1 = jnp.where(
            row >= sweeps,
            jnp.where(col >= sweeps, l_here, jnp.where(row < rest_below, rest, 0.0)),
            jnp.where(col >= sweeps, d_before, l_before),
        )
        c1 = jnp.where(row < lim, c1, 0.0)
        c2 = jnp.where(col >= sweeps, l_before, jnp.where(row < rest_last, rest, 0.0))
        c2 = jnp.where(row < sweeps, c2, 0.0)
        c2 = jnp.where(row < lim, c2, 0.0)
        lower = jnp.where(col <= row, c0, c1)
        upper = jnp.where(col <= row, c1, c2)
        part = jnp.where(row < jnp.where(position < half, half, 0), lower, upper)
        turned = jnp.dot(part, flip, precision=lax.Precision.HIGHEST)
        turn_ref[m] = pltpu.roll(turned, 0, 1, stride=1, stride_axis=0).T
        turned = turn_ref[m, pl.ds(pl.multiple_of(position % half, 8), piece_count), :]
        place = b * half + across - diagonal
        cleared = (place & (half - 1) == sweeps) & (diagonal > half) & (place < (steps - 1) * half)
        cleared = cleared | ((place < sweeps) & (diagonal >= 2))
        span = slice(m * half, (m + 1) * half)
        band_out[:, span] = jnp.where(cleared, 0.0, band_ref[:, span] + turned)


def body(band_diagonals, eigenvectors):
    piece_count, rows_dev = band_diagonals.shape
    cols = lax.axis_size("cols")
    double = piece_count * cols
    half = double // 2
    blocks_dev = rows_dev // half
    devices = lax.axis_size("band")
    blocks = blocks_dev * devices
    sweeps = SWEEPS
    halo = sweeps
    columns = eigenvectors.shape[1]
    f32 = jnp.float32
    vmem = pl.BlockSpec(memory_space=pltpu.VMEM)

    takes = []
    while sum(takes) < halo * half:
        takes.append(min(halo * half - sum(takes), rows_dev))
    pieces = half // piece_count + 1
    dma = pltpu.SemaphoreType.DMA
    slots = blocks + 4
    pair_count = sweeps * (sweeps - 1) // 2 + 1
    scratch = (
        [
            pltpu.VMEM((blocks, half + 8, half), f32),
            pltpu.VMEM((piece_count, rows_dev), f32),
            pltpu.VMEM((blocks_dev, piece_count, half), f32),
            dma,
            [
                dma((blocks_dev, cols)),
                dma((pieces, blocks_dev)),
                dma((blocks_dev,)),
                dma((devices // 2, blocks_dev, pieces)),
                dma((devices // 2, blocks_dev, pieces)),
                dma((devices // 2, blocks_dev)),
                dma((devices // 2, blocks_dev)),
                dma((len(takes) + 1,)),
                dma((len(takes) + 1,)),
            ],
        ]
        + [pltpu.VMEM((slots, half, half), f32)] * 3
        + [
            pltpu.VMEM((half, half), f32),
            pltpu.VMEM((sweeps, 8, half), f32),
        ]
        + [pltpu.VMEM((blocks + 1, 8, half), f32)] * (2 * sweeps)
        + [pltpu.VMEM((slots, 8, half), f32)] * pair_count
    )
    anywhere = pl.BlockSpec(memory_space=pl.ANY)
    lines = -(-(halo + blocks_dev) // 8) * 8
    fields, v, tau, above, under = pl.pallas_call(
        functools.partial(kernel, half, devices, cols, takes, blocks, halo, sweeps),
        out_shape=(
            jax.ShapeDtypeStruct((sweeps, blocks_dev + 2, 8, half), f32),
            jax.ShapeDtypeStruct((sweeps, lines, half), f32),
            jax.ShapeDtypeStruct((sweeps, lines, half), f32),
            jax.ShapeDtypeStruct((halo * half, columns), f32),
            jax.ShapeDtypeStruct((8, columns), f32),
        ),
        in_specs=[anywhere] * 2,
        out_specs=(vmem,) * 3 + (anywhere,) * 2,
        scratch_shapes=scratch,
        compiler_params=pltpu.CompilerParams(
            collective_id=0, has_side_effects=True, vmem_limit_bytes=62 * 1024 * 1024
        ),
    )(band_diagonals, eigenvectors)
    return pl.pallas_call(
        functools.partial(finish_kernel, half, blocks, halo, sweeps),
        out_shape=(
            jax.ShapeDtypeStruct((piece_count, rows_dev), f32),
            jax.ShapeDtypeStruct((rows_dev, columns), f32),
        ),
        in_specs=[vmem] * 7,
        out_specs=(vmem, vmem),
        scratch_shapes=[pltpu.VMEM((blocks_dev, half, half), f32)],
    )(band_diagonals, eigenvectors, fields, v, tau, above, under)


def solution(mesh):
    return jax.shard_map(
        body,
        mesh=mesh,
        in_specs=(P("cols", "band"), P("band", "cols")),
        out_specs=(P("cols", "band"), P("band", "cols")),
        check_vma=False,
    )
```

```python
import functools

import jax
import jax.numpy as jnp
from jax import lax
from jax.experimental import pallas as pl
from jax.experimental.pallas import tpu as pltpu
from jax.sharding import PartitionSpec as P

SWEEPS = 4
LAG = 3
AHEAD = 3
EARLY = 3
GROUP = 3


def kernel(half, devices, cols, takes, blocks, halo, sweeps, band_ref, eig_ref, *refs):
    field_out, v_out, tau_out, above_ref, under_ref = refs[:5]
    all_ref, band_in, rev_ref, in_sem, sems = refs[5:10]
    refs = refs[10:]
    d_ref, l_ref, t_ref, eye_ref, raw_ref = refs[:5]
    v_refs = refs[5 : 5 + sweeps]
    tau_refs = refs[5 + sweeps : 5 + 2 * sweeps]
    last = sweeps - 1
    pairs = [(a, b) for b in range(1, sweeps) for a in range(b)] + [(last, last)]
    fields = dict(zip(pairs, refs[5 + 2 * sweeps :]))
    blocks_dev = band_ref.shape[1] // half
    steps = blocks - 2
    row = lax.broadcasted_iota(jnp.int32, (half, half), 0)
    col = lax.broadcasted_iota(jnp.int32, (half, half), 1)
    eye = row == col
    row8 = lax.broadcasted_iota(jnp.int32, (8, half), 0)
    col8 = lax.broadcasted_iota(jnp.int32, (8, half), 1)
    zero = jnp.zeros((half, half), jnp.float32)
    count = half // 8

    z_send, z_recv, own_sem, x_send, x_recv, p_send, p_recv, e_send, e_recv = sems
    d, c = lax.axis_index("band"), lax.axis_index("cols")
    deep, rows_dev = band_ref.shape
    full = half // deep
    pieces = full + 1
    parts = rows_dev // half
    chips = devices // 2
    chip, core = d // 2, d % 2
    partner = chip * 2 + 1 - core

    inward = pltpu.make_async_copy(band_ref, band_in, in_sem)
    inward.start()
    barrier = pltpu.get_barrier_semaphore()
    peers = [(d, (c + hop) % cols) for hop in range(1, cols)]
    peers += [((chip + hop) % chips * 2 + core, c) for hop in range(1, chips)]
    peers.append((partner, c))
    for hop in range(1, len(takes) + 1):
        peers += [((d + hop) % devices, c), ((d - hop + devices) % devices, c)]
    for peer in peers:
        pl.semaphore_signal(barrier, inc=1, device_id=peer, device_id_type=pl.DeviceIdType.MESH)

    for spot in (0, 1, blocks + 2):
        d_ref[spot] = zero
    for spot in (0, blocks + 1):
        l_ref[spot] = zero
        t_ref[spot] = zero
    for ref in v_refs + tau_refs + tuple(fields.values()) + (raw_ref,):
        ref[...] = jnp.zeros(ref.shape, jnp.float32)
    eye_ref[...] = jnp.where(eye, 1.0, 0.0)

    inward.wait()
    for r in range(deep):
        for m in range(parts):
            rev_ref[m, r : r + 1, :] = band_in[deep - 1 - r : deep - r, m * half : (m + 1) * half]

    pl.semaphore_wait(barrier, len(peers))

    def send(src, dst, send_sem, recv_sem, device):
        return pltpu.make_async_remote_copy(
            src_ref=src,
            dst_ref=dst,
            send_sem=send_sem,
            recv_sem=recv_sem,
            device_id=device,
            device_id_type=pl.DeviceIdType.MESH,
        )

    def rows_of(p):
        return pl.ds(half - (p + 1) * deep, deep) if p < full else pl.ds(half, 8)

    def source(p, m):
        return rev_ref.at[m] if p < full else band_in.at[pl.ds(0, 8), pl.ds(m * half, half)]

    def place(p, m):
        return all_ref.at[d * parts + m, rows_of(p)]

    def along(p, m, to):
        return send(source(p, m), place(p, m), z_send.at[m, to], z_recv.at[p, m], (d, to))

    def own(p, m):
        return pltpu.make_async_copy(source(p, m), place(p, m), own_sem.at[m])

    def chunk(owner, m):
        return all_ref.at[owner * parts + m]

    def across(to, m, p, src=None):
        dst = place(p, m)
        src = dst if src is None else src
        return send(src, dst, x_send.at[to, m, p], x_recv.at[chip, m, p], (to * 2 + core, c))

    def arrived(owner, m, p):
        dst = all_ref.at[(owner * 2 + core) * parts + m, rows_of(p)]
        return send(dst, dst, x_send.at[owner, m, p], x_recv.at[owner, m, p], (owner * 2 + core, c))

    def spread(m, p, src=None):
        for to in reversed(range(chips)):

            @pl.when(chip != to)
            def _():
                across(to, m, p, src).start()

    def share(owner, m):
        src = chunk(owner * 2 + core, m)
        return send(src, src, p_send.at[owner, m], p_recv.at[owner, m], (partner, c))

    halos = []
    end = sum(takes)
    for hop, take in enumerate(takes, 1):
        halos.append(
            send(
                eig_ref.at[pl.ds(rows_dev - take, take)],
                above_ref.at[pl.ds(end - take, take)],
                e_send.at[hop],
                e_recv.at[hop],
                ((d + hop) % devices, c),
            )
        )
        end -= take
    halos.append(
        send(eig_ref.at[pl.ds(0, 8)], under_ref, e_send.at[0], e_recv.at[0], ((d - 1 + devices) % devices, c))
    )

    for p in range(pieces):

        @pl.when(c == p)
        def _():
            for m in range(parts):
                for to in range(cols):
                    if to != p:
                        along(p, m, to).start()
                own(p, m).start()
                spread(m, p, source(p, m))

    for m in range(parts):
        for p in reversed(range(pieces)):

            @pl.when(c == p)
            def _():
                own(p, m).wait()

            @pl.when(c != p)
            def _():
                along(p, m, c).wait_recv()
                spread(m, p)

        share(chip, m).start()

    def sides(block):
        owner, m = block // parts, block % parts
        return owner // 2, owner % 2, m

    def duty(block):
        owner, side, m = sides(block)

        if block >= blocks:
            return

        @pl.when((core == side) & (chip != owner))
        def _():
            for p in range(pieces):
                arrived(owner, m, p).wait_recv()
            share(owner, m).start()

    def need(block):
        owner, side, m = sides(block)

        if block >= blocks:
            return

        @pl.when(core != side)
        def _():
            share(owner, m).wait_recv()

    def unpack(block):
        piece = all_ref[block, :half]
        extra = all_ref[block, half : half + 1]
        rows = pltpu.roll(piece.T, 1, 1, stride=1, stride_axis=0)
        turned = rows.T
        extra = jnp.where(eye, jnp.broadcast_to(extra, (half, half)), 0.0)
        d_ref[block + 2] = jnp.where(row >= col, rows, turned)
        l_ref[block + 1] = jnp.where(col > row, rows, extra)
        t_ref[block + 1] = jnp.where(row > col, turned, extra)

    def tile(ref, k, i=0):
        return ref[k + 2, 8 * i : 8 * i + 8, :]

    def lanes(x):
        return jnp.broadcast_to(jnp.sum(x, axis=1, keepdims=True), (8, half))

    def rows_sum(x):
        return jnp.broadcast_to(jnp.sum(x, axis=0, keepdims=True), (8, half))

    def at_lane(x, spot):
        return jnp.broadcast_to(x[:, spot : spot + 1], (8, half))

    def total(parts):
        while len(parts) > 1:
            rest = parts[len(parts) // 2 * 2 :]
            parts = [a + b for a, b in zip(parts[::2], parts[1::2])] + rest
        return parts[0]

    def to_lane(x, fill, spot):
        return jnp.where(col8 == spot, fill, x)

    def norms(x, new):
        rest = lanes(to_lane(x * x, 0.0, new))
        top = at_lane(x, new)
        square = rest + top * top
        inverse = lax.rsqrt(square)
        return rest, top, square * inverse, inverse

    def wide(line):
        return jnp.broadcast_to(line, (8, half))

    def begin(s):
        x = jnp.where(col8 > s, wide(d_ref[2, s : s + 1, :]), wide(t_ref[2, s : s + 1, :]))
        for a in range(s):
            x = x - rows_sum(fields[a, s][2] * at_lane(raw_ref[a], s))
        return (x,) + (jnp.zeros((8, half), jnp.float32),) * 4

    def targets(s):
        return range(s + 1, sweeps) if s < last else (last,)

    def settle(s, k, inside, v, tau):
        inside = inside - 0.5 * tau * lanes(v * inside) * v
        for b in targets(s):
            ref = fields[s, b]
            other = (col8 > s) & (col8 <= b)
            ref[k + 2, 4:5, :] = jnp.where(other, wide(ref[k + 2, 4:5, :]), inside)[0:1]
            if b > s:
                ref[k + 1, 7:8, :] = jnp.where(other, inside, wide(ref[k + 1, 7:8, :]))[0:1]
        if s < last and k == 0:
            raw_ref[s, 0:1, :] = inside[0:1]

    def chain(s, k, x, hung, inside_past, v_past, tau_past):
        new = s + 1
        main = col8 > s
        x_col = [
            jnp.sum(x * eye_ref[8 * i : 8 * i + 8, :], axis=1, keepdims=True) for i in range(count)
        ]
        rest, top, length, inverse = norms(x, new)
        x_main = jnp.where(row8 > s, x_col[0], 0.0)
        x_tail = jnp.where(row8 > s, 0.0, x_col[0])

        def times(ref, spot, extra):
            parts = [tile(ref, spot, i) * x_col[i] for i in range(1, count)]
            return total(parts + [tile(ref, spot) * x_main] + extra)

        here = times(d_ref, k, [tile(l_ref, k) * x_tail])
        after = times(t_ref, k, [tile(d_ref, k + 1) * x_tail])
        beyond = tile(t_ref, k + 1) * x_tail
        before = times(l_ref, k - 1, [])
        here_top = wide(d_ref[k + 2, new : new + 1, :])
        after_top = wide(t_ref[k + 2, new : new + 1, :])
        before_top = wide(l_ref[k + 1, new : new + 1, :])
        inside = jnp.where(main, here, after)
        beneath = jnp.where(main, after, beyond)
        across = jnp.where(main, before, here)
        fixes = []
        for a in range(s):
            now = fields[a, s][k + 2]
            up = jnp.where(row8 == 1, 0.0, fields[a, s][k + 1])
            down = jnp.where(row8 == 2, 0.0, fields[a, s][k + 3])
            unit = at_lane(now, new)
            dots = lanes(now * x)
            beneath = beneath - down * pltpu.roll(dots, 1, 0)
            fixes.append(down * pltpu.roll(unit, 1, 0))
            dots = dots + length * unit
            inside = inside - now * pltpu.roll(dots, 4, 0)
            across = across - up * pltpu.roll(dots, 7, 0)
        beneath = rows_sum(beneath)
        x_next = beneath * -inverse
        column = jnp.where(main, after_top, 0.0)
        if fixes:
            column = column - rows_sum(total(fixes))
        hang = lanes(hung * x) + length * at_lane(hung, new)
        v_top = top + length
        tau = 2.0 / (rest + v_top * v_top)
        v = to_lane(x, v_top, new)
        beneath = tau * (beneath + length * column)
        inside = tau * (rows_sum(inside) + length * jnp.where(main, here_top, after_top))
        across = tau * (rows_sum(across) + length * jnp.where(main, before_top, here_top) - v_past * hang)

        settle(s, k - 1, inside_past, v_past, tau_past)
        v_refs[s][k + 1] = v
        tau_refs[s][k + 1] = tau
        for b in targets(s):
            ref = fields[s, b]
            other = (col8 > s) & (col8 <= b)
            ref[k + 2, 0:1, :] = jnp.where(other, 0.0, v)[0:1]
            ref[k + 1, 7:8, :] = across[0:1]
            ref[k + 3, 1:2, :] = jnp.where(other, 0.0, beneath)[0:1]
            if b > s:
                ref[k + 2, 4:5, :] = beneath[0:1]
                ref[k + 1, 3:4, :] = jnp.where(other, v, 0.0)[0:1]
                ref[k, 2:3, :] = jnp.where(other, across, 0.0)[0:1]
        if s < last and k == 1:
            raw_ref[s, 3:4, :] = across[0:1]
        if s < last and k == 0:
            raw_ref[s, 4:5, :] = v[0:1]
        return x_next, beneath, inside, v, tau

    def phase(start, stop, chains, states):
        def wave(t, states):
            done = {s: chain(s, t - LAG * s, *state) for s, state in reversed(list(zip(chains, states)))}
            if t + AHEAD < blocks:
                unpack(t + AHEAD)
            return tuple(done[s] for s in chains)

        for begun in range(start, stop, GROUP):
            waves = range(begun, min(begun + GROUP, stop))
            for t in waves:
                duty(t + AHEAD + EARLY)
            for t in waves:
                need(t + AHEAD)
            for t in waves:
                states = wave(t, states)
        return states

    def drain(s, state):
        settle(s, steps - 1, *state[2:])

    for block in range(AHEAD + EARLY):
        duty(block)
    for block in range(AHEAD):
        need(block)
        unpack(block)
    states = ()
    for s in range(last):
        states = phase(LAG * s, LAG * (s + 1), range(s + 1), states + (begin(s),))
    for copy in halos:
        copy.start()
    states = phase(LAG * last, steps, range(sweeps), states + (begin(last),))
    for s in range(1, sweeps):
        drain(s - 1, states[0])
        states = phase(steps + LAG * (s - 1), steps + LAG * s, range(s, sweeps), states[1:])
    drain(last, states[0])

    for m in range(parts):
        for p in range(pieces):

            @pl.when(c == p)
            def _():
                for to in range(cols):
                    if to != p:
                        along(p, m, to).wait_send()

        for owner in range(chips):

            @pl.when(chip != owner)
            def _():
                for p in range(pieces):
                    across(owner, m, p).wait_send()

            share(owner, m).wait_send()
    for copy in halos:
        copy.wait()

    first = d * parts
    for s in range(sweeps):
        for e in range(halo + parts):
            spot = jnp.clip(first - halo + e, -1, blocks - 1) + 1
            v_out[s, e : e + 1, :] = v_refs[s][spot, 0:1, :]
            tau_out[s, e : e + 1, :] = tau_refs[s][spot, 0:1, :]
        for n in range(parts + 2):
            field_out[s, n] = fields[s, last][first + n]


def finish_kernel(half, blocks, halo, sweeps, *refs):
    band_ref, eig_ref, field_ref, v_ref, tau_ref, above_ref, under_ref, band_out, eig_out, turn_ref = refs
    piece_count, blocks_dev = band_ref.shape[0], band_ref.shape[1] // half
    steps = blocks - 2
    row = lax.broadcasted_iota(jnp.int32, (half, half), 0)
    col = lax.broadcasted_iota(jnp.int32, (half, half), 1)
    eye = row == col
    row8 = lax.broadcasted_iota(jnp.int32, (8, half), 0)
    device = lax.axis_index("band")
    first = device * blocks_dev
    eig = [above_ref[e * half : (e + 1) * half, :] for e in range(halo)]
    eig += [eig_ref[e * half : (e + 1) * half, :] for e in range(blocks_dev)]
    eig.append(under_ref[...])
    for s in reversed(range(sweeps)):
        lead_rows = s + 1
        for e in range(sweeps - 1 - s + halo - sweeps, halo + blocks_dev):
            v = jnp.sum(jnp.where(eye, v_ref[s, e : e + 1, :], 0.0), axis=1, keepdims=True)
            tau = tau_ref[s, e : e + 1, :]
            low, high = eig[e], eig[e + 1]
            mixed = jnp.concatenate([jnp.where(row8 < lead_rows, high[:8], low[:8]), low[8:]], 0)
            inner = tau * jnp.sum(v * mixed, axis=0, keepdims=True)
            mixed = mixed - v * inner
            eig[e] = jnp.concatenate([jnp.where(row8 < lead_rows, low[:8], mixed[:8]), mixed[8:]], 0)
            top = jnp.where(row8 < lead_rows, mixed[:8], high[:8])
            eig[e + 1] = jnp.concatenate([top, high[8:]], 0) if high.shape[0] > 8 else top
    for m in range(blocks_dev):
        eig_out[m * half : (m + 1) * half, :] = eig[halo + m]

    def product(a, b):
        return lax.dot_general(
            a, b, (((0,), (0,)), ((), ())),
            precision=lax.Precision.HIGHEST, preferred_element_type=jnp.float32,
        )

    def stack(n, shift=0, drop=None):
        parts = []
        for a in range(sweeps):
            part = field_ref[a, n]
            part = part if drop is None else jnp.where(row8 == drop, 0.0, part)
            parts.append(pltpu.roll(part, shift, 0) if shift else part)
        return jnp.concatenate(parts, 0)

    bottom, lead = [], []
    for a in range(sweeps - 1):
        bottom.append(jnp.where(row8 == 1, field_ref[a, blocks_dev], 0.0))
        lead.append(pltpu.roll(jnp.where(row8 == 3, field_ref[a, blocks_dev - 2], 0.0), 6, 0))
    rest = -product(jnp.concatenate(bottom, 0), jnp.concatenate(lead, 0))
    flip = jnp.where((row + col == half) | ((row == 0) & (col == 0)), 1.0, 0.0)
    position = lax.axis_index("cols") * piece_count
    d_last = [-product(stack(m + 1), stack(m + 1, 4)) for m in range(blocks_dev + 1)]
    l_last = [-product(stack(m + 1, 0, 2), stack(m, 1)) for m in range(blocks_dev + 1)]
    diagonal = position + lax.broadcasted_iota(jnp.int32, (piece_count, half), 0)
    across = lax.broadcasted_iota(jnp.int32, (piece_count, half), 1)
    for m in range(blocks_dev):
        b = first + m
        lim = jnp.where(b > 0, half, 0)
        rest_below = jnp.where(b == steps, half, 0)
        rest_last = jnp.where(b == steps + 1, half, 0)
        d_here, d_before = d_last[m + 1], d_last[m]
        l_here, l_before = l_last[m + 1], l_last[m]
        c0 = jnp.where(
            row >= sweeps, jnp.where(col >= sweeps, d_here, l_here), jnp.where(col < sweeps, d_before, 0.0)
        )
        c1 = jnp.where(
            row >= sweeps,
            jnp.where(col >= sweeps, l_here, jnp.where(row < rest_below, rest, 0.0)),
            jnp.where(col >= sweeps, d_before, l_before),
        )
        c1 = jnp.where(row < lim, c1, 0.0)
        c2 = jnp.where(col >= sweeps, l_before, jnp.where(row < rest_last, rest, 0.0))
        c2 = jnp.where(row < sweeps, c2, 0.0)
        c2 = jnp.where(row < lim, c2, 0.0)
        lower = jnp.where(col <= row, c0, c1)
        upper = jnp.where(col <= row, c1, c2)
        part = jnp.where(row < jnp.where(position < half, half, 0), lower, upper)
        turned = jnp.dot(part, flip, precision=lax.Precision.HIGHEST)
        turn_ref[m] = pltpu.roll(turned, 0, 1, stride=1, stride_axis=0).T
        turned = turn_ref[m, pl.ds(pl.multiple_of(position % half, 8), piece_count), :]
        place = b * half + across - diagonal
        cleared = (place & (half - 1) == sweeps) & (diagonal > half) & (place < (steps - 1) * half)
        cleared = cleared | ((place < sweeps) & (diagonal >= 2))
        span = slice(m * half, (m + 1) * half)
        band_out[:, span] = jnp.where(cleared, 0.0, band_ref[:, span] + turned)


def body(band_diagonals, eigenvectors):
    piece_count, rows_dev = band_diagonals.shape
    cols = lax.axis_size("cols")
    double = piece_count * cols
    half = double // 2
    blocks_dev = rows_dev // half
    devices = lax.axis_size("band")
    blocks = blocks_dev * devices
    sweeps = SWEEPS
    halo = sweeps
    columns = eigenvectors.shape[1]
    f32 = jnp.float32
    vmem = pl.BlockSpec(memory_space=pltpu.VMEM)

    takes = []
    while sum(takes) < halo * half:
        takes.append(min(halo * half - sum(takes), rows_dev))
    pieces = half // piece_count + 1
    dma = pltpu.SemaphoreType.DMA
    slots = blocks + 4
    pair_count = sweeps * (sweeps - 1) // 2 + 1
    scratch = (
        [
            pltpu.VMEM((blocks, half + 8, half), f32),
            pltpu.VMEM((piece_count, rows_dev), f32),
            pltpu.VMEM((blocks_dev, piece_count, half), f32),
            dma,
            [
                dma((blocks_dev, cols)),
                dma((pieces, blocks_dev)),
                dma((blocks_dev,)),
                dma((devices // 2, blocks_dev, pieces)),
                dma((devices // 2, blocks_dev, pieces)),
                dma((devices // 2, blocks_dev)),
                dma((devices // 2, blocks_dev)),
                dma((len(takes) + 1,)),
                dma((len(takes) + 1,)),
            ],
        ]
        + [pltpu.VMEM((slots, half, half), f32)] * 3
        + [
            pltpu.VMEM((half, half), f32),
            pltpu.VMEM((sweeps, 8, half), f32),
        ]
        + [pltpu.VMEM((blocks + 1, 8, half), f32)] * (2 * sweeps)
        + [pltpu.VMEM((slots, 8, half), f32)] * pair_count
    )
    anywhere = pl.BlockSpec(memory_space=pl.ANY)
    lines = -(-(halo + blocks_dev) // 8) * 8
    fields, v, tau, above, under = pl.pallas_call(
        functools.partial(kernel, half, devices, cols, takes, blocks, halo, sweeps),
        out_shape=(
            jax.ShapeDtypeStruct((sweeps, blocks_dev + 2, 8, half), f32),
            jax.ShapeDtypeStruct((sweeps, lines, half), f32),
            jax.ShapeDtypeStruct((sweeps, lines, half), f32),
            jax.ShapeDtypeStruct((halo * half, columns), f32),
            jax.ShapeDtypeStruct((8, columns), f32),
        ),
        in_specs=[anywhere] * 2,
        out_specs=(vmem,) * 3 + (anywhere,) * 2,
        scratch_shapes=scratch,
        compiler_params=pltpu.CompilerParams(
            collective_id=0, has_side_effects=True, vmem_limit_bytes=62 * 1024 * 1024
        ),
    )(band_diagonals, eigenvectors)
    return pl.pallas_call(
        functools.partial(finish_kernel, half, blocks, halo, sweeps),
        out_shape=(
            jax.ShapeDtypeStruct((piece_count, rows_dev), f32),
            jax.ShapeDtypeStruct((rows_dev, columns), f32),
        ),
        in_specs=[vmem] * 7,
        out_specs=(vmem, vmem),
        scratch_shapes=[pltpu.VMEM((blocks_dev, half, half), f32)],
    )(band_diagonals, eigenvectors, fields, v, tau, above, under)


def solution(mesh):
    return jax.shard_map(
        body,
        mesh=mesh,
        in_specs=(P("cols", "band"), P("band", "cols")),
        out_specs=(P("cols", "band"), P("band", "cols")),
        check_vma=False,
    )
```

```python
import functools

import jax
import jax.numpy as jnp
from jax import lax
from jax.experimental import pallas as pl
from jax.experimental.pallas import tpu as pltpu
from jax.sharding import PartitionSpec as P

SWEEPS = 4
LAG = 3
AHEAD = 3
EARLY = 4
GROUP = 3


def kernel(half, devices, cols, takes, blocks, halo, sweeps, band_ref, eig_ref, *refs):
    field_out, v_out, tau_out, above_ref, under_ref = refs[:5]
    all_ref, band_in, rev_ref, in_sem, sems = refs[5:10]
    refs = refs[10:]
    d_ref, l_ref, t_ref, eye_ref, raw_ref = refs[:5]
    v_refs = refs[5 : 5 + sweeps]
    tau_refs = refs[5 + sweeps : 5 + 2 * sweeps]
    last = sweeps - 1
    pairs = [(a, b) for b in range(1, sweeps) for a in range(b)] + [(last, last)]
    fields = dict(zip(pairs, refs[5 + 2 * sweeps :]))
    blocks_dev = band_ref.shape[1] // half
    steps = blocks - 2
    row = lax.broadcasted_iota(jnp.int32, (half, half), 0)
    col = lax.broadcasted_iota(jnp.int32, (half, half), 1)
    eye = row == col
    row8 = lax.broadcasted_iota(jnp.int32, (8, half), 0)
    col8 = lax.broadcasted_iota(jnp.int32, (8, half), 1)
    zero = jnp.zeros((half, half), jnp.float32)
    count = half // 8

    z_send, z_recv, own_sem, x_send, x_recv, p_send, p_recv, e_send, e_recv = sems
    d, c = lax.axis_index("band"), lax.axis_index("cols")
    deep, rows_dev = band_ref.shape
    full = half // deep
    pieces = full + 1
    parts = rows_dev // half
    chips = devices // 2
    chip, core = d // 2, d % 2
    partner = chip * 2 + 1 - core

    inward = pltpu.make_async_copy(band_ref, band_in, in_sem)
    inward.start()
    barrier = pltpu.get_barrier_semaphore()
    peers = [(d, (c + hop) % cols) for hop in range(1, cols)]
    peers += [((chip + hop) % chips * 2 + core, c) for hop in range(1, chips)]
    peers.append((partner, c))
    for hop in range(1, len(takes) + 1):
        peers += [((d + hop) % devices, c), ((d - hop + devices) % devices, c)]
    for peer in peers:
        pl.semaphore_signal(barrier, inc=1, device_id=peer, device_id_type=pl.DeviceIdType.MESH)

    for spot in (0, 1, blocks + 2):
        d_ref[spot] = zero
    for spot in (0, blocks + 1):
        l_ref[spot] = zero
        t_ref[spot] = zero
    for ref in v_refs + tau_refs + tuple(fields.values()) + (raw_ref,):
        ref[...] = jnp.zeros(ref.shape, jnp.float32)
    eye_ref[...] = jnp.where(eye, 1.0, 0.0)

    inward.wait()
    for r in range(deep):
        for m in range(parts):
            rev_ref[m, r : r + 1, :] = band_in[deep - 1 - r : deep - r, m * half : (m + 1) * half]

    pl.semaphore_wait(barrier, len(peers))

    def send(src, dst, send_sem, recv_sem, device):
        return pltpu.make_async_remote_copy(
            src_ref=src,
            dst_ref=dst,
            send_sem=send_sem,
            recv_sem=recv_sem,
            device_id=device,
            device_id_type=pl.DeviceIdType.MESH,
        )

    def rows_of(p):
        return pl.ds(half - (p + 1) * deep, deep) if p < full else pl.ds(half, 8)

    def source(p, m):
        return rev_ref.at[m] if p < full else band_in.at[pl.ds(0, 8), pl.ds(m * half, half)]

    def place(p, m):
        return all_ref.at[d * parts + m, rows_of(p)]

    def along(p, m, to):
        return send(source(p, m), place(p, m), z_send.at[m, to], z_recv.at[p, m], (d, to))

    def own(p, m):
        return pltpu.make_async_copy(source(p, m), place(p, m), own_sem.at[m])

    def chunk(owner, m):
        return all_ref.at[owner * parts + m]

    def across(to, m, p, src=None):
        dst = place(p, m)
        src = dst if src is None else src
        return send(src, dst, x_send.at[to, m, p], x_recv.at[chip, m, p], (to * 2 + core, c))

    def arrived(owner, m, p):
        dst = all_ref.at[(owner * 2 + core) * parts + m, rows_of(p)]
        return send(dst, dst, x_send.at[owner, m, p], x_recv.at[owner, m, p], (owner * 2 + core, c))

    def spread(m, p, src=None):
        for to in reversed(range(chips)):

            @pl.when(chip != to)
            def _():
                across(to, m, p, src).start()

    def share(owner, m):
        src = chunk(owner * 2 + core, m)
        return send(src, src, p_send.at[owner, m], p_recv.at[owner, m], (partner, c))

    halos = []
    end = sum(takes)
    for hop, take in enumerate(takes, 1):
        halos.append(
            send(
                eig_ref.at[pl.ds(rows_dev - take, take)],
                above_ref.at[pl.ds(end - take, take)],
                e_send.at[hop],
                e_recv.at[hop],
                ((d + hop) % devices, c),
            )
        )
        end -= take
    halos.append(
        send(eig_ref.at[pl.ds(0, 8)], under_ref, e_send.at[0], e_recv.at[0], ((d - 1 + devices) % devices, c))
    )

    for p in range(pieces):

        @pl.when(c == p)
        def _():
            for m in range(parts):
                for to in range(cols):
                    if to != p:
                        along(p, m, to).start()
                own(p, m).start()
                spread(m, p, source(p, m))

    for m in range(parts):
        for p in reversed(range(pieces)):

            @pl.when(c == p)
            def _():
                own(p, m).wait()

            @pl.when(c != p)
            def _():
                along(p, m, c).wait_recv()
                spread(m, p)

        share(chip, m).start()

    def sides(block):
        owner, m = block // parts, block % parts
        return owner // 2, owner % 2, m

    def duty(block):
        owner, side, m = sides(block)

        if block >= blocks:
            return

        @pl.when((core == side) & (chip != owner))
        def _():
            for p in range(pieces):
                arrived(owner, m, p).wait_recv()
            share(owner, m).start()

    def need(block):
        owner, side, m = sides(block)

        if block >= blocks:
            return

        @pl.when(core != side)
        def _():
            share(owner, m).wait_recv()

    def unpack(block):
        piece = all_ref[block, :half]
        extra = all_ref[block, half : half + 1]
        rows = pltpu.roll(piece.T, 1, 1, stride=1, stride_axis=0)
        turned = rows.T
        extra = jnp.where(eye, jnp.broadcast_to(extra, (half, half)), 0.0)
        d_ref[block + 2] = jnp.where(row >= col, rows, turned)
        l_ref[block + 1] = jnp.where(col > row, rows, extra)
        t_ref[block + 1] = jnp.where(row > col, turned, extra)

    def tile(ref, k, i=0):
        return ref[k + 2, 8 * i : 8 * i + 8, :]

    def lanes(x):
        return jnp.broadcast_to(jnp.sum(x, axis=1, keepdims=True), (8, half))

    def rows_sum(x):
        return jnp.broadcast_to(jnp.sum(x, axis=0, keepdims=True), (8, half))

    def at_lane(x, spot):
        return jnp.broadcast_to(x[:, spot : spot + 1], (8, half))

    def total(parts):
        while len(parts) > 1:
            rest = parts[len(parts) // 2 * 2 :]
            parts = [a + b for a, b in zip(parts[::2], parts[1::2])] + rest
        return parts[0]

    def to_lane(x, fill, spot):
        return jnp.where(col8 == spot, fill, x)

    def norms(x, new):
        rest = lanes(to_lane(x * x, 0.0, new))
        top = at_lane(x, new)
        square = rest + top * top
        inverse = lax.rsqrt(square)
        return rest, top, square * inverse, inverse

    def wide(line):
        return jnp.broadcast_to(line, (8, half))

    def begin(s):
        x = jnp.where(col8 > s, wide(d_ref[2, s : s + 1, :]), wide(t_ref[2, s : s + 1, :]))
        for a in range(s):
            x = x - rows_sum(fields[a, s][2] * at_lane(raw_ref[a], s))
        return (x,) + (jnp.zeros((8, half), jnp.float32),) * 4

    def targets(s):
        return range(s + 1, sweeps) if s < last else (last,)

    def settle(s, k, inside, v, tau):
        inside = inside - 0.5 * tau * lanes(v * inside) * v
        for b in targets(s):
            ref = fields[s, b]
            other = (col8 > s) & (col8 <= b)
            ref[k + 2, 4:5, :] = jnp.where(other, wide(ref[k + 2, 4:5, :]), inside)[0:1]
            if b > s:
                ref[k + 1, 7:8, :] = jnp.where(other, inside, wide(ref[k + 1, 7:8, :]))[0:1]
        if s < last and k == 0:
            raw_ref[s, 0:1, :] = inside[0:1]

    def chain(s, k, x, hung, inside_past, v_past, tau_past):
        new = s + 1
        main = col8 > s
        x_col = [
            jnp.sum(x * eye_ref[8 * i : 8 * i + 8, :], axis=1, keepdims=True) for i in range(count)
        ]
        rest, top, length, inverse = norms(x, new)
        x_main = jnp.where(row8 > s, x_col[0], 0.0)
        x_tail = jnp.where(row8 > s, 0.0, x_col[0])

        def times(ref, spot, extra):
            parts = [tile(ref, spot, i) * x_col[i] for i in range(1, count)]
            return total(parts + [tile(ref, spot) * x_main] + extra)

        here = times(d_ref, k, [tile(l_ref, k) * x_tail])
        after = times(t_ref, k, [tile(d_ref, k + 1) * x_tail])
        beyond = tile(t_ref, k + 1) * x_tail
        before = times(l_ref, k - 1, [])
        here_top = wide(d_ref[k + 2, new : new + 1, :])
        after_top = wide(t_ref[k + 2, new : new + 1, :])
        before_top = wide(l_ref[k + 1, new : new + 1, :])
        inside = jnp.where(main, here, after)
        beneath = jnp.where(main, after, beyond)
        across = jnp.where(main, before, here)
        fixes = []
        for a in range(s):
            now = fields[a, s][k + 2]
            up = jnp.where(row8 == 1, 0.0, fields[a, s][k + 1])
            down = jnp.where(row8 == 2, 0.0, fields[a, s][k + 3])
            unit = at_lane(now, new)
            dots = lanes(now * x)
            beneath = beneath - down * pltpu.roll(dots, 1, 0)
            fixes.append(down * pltpu.roll(unit, 1, 0))
            dots = dots + length * unit
            inside = inside - now * pltpu.roll(dots, 4, 0)
            across = across - up * pltpu.roll(dots, 7, 0)
        beneath = rows_sum(beneath)
        x_next = beneath * -inverse
        column = jnp.where(main, after_top, 0.0)
        if fixes:
            column = column - rows_sum(total(fixes))
        hang = lanes(hung * x) + length * at_lane(hung, new)
        v_top = top + length
        tau = 2.0 / (rest + v_top * v_top)
        v = to_lane(x, v_top, new)
        beneath = tau * (beneath + length * column)
        inside = tau * (rows_sum(inside) + length * jnp.where(main, here_top, after_top))
        across = tau * (rows_sum(across) + length * jnp.where(main, before_top, here_top) - v_past * hang)

        settle(s, k - 1, inside_past, v_past, tau_past)
        v_refs[s][k + 1] = v
        tau_refs[s][k + 1] = tau
        for b in targets(s):
            ref = fields[s, b]
            other = (col8 > s) & (col8 <= b)
            ref[k + 2, 0:1, :] = jnp.where(other, 0.0, v)[0:1]
            ref[k + 1, 7:8, :] = across[0:1]
            ref[k + 3, 1:2, :] = jnp.where(other, 0.0, beneath)[0:1]
            if b > s:
                ref[k + 2, 4:5, :] = beneath[0:1]
                ref[k + 1, 3:4, :] = jnp.where(other, v, 0.0)[0:1]
                ref[k, 2:3, :] = jnp.where(other, across, 0.0)[0:1]
        if s < last and k == 1:
            raw_ref[s, 3:4, :] = across[0:1]
        if s < last and k == 0:
            raw_ref[s, 4:5, :] = v[0:1]
        return x_next, beneath, inside, v, tau

    def phase(start, stop, chains, states):
        def wave(t, states):
            done = {s: chain(s, t - LAG * s, *state) for s, state in reversed(list(zip(chains, states)))}
            if t + AHEAD < blocks:
                unpack(t + AHEAD)
            return tuple(done[s] for s in chains)

        for begun in range(start, stop, GROUP):
            waves = range(begun, min(begun + GROUP, stop))
            for t in waves:
                duty(t + AHEAD + EARLY)
            for t in waves:
                need(t + AHEAD)
            for t in waves:
                states = wave(t, states)
        return states

    def drain(s, state):
        settle(s, steps - 1, *state[2:])

    for block in range(AHEAD + EARLY):
        duty(block)
    for block in range(AHEAD):
        need(block)
        unpack(block)
    states = ()
    for s in range(last):
        states = phase(LAG * s, LAG * (s + 1), range(s + 1), states + (begin(s),))
    for copy in halos:
        copy.start()
    states = phase(LAG * last, steps, range(sweeps), states + (begin(last),))
    for s in range(1, sweeps):
        drain(s - 1, states[0])
        states = phase(steps + LAG * (s - 1), steps + LAG * s, range(s, sweeps), states[1:])
    drain(last, states[0])

    for m in range(parts):
        for p in range(pieces):

            @pl.when(c == p)
            def _():
                for to in range(cols):
                    if to != p:
                        along(p, m, to).wait_send()

        for owner in range(chips):

            @pl.when(chip != owner)
            def _():
                for p in range(pieces):
                    across(owner, m, p).wait_send()

            share(owner, m).wait_send()
    for copy in halos:
        copy.wait()

    first = d * parts
    for s in range(sweeps):
        for e in range(halo + parts):
            spot = jnp.clip(first - halo + e, -1, blocks - 1) + 1
            v_out[s, e : e + 1, :] = v_refs[s][spot, 0:1, :]
            tau_out[s, e : e + 1, :] = tau_refs[s][spot, 0:1, :]
        for n in range(parts + 2):
            field_out[s, n] = fields[s, last][first + n]


def finish_kernel(half, blocks, halo, sweeps, *refs):
    band_ref, eig_ref, field_ref, v_ref, tau_ref, above_ref, under_ref, band_out, eig_out, turn_ref = refs
    piece_count, blocks_dev = band_ref.shape[0], band_ref.shape[1] // half
    steps = blocks - 2
    row = lax.broadcasted_iota(jnp.int32, (half, half), 0)
    col = lax.broadcasted_iota(jnp.int32, (half, half), 1)
    eye = row == col
    row8 = lax.broadcasted_iota(jnp.int32, (8, half), 0)
    device = lax.axis_index("band")
    first = device * blocks_dev
    eig = [above_ref[e * half : (e + 1) * half, :] for e in range(halo)]
    eig += [eig_ref[e * half : (e + 1) * half, :] for e in range(blocks_dev)]
    eig.append(under_ref[...])
    for s in reversed(range(sweeps)):
        lead_rows = s + 1
        for e in range(sweeps - 1 - s + halo - sweeps, halo + blocks_dev):
            v = jnp.sum(jnp.where(eye, v_ref[s, e : e + 1, :], 0.0), axis=1, keepdims=True)
            tau = tau_ref[s, e : e + 1, :]
            low, high = eig[e], eig[e + 1]
            mixed = jnp.concatenate([jnp.where(row8 < lead_rows, high[:8], low[:8]), low[8:]], 0)
            inner = tau * jnp.sum(v * mixed, axis=0, keepdims=True)
            mixed = mixed - v * inner
            eig[e] = jnp.concatenate([jnp.where(row8 < lead_rows, low[:8], mixed[:8]), mixed[8:]], 0)
            top = jnp.where(row8 < lead_rows, mixed[:8], high[:8])
            eig[e + 1] = jnp.concatenate([top, high[8:]], 0) if high.shape[0] > 8 else top
    for m in range(blocks_dev):
        eig_out[m * half : (m + 1) * half, :] = eig[halo + m]

    def product(a, b):
        return lax.dot_general(
            a, b, (((0,), (0,)), ((), ())),
            precision=lax.Precision.HIGHEST, preferred_element_type=jnp.float32,
        )

    def stack(n, shift=0, drop=None):
        parts = []
        for a in range(sweeps):
            part = field_ref[a, n]
            part = part if drop is None else jnp.where(row8 == drop, 0.0, part)
            parts.append(pltpu.roll(part, shift, 0) if shift else part)
        return jnp.concatenate(parts, 0)

    bottom, lead = [], []
    for a in range(sweeps - 1):
        bottom.append(jnp.where(row8 == 1, field_ref[a, blocks_dev], 0.0))
        lead.append(pltpu.roll(jnp.where(row8 == 3, field_ref[a, blocks_dev - 2], 0.0), 6, 0))
    rest = -product(jnp.concatenate(bottom, 0), jnp.concatenate(lead, 0))
    flip = jnp.where((row + col == half) | ((row == 0) & (col == 0)), 1.0, 0.0)
    position = lax.axis_index("cols") * piece_count
    d_last = [-product(stack(m + 1), stack(m + 1, 4)) for m in range(blocks_dev + 1)]
    l_last = [-product(stack(m + 1, 0, 2), stack(m, 1)) for m in range(blocks_dev + 1)]
    diagonal = position + lax.broadcasted_iota(jnp.int32, (piece_count, half), 0)
    across = lax.broadcasted_iota(jnp.int32, (piece_count, half), 1)
    for m in range(blocks_dev):
        b = first + m
        lim = jnp.where(b > 0, half, 0)
        rest_below = jnp.where(b == steps, half, 0)
        rest_last = jnp.where(b == steps + 1, half, 0)
        d_here, d_before = d_last[m + 1], d_last[m]
        l_here, l_before = l_last[m + 1], l_last[m]
        c0 = jnp.where(
            row >= sweeps, jnp.where(col >= sweeps, d_here, l_here), jnp.where(col < sweeps, d_before, 0.0)
        )
        c1 = jnp.where(
            row >= sweeps,
            jnp.where(col >= sweeps, l_here, jnp.where(row < rest_below, rest, 0.0)),
            jnp.where(col >= sweeps, d_before, l_before),
        )
        c1 = jnp.where(row < lim, c1, 0.0)
        c2 = jnp.where(col >= sweeps, l_before, jnp.where(row < rest_last, rest, 0.0))
        c2 = jnp.where(row < sweeps, c2, 0.0)
        c2 = jnp.where(row < lim, c2, 0.0)
        lower = jnp.where(col <= row, c0, c1)
        upper = jnp.where(col <= row, c1, c2)
        part = jnp.where(row < jnp.where(position < half, half, 0), lower, upper)
        turned = jnp.dot(part, flip, precision=lax.Precision.HIGHEST)
        turn_ref[m] = pltpu.roll(turned, 0, 1, stride=1, stride_axis=0).T
        turned = turn_ref[m, pl.ds(pl.multiple_of(position % half, 8), piece_count), :]
        place = b * half + across - diagonal
        cleared = (place & (half - 1) == sweeps) & (diagonal > half) & (place < (steps - 1) * half)
        cleared = cleared | ((place < sweeps) & (diagonal >= 2))
        span = slice(m * half, (m + 1) * half)
        band_out[:, span] = jnp.where(cleared, 0.0, band_ref[:, span] + turned)


def body(band_diagonals, eigenvectors):
    piece_count, rows_dev = band_diagonals.shape
    cols = lax.axis_size("cols")
    double = piece_count * cols
    half = double // 2
    blocks_dev = rows_dev // half
    devices = lax.axis_size("band")
    blocks = blocks_dev * devices
    sweeps = SWEEPS
    halo = sweeps
    columns = eigenvectors.shape[1]
    f32 = jnp.float32
    vmem = pl.BlockSpec(memory_space=pltpu.VMEM)

    takes = []
    while sum(takes) < halo * half:
        takes.append(min(halo * half - sum(takes), rows_dev))
    pieces = half // piece_count + 1
    dma = pltpu.SemaphoreType.DMA
    slots = blocks + 4
    pair_count = sweeps * (sweeps - 1) // 2 + 1
    scratch = (
        [
            pltpu.VMEM((blocks, half + 8, half), f32),
            pltpu.VMEM((piece_count, rows_dev), f32),
            pltpu.VMEM((blocks_dev, piece_count, half), f32),
            dma,
            [
                dma((blocks_dev, cols)),
                dma((pieces, blocks_dev)),
                dma((blocks_dev,)),
                dma((devices // 2, blocks_dev, pieces)),
                dma((devices // 2, blocks_dev, pieces)),
                dma((devices // 2, blocks_dev)),
                dma((devices // 2, blocks_dev)),
                dma((len(takes) + 1,)),
                dma((len(takes) + 1,)),
            ],
        ]
        + [pltpu.VMEM((slots, half, half), f32)] * 3
        + [
            pltpu.VMEM((half, half), f32),
            pltpu.VMEM((sweeps, 8, half), f32),
        ]
        + [pltpu.VMEM((blocks + 1, 8, half), f32)] * (2 * sweeps)
        + [pltpu.VMEM((slots, 8, half), f32)] * pair_count
    )
    anywhere = pl.BlockSpec(memory_space=pl.ANY)
    lines = -(-(halo + blocks_dev) // 8) * 8
    fields, v, tau, above, under = pl.pallas_call(
        functools.partial(kernel, half, devices, cols, takes, blocks, halo, sweeps),
        out_shape=(
            jax.ShapeDtypeStruct((sweeps, blocks_dev + 2, 8, half), f32),
            jax.ShapeDtypeStruct((sweeps, lines, half), f32),
            jax.ShapeDtypeStruct((sweeps, lines, half), f32),
            jax.ShapeDtypeStruct((halo * half, columns), f32),
            jax.ShapeDtypeStruct((8, columns), f32),
        ),
        in_specs=[anywhere] * 2,
        out_specs=(vmem,) * 3 + (anywhere,) * 2,
        scratch_shapes=scratch,
        compiler_params=pltpu.CompilerParams(
            collective_id=0, has_side_effects=True, vmem_limit_bytes=62 * 1024 * 1024
        ),
    )(band_diagonals, eigenvectors)
    return pl.pallas_call(
        functools.partial(finish_kernel, half, blocks, halo, sweeps),
        out_shape=(
            jax.ShapeDtypeStruct((piece_count, rows_dev), f32),
            jax.ShapeDtypeStruct((rows_dev, columns), f32),
        ),
        in_specs=[vmem] * 7,
        out_specs=(vmem, vmem),
        scratch_shapes=[pltpu.VMEM((blocks_dev, half, half), f32)],
    )(band_diagonals, eigenvectors, fields, v, tau, above, under)


def solution(mesh):
    return jax.shard_map(
        body,
        mesh=mesh,
        in_specs=(P("cols", "band"), P("band", "cols")),
        out_specs=(P("cols", "band"), P("band", "cols")),
        check_vma=False,
    )
```
